32 devices in a mesh: dp: 16 (over z, y, core), rep: 2 (over x).
Axes of the slice: x: 2, y: 2, z: 4, core: 2. Of those that a mesh axis runs over, the one named last changes fastest.
Arguments:
- inputs: bfloat16 [36864, 768], P(('dp', 'rep')), may hold values from -6 to 6
- skips: bfloat16 [36864, 768], P(('dp', 'rep')), may hold values from -6 to 6
- cotangent: bfloat16 [36864, 768], P(('dp', 'rep')), may hold values from -6 to 6
- lengths: int32 [128], P(('dp', 'rep')), may hold values from 0 to 1025, as said below
- patch_keep: int32 [36864], P(('dp', 'rep')), may hold values 0 or 1
- group_ids: int32 [128], P(('dp', 'rep')), may hold values from 0 to 7
- group_counts: int32 [8], replicated, may hold values from 1152 to 9215
- skip_weight: bfloat16 [1536, 768], replicated, may hold values from -0.15625 to 0.15625
- skip_bias: bfloat16 [768], replicated, may hold values from -2 to 2
- first_gain: bfloat16 [768], replicated, may hold values from 0.25 to 1.75
- first_shift: bfloat16 [768], replicated, may hold values from -2 to 2
- joint_weight: bfloat16 [768, 2304], replicated, may hold values from -0.21875 to 0.21875
- output_weight: bfloat16 [768, 768], replicated, may hold values from -0.875 to 0.875
- output_bias: bfloat16 [768], replicated, may hold values from -2 to 2
- second_gain: bfloat16 [768], replicated, may hold values from 0.25 to 1.75
- second_shift: bfloat16 [768], replicated, may hold values from -2 to 2
- expand_weight: bfloat16 [768, 3072], replicated, may hold values from -0.21875 to 0.21875
- expand_bias: bfloat16 [3072], replicated, may hold values from -3 to 3
- reduce_weight: bfloat16 [3072, 768], replicated, may hold values from -0.109375 to 0.109375
- reduce_bias: bfloat16 [768], replicated, may hold values from -2 to 2
Outputs:
- outcome: bfloat16 [36864, 768], P(('dp', 'rep'))
- inputs_grad: bfloat16 [36864, 768], P(('dp', 'rep'))
- skips_grad: bfloat16 [36864, 768], P(('dp', 'rep'))
- skip_weight_grad: float32 [1536, 768], P(None, 'dp')
- skip_bias_grad: float32 [768], P('dp')
- first_gain_grad: float32 [768], P('dp')
- first_shift_grad: float32 [768], P('dp')
- joint_weight_grad: float32 [768, 2304], P(None, 'dp')
- output_weight_grad: float32 [768, 768], P(None, 'dp')
- output_bias_grad: float32 [768], P('dp')
- second_gain_grad: float32 [768], P('dp')
- second_shift_grad: float32 [768], P('dp')
- expand_weight_grad: float32 [768, 3072], P(None, 'dp')
- expand_bias_grad: float32 [3072], P('dp')
- reduce_weight_grad: float32 [3072, 768], P(None, 'dp')
- reduce_bias_grad: float32 [768], P('dp')
The draws below stay inside these ranges and needn't reach their ends.
Inputs may be any that keep to these rules, and one draw needn't show every extreme that they name: `lengths`: in every device buffer either the first slot holds 1025 and the other slots 0, or all 4 slots hold 257; both kinds occur in every draw.
All inputs are finite; a program needn't handle non-finite values. No bound on the sum of `patch_keep` on one device may be relied on, other than what follows from the above.
Results may differ from the reference program's by a relative error of at most 0.014.
Values sent between devices are 32-bit elements; how exact they have to be, the bound alone decides.
No kernel may reach another device: no remote copies, remote signals or barrier semaphores. Data moves between devices by JAX's collectives and lax.ppermute only.
A program may use at most 192 MiB of HBM per device.

```python
import jax
import jax.numpy as jnp
from jax import lax

D = 768
FF = 3072
HEADS = 12
HEAD_DIM = 64
LONG = 1025
SHORT = 257
SLOTS = 4
TOK_DEV = 1152
GROUPS = 8
BUFFERS = 32
TOKENS = 36864
ITEMS = 128
GROUP_TOKENS = 4608


def draw_lengths(key, part):
    kinds = jax.random.randint(key, (BUFFERS,), 0, 2)
    places = jnp.arange(BUFFERS, dtype=jnp.int32)
    kinds = jnp.where(places == 0, 1, jnp.where(places == 1, 0, kinds))
    slot_index = jnp.arange(SLOTS, dtype=jnp.int32)
    long_row = jnp.where(slot_index == 0, LONG, 0)
    short_row = jnp.full((SLOTS,), SHORT, dtype=jnp.int32)
    table = jnp.where(kinds[:, None] == 1, long_row[None, :], short_row[None, :])
    return table.reshape(-1).astype(jnp.int32)


def plant(array, rng, least, high):
    extent = array.shape
    place = [jax.random.randint(jax.random.fold_in(rng, axis), (), 0, extent[axis]) for axis in range(len(extent))]
    array = array.at[tuple(place)].set(least)
    longest = extent.index(max(extent))
    place[longest] = (place[longest] + 1) % extent[longest]
    return array.at[tuple(place)].set(high)


def raised(entries, stream_key, source, target, parts, factor):
    def block_of(position):
        return (jnp.arange(entries.shape[position]) // (entries.shape[position] // parts)).reshape((-1,) + (1,) * (entries.ndim - 1 - position))

    near = jax.random.permutation(stream_key, parts)[block_of(target)]
    second = (block_of(target) + parts // 2) % parts
    return jnp.where((block_of(source) == near) | (block_of(source) == second), factor * entries, entries)


def levels(stream_key, shape, pieces, smallest, high):
    level = 1.0
    for axis_at, blocks in pieces:
        heights = jax.random.uniform(jax.random.fold_in(jax.random.fold_in(stream_key, 6), axis_at), (blocks,), jnp.float32, smallest / len(pieces), high / len(pieces))
        level = level * jnp.repeat(jnp.exp(heights), shape[axis_at] // blocks).reshape((-1,) + (1,) * (len(shape) - 1 - axis_at))
    return level


def normal_values(key, shape, scale, reach, shards=(), kind=jnp.bfloat16):
    result = scale * jax.random.normal(key, shape, jnp.float32)
    if shards:
        result = result * levels(key, shape, shards, -0.22, 0.18)
    return jnp.clip(result, -reach, reach).astype(kind)


def gaussian_with(own_key, shape, deviation, reach, shards, heavy, held_as=jnp.bfloat16):
    values = deviation * jax.random.normal(own_key, shape, jnp.float32)
    if shards:
        values = values * levels(own_key, shape, shards, -0.22, 0.18)
    return jnp.clip(raised(values, jax.random.fold_in(own_key, 3), *heavy), -reach, reach).astype(held_as)


def setup_inputs(seed: int = 0) -> dict:
    key_list = jax.random.split(jax.random.key(seed), 21)
    inputs = normal_values(key_list[0], (TOKENS, D), 1.0, 6.0, ((0, 32),))
    skips = normal_values(key_list[1], (TOKENS, D), 1.0, 6.0, ((0, 32),))
    cotangent = gaussian_with(key_list[2], (TOKENS, D), 1.0, 6.0, ((0, 32),), (0, 1, 32, 2.75))
    lengths = draw_lengths(jax.random.fold_in(key_list[20], 71), 0)
    patch_keep = plant((jax.random.randint(key_list[4], (TOKENS,), 0, 5) < 4).astype(jnp.int32), jax.random.fold_in(key_list[4], 1), 0, 1)
    group_ids = plant(jax.random.randint(key_list[5], (ITEMS,), 0, GROUPS), jax.random.fold_in(key_list[5], 1), 0, GROUPS - 1).astype(jnp.int32)
    group_counts = plant(jax.random.randint(key_list[6], (GROUPS,), GROUP_TOKENS // 4, 2 * GROUP_TOKENS), jax.random.fold_in(key_list[6], 1), GROUP_TOKENS // 4, (2 * GROUP_TOKENS) - 1).astype(jnp.int32)
    skip_weight = normal_values(key_list[7], (2 * D, D), (2 * D) ** -0.5, 0.15625)
    skip_bias = normal_values(key_list[8], (D,), 0.3, 2.0)
    first_gain = jnp.clip(1.0 + 0.15 * jax.random.normal(key_list[9], (D,), jnp.float32), 0.25, 1.75).astype(jnp.bfloat16)
    first_shift = normal_values(key_list[10], (D,), 0.3, 2.0)
    joint_weight = normal_values(key_list[11], (D, 3 * D), D ** -0.5, 0.21875)
    output_weight = normal_values(key_list[12], (D, D), (D // 16) ** -0.5, 0.875)
    output_bias = normal_values(key_list[13], (D,), 0.3, 2.0)
    second_gain = jnp.clip(1.0 + 0.15 * jax.random.normal(key_list[14], (D,), jnp.float32), 0.25, 1.75).astype(jnp.bfloat16)
    second_shift = normal_values(key_list[15], (D,), 0.3, 2.0)
    expand_weight = normal_values(key_list[16], (D, FF), D ** -0.5, 0.21875)
    expand_bias = normal_values(key_list[17], (FF,), 0.5, 3.0)
    reduce_weight = normal_values(key_list[18], (FF, D), FF ** -0.5, 0.109375)
    reduce_bias = normal_values(key_list[19], (D,), 0.3, 2.0)
    return {"inputs": inputs, "skips": skips, "cotangent": cotangent, "lengths": lengths, "patch_keep": patch_keep, "group_ids": group_ids, "group_counts": group_counts, "skip_weight": skip_weight, "skip_bias": skip_bias, "first_gain": first_gain, "first_shift": first_shift, "joint_weight": joint_weight, "output_weight": output_weight, "output_bias": output_bias, "second_gain": second_gain, "second_shift": second_shift, "expand_weight": expand_weight, "expand_bias": expand_bias, "reduce_weight": reduce_weight, "reduce_bias": reduce_bias}


@jax.custom_vjp
def low(v):
    return lax.optimization_barrier(v.astype(jnp.bfloat16)).astype(jnp.float32)

@jax.custom_vjp
def low_back(v):
    return v

def low_keep(v):
    return (low(v), None)

def low_pass(kept, grad):
    return (grad,)

def back_keep(v):
    return (v, None)

def back_low(kept, grad):
    return (low(grad),)
low.defvjp(low_keep, low_pass)
low_back.defvjp(back_keep, back_low)
epsilon = 1e-05

def product(left, right):
    return jnp.dot(left, right, preferred_element_type=jnp.float32, precision=lax.Precision.HIGHEST)

def layer_norm(values_in, norm_gain, norm_shift):
    row_mean = lax.optimization_barrier(jnp.mean(values_in, axis=-1, keepdims=True))
    centred = values_in - row_mean
    variance = lax.optimization_barrier(jnp.mean(centred * centred, axis=-1, keepdims=True))
    return centred * lax.rsqrt(variance + epsilon) * norm_gain + norm_shift

def buffer_layout(lengths_row, keep_row, groups_row, group_counts):
    item_ends = jnp.cumsum(lengths_row)
    positions = jnp.arange(TOK_DEV, dtype=jnp.int32)
    segment = lax.optimization_barrier(jnp.sum((positions[:, None] >= item_ends[None, :]).astype(jnp.int32), axis=1))
    same_item = segment[:, None] == segment[None, :]
    allowed = same_item & ((keep_row[None, :] == 1) | (positions[:, None] == positions[None, :]))
    chosen = groups_row[:, None] == jnp.arange(GROUPS, dtype=jnp.int32)[None, :]
    slot_count = lax.optimization_barrier(jnp.sum(jnp.where(chosen, group_counts[None, :], 0), axis=1)).astype(jnp.float32)
    slot_weight = GROUP_TOKENS / slot_count
    in_slot = segment[:, None] == jnp.arange(SLOTS, dtype=jnp.int32)[None, :]
    token_weight = lax.optimization_barrier(jnp.sum(jnp.where(in_slot, slot_weight[None, :], 0.0), axis=1))
    return (allowed, token_weight)

def forward(weights_all, first_in, second_in, allowed):
    skip_weight, skip_bias, first_gain, first_shift, joint_weight, output_weight, output_bias, second_gain, second_shift, expand_weight, expand_bias, reduce_weight, reduce_bias = weights_all
    joined = jnp.concatenate([first_in, second_in], axis=1)
    hidden = low_back(product(joined, skip_weight) + skip_bias)
    normed1 = low(layer_norm(hidden, first_gain, first_shift))
    packed = low(low_back(product(normed1, joint_weight)))
    row_count = packed.shape[0]
    split_parts = packed.reshape(row_count, 3, HEADS, HEAD_DIM)
    scores = jnp.einsum('qhd,khd->hqk', split_parts[:, 0], split_parts[:, 1], precision=lax.Precision.HIGHEST)
    scores = low_back(scores * HEAD_DIM ** (-0.5))
    masked = jnp.where(allowed[None], scores, -1e+30)
    row_top = lax.optimization_barrier(jnp.max(masked, axis=2, keepdims=True))
    exponent = jnp.exp(masked - row_top)
    probs = low(exponent / lax.optimization_barrier(jnp.sum(exponent, axis=2, keepdims=True)))
    attended = jnp.einsum('hqk,khd->qhd', probs, split_parts[:, 2], precision=lax.Precision.HIGHEST)
    attended = low(low_back(attended.reshape(row_count, HEADS * HEAD_DIM)))
    branch = low_back(product(attended, output_weight) + output_bias)
    middle = hidden + branch
    normed2 = low(layer_norm(middle, second_gain, second_shift))
    pre_act = low_back(product(normed2, expand_weight) + expand_bias)
    activated = low(jax.nn.gelu(pre_act, approximate=False))
    return middle + low_back(product(activated, reduce_weight) + reduce_bias)

def reference(inputs, skips, cotangent, lengths, patch_keep, group_ids, group_counts, skip_weight, skip_bias, first_gain, first_shift, joint_weight, output_weight, output_bias, second_gain, second_shift, expand_weight, expand_bias, reduce_weight, reduce_bias):
    weights_all = jax.tree.map(lambda weight_array: weight_array.astype(jnp.float32), (skip_weight, skip_bias, first_gain, first_shift, joint_weight, output_weight, output_bias, second_gain, second_shift, expand_weight, expand_bias, reduce_weight, reduce_bias))

    def one_buffer(running, slices):
        inputs_row, skips_row, cotan_row, lengths_row, keep_row, groups_row = slices
        allowed, token_weight = buffer_layout(lengths_row, keep_row, groups_row, group_counts)

        def apply_layer(weight_tuple, first_in, second_in):
            return forward(weight_tuple, first_in, second_in, allowed)
        outcome, pullback = jax.vjp(apply_layer, weights_all, inputs_row.astype(jnp.float32), skips_row.astype(jnp.float32))
        weight_grads, first_grad, second_grad = pullback(cotan_row.astype(jnp.float32) * token_weight[:, None])
        running = jax.tree.map(jnp.add, running, weight_grads)
        return (running, (outcome.astype(jnp.bfloat16), first_grad.astype(jnp.bfloat16), second_grad.astype(jnp.bfloat16)))
    zeros_start = jax.tree.map(jnp.zeros_like, weights_all)
    totals, stacked = lax.scan(one_buffer, zeros_start, (inputs.reshape(BUFFERS, TOK_DEV, D), skips.reshape(BUFFERS, TOK_DEV, D), cotangent.reshape(BUFFERS, TOK_DEV, D), lengths.reshape(BUFFERS, SLOTS), patch_keep.reshape(BUFFERS, TOK_DEV), group_ids.reshape(BUFFERS, SLOTS)))
    grad_scale = TOKENS ** (-0.5)
    return (stacked[0].reshape(TOKENS, D), stacked[1].reshape(TOKENS, D), stacked[2].reshape(TOKENS, D), totals[0] * grad_scale, totals[1] * grad_scale, totals[2] * grad_scale, totals[3] * grad_scale, totals[4] * grad_scale, totals[5] * grad_scale, totals[6] * grad_scale, totals[7] * grad_scale, totals[8] * grad_scale, totals[9] * grad_scale, totals[10] * grad_scale, totals[11] * grad_scale, totals[12] * grad_scale)
```

```python
import functools

import jax
import jax.numpy as jnp
from jax import lax
from jax.experimental import pallas as pl
from jax.experimental.pallas import tpu as pltpu
from jax.sharding import PartitionSpec as P

HEAD_DIM = 64
PAIR = 2 * HEAD_DIM
EPS = 1e-05
BIG = 1e30
f32 = jnp.float32
bf16 = jnp.bfloat16
NT = (((1,), (1,)), ((), ()))
NN = (((1,), (0,)), ((), ()))
TN = (((0,), (0,)), ((), ()))


def mm(a, b, dims=NN):
    return lax.dot_general(a, b, dims, preferred_element_type=f32)


def params(mb=56):
    return pltpu.CompilerParams(vmem_limit_bytes=mb << 20)


def cost(flops, nbytes, trans=0):
    return pl.CostEstimate(flops=int(flops), bytes_accessed=int(nbytes), transcendentals=int(trans))


def whole(shape):
    return pl.BlockSpec(shape, lambda *_: (0,) * len(shape), pipeline_mode=pl.Buffered(1))


def row_stats(x):
    mean = jnp.mean(x, axis=1, keepdims=True)
    cen = x - mean
    inv = lax.rsqrt(jnp.mean(cen * cen, axis=1, keepdims=True) + EPS)
    return cen * inv, inv


def norm_back(g, std, inv, gain):
    e = g * gain
    return inv * (e - jnp.mean(e, axis=1, keepdims=True) - std * jnp.mean(e * std, axis=1, keepdims=True))


def front_kernel(x_ref, s_ref, ws_ref, bs_ref, g_ref, b_ref, wj_ref, hid_ref, n1_ref, q_ref):
    w = x_ref.shape[1]
    hid = mm(x_ref[...], ws_ref[:w, :]) + mm(s_ref[...], ws_ref[w:, :]) + bs_ref[...].astype(f32)
    hid_ref[...] = hid
    std, _ = row_stats(hid)
    n1 = (std * g_ref[...].astype(f32) + b_ref[...].astype(f32)).astype(bf16)
    n1_ref[...] = n1
    q_ref[...] = mm(n1, wj_ref[...]).astype(bf16)


def front(x, s, ws, bs, g, b, wj, rb):
    n, w = x.shape
    c = wj.shape[1]
    row = lambda cols: pl.BlockSpec((rb, cols), lambda i: (i, 0))
    return pl.pallas_call(
        front_kernel,
        grid=(n // rb,),
        in_specs=[row(w), row(w), whole(ws.shape), whole((1, w)), whole((1, w)), whole((1, w)), whole(wj.shape)],
        out_specs=[row(w), row(w), row(c)],
        out_shape=[
            jax.ShapeDtypeStruct((n, w), f32),
            jax.ShapeDtypeStruct((n, w), bf16),
            jax.ShapeDtypeStruct((n, c), bf16),
        ],
        compiler_params=params(),
        cost_estimate=cost(2 * n * w * (2 * w + c), n * w * 20 + 5 * w * w * 2),
        name="front",
    )(x, s, ws, bs, g, b, wj)


def half_mask(h):
    lane = lax.broadcasted_iota(jnp.int32, (1, PAIR), 1)
    return (lane < HEAD_DIM) if h == 0 else (lane >= HEAD_DIM)


def eye_mask(t):
    return lax.broadcasted_iota(jnp.int32, (t, t), 0) == lax.broadcasted_iota(jnp.int32, (t, t), 1)


def pieces(x):
    a = x.astype(bf16)
    r = x - a.astype(f32)
    b = r.astype(bf16)
    c = (r - b.astype(f32)).astype(bf16)
    return a, b, c


def attn_fwd_kernel(q_ref, k_ref, v_ref, qf_ref, kf_ref, o_ref, feat_ref, ka_ref, vm_ref, s_ref, *, tq):
    n = q_ref.shape[0]
    ka_ref[:, :PAIR] = k_ref[...]
    ka_ref[:, PAIR:] = kf_ref[...]
    for h in range(2):
        vm_ref[h] = jnp.where(half_mask(h), v_ref[...], jnp.zeros_like(v_ref))
    eye = eye_mask(tq)
    lane = lax.broadcasted_iota(jnp.int32, (1, PAIR), 1)

    @pl.loop(0, n // tq)
    def _(i):
        start = pl.multiple_of(i * tq, tq)
        rows = pl.ds(start, tq)
        q = q_ref[rows, :] * jnp.asarray(HEAD_DIM**-0.5, bf16)
        qf = qf_ref[rows, :]
        kd = k_ref[rows, :]
        out = None
        for h in range(2):
            qm = jnp.where(half_mask(h), q, jnp.zeros_like(q))
            s_ref[h] = mm(jnp.concatenate([qm, qf], axis=1), ka_ref[...], NT)
            sd = mm(qm, kd, NT)
            s_ref[h, :, rows] = jnp.where(eye, sd, s_ref[h, :, rows])
        for h in range(2):
            s = s_ref[h]
            top = jnp.max(s, axis=1, keepdims=True)
            p = jnp.exp(s - top)
            total = jnp.sum(p, axis=1, keepdims=True)
            o = mm(p.astype(bf16), vm_ref[h]) / total
            out = o if out is None else out + o
            a, b, c = pieces(-(top + jnp.log(total)))
            feat = jnp.where(lane == 5, a, jnp.where(lane == 6, b, jnp.where(lane == 7, c, qf)))
            feat_ref[h, rows, :] = feat
        o_ref[rows, :] = out.astype(bf16)


def attn_fwd(packed, qf, kf, tq=128):
    n, c = packed.shape
    w = c // 3
    pairs = w // PAIR
    part = lambda p: pl.BlockSpec((n, PAIR), lambda j: (0, p * pairs + j))
    return pl.pallas_call(
        functools.partial(attn_fwd_kernel, tq=tq),
        grid=(pairs,),
        in_specs=[part(0), part(1), part(2), whole((n, PAIR)), whole((n, PAIR))],
        out_specs=[
            pl.BlockSpec((n, PAIR), lambda j: (0, j)),
            pl.BlockSpec((2, n, PAIR), lambda j: (j, 0, 0)),
        ],
        out_shape=[
            jax.ShapeDtypeStruct((n, w), bf16),
            jax.ShapeDtypeStruct((2 * pairs, n, PAIR), bf16),
        ],
        scratch_shapes=[
            pltpu.VMEM((n, 2 * PAIR), bf16),
            pltpu.VMEM((2, n, PAIR), bf16),
            pltpu.VMEM((2, tq, n), f32),
        ],
        compiler_params=params(),
        cost_estimate=cost(2 * n * n * (4 * PAIR) * pairs * 2, n * c * 4, n * n * 2 * pairs),
        name="attn_fwd",
    )(packed, packed, packed, qf, kf)


def attn_bwd_kernel(
    q_ref, k_ref, v_ref, o_ref, g_ref, feat_ref, kf_ref, out_ref, ka_ref, va_ref, qa_ref, ga_ref, dq_ref, st_ref, *, tk
):
    n = q_ref.shape[0]
    lane = lax.broadcasted_iota(jnp.int32, (1, PAIR), 1)
    none = jnp.zeros((1, PAIR), bf16)
    scale = HEAD_DIM**-0.5
    ka_ref[:, :PAIR] = k_ref[...]
    ka_ref[:, PAIR:] = kf_ref[...]
    va_ref[:, :PAIR] = v_ref[...]
    va_ref[:, PAIR:] = jnp.broadcast_to(jnp.where(lane < 3, 1.0, 0.0).astype(bf16), (n, PAIR))
    q = q_ref[...] * jnp.asarray(scale, bf16)
    g = g_ref[...]
    prod = g.astype(f32) * o_ref[...].astype(f32)
    for h in range(2):
        own = half_mask(h)
        qa_ref[h, :, :PAIR] = jnp.where(own, q, none)
        qa_ref[h, :, PAIR:] = feat_ref[h]
        ga_ref[h, :, :PAIR] = jnp.where(own, g, none)
        delta = jnp.sum(jnp.where(own, prod, 0.0), axis=1, keepdims=True)
        a, b, c = pieces(-delta)
        ga_ref[h, :, PAIR:] = jnp.where(lane == 0, a, jnp.where(lane == 1, b, jnp.where(lane == 2, c, none)))
    dq_ref[...] = jnp.zeros_like(dq_ref)
    eye = eye_mask(tk)

    @pl.loop(0, n // tk)
    def _(i):
        start = pl.multiple_of(i * tk, tk)
        rows = pl.ds(start, tk)
        ka = ka_ref[rows, :]
        k = k_ref[rows, :]
        kplain = jnp.concatenate([k, jnp.where(lane < 5, none, kf_ref[rows, :])], axis=1)
        va = va_ref[rows, :]
        for h in range(2):
            st_ref[h] = mm(ka, qa_ref[h], NT)
            sd = mm(kplain, qa_ref[h, rows, :], NT)
            st_ref[h, :, rows] = jnp.where(eye, sd, st_ref[h, :, rows])
        dv = None
        dk = None
        dq = None
        for h in range(2):
            p = jnp.exp(st_ref[h])
            dp = mm(va, ga_ref[h], NT)
            ds = (p * dp).astype(bf16)
            km = jnp.where(half_mask(h), k, none)
            dv_h = mm(p.astype(bf16), ga_ref[h, :, :PAIR])
            dk_h = mm(ds, qa_ref[h, :, :PAIR])
            dq_h = mm(ds, km, TN)
            dv = dv_h if dv is None else dv + dv_h
            dk = dk_h if dk is None else dk + dk_h
            dq = dq_h if dq is None else dq + dq_h
        dq_ref[...] += dq
        out_ref[1, rows, :] = dk.astype(bf16)
        out_ref[2, rows, :] = dv.astype(bf16)

    out_ref[0] = (dq_ref[...] * scale).astype(bf16)


def attn_bwd(packed, att, grad, feat, kf, tk=128):
    n, c = packed.shape
    w = c // 3
    pairs = w // PAIR
    part = lambda p: pl.BlockSpec((n, PAIR), lambda j: (0, p * pairs + j))
    return pl.pallas_call(
        functools.partial(attn_bwd_kernel, tk=tk),
        grid=(pairs,),
        in_specs=[
            part(0),
            part(1),
            part(2),
            part(0),
            part(0),
            pl.BlockSpec((2, n, PAIR), lambda j: (j, 0, 0)),
            whole((n, PAIR)),
        ],
        out_specs=pl.BlockSpec((3, n, PAIR), lambda j: (0, 0, j)),
        out_shape=jax.ShapeDtypeStruct((3, n, w), bf16),
        scratch_shapes=[
            pltpu.VMEM((n, 2 * PAIR), bf16),
            pltpu.VMEM((n, 2 * PAIR), bf16),
            pltpu.VMEM((2, n, 2 * PAIR), bf16),
            pltpu.VMEM((2, n, 2 * PAIR), bf16),
            pltpu.VMEM((n, PAIR), f32),
            pltpu.VMEM((2, tk, n), f32),
        ],
        compiler_params=params(),
        cost_estimate=cost(2 * n * n * (9 * PAIR) * pairs * 2, n * c * 8, n * n * 2 * pairs),
        name="attn_bwd",
    )(packed, packed, packed, att, grad, feat, kf)


def mid_kernel(a_ref, hid_ref, cot_ref, tw_ref, wo_ref, bo_ref, g_ref, b_ref, mid_ref, n2_ref, gr_ref, grt_ref):
    mid = hid_ref[...] + mm(a_ref[...], wo_ref[...]) + bo_ref[...].astype(f32)
    mid_ref[...] = mid
    std, _ = row_stats(mid)
    n2_ref[...] = (std * g_ref[...].astype(f32) + b_ref[...].astype(f32)).astype(bf16)
    gr = (cot_ref[...].astype(f32) * tw_ref[...]).astype(bf16)
    gr_ref[...] = gr
    grt_ref[...] = gr.T


def mid_part(att, hid, cot, tw, wo, bo, g, b, rb):
    n, w = att.shape
    row = lambda cols: pl.BlockSpec((rb, cols), lambda i: (i, 0))
    return pl.pallas_call(
        mid_kernel,
        grid=(n // rb,),
        in_specs=[row(w), row(w), row(w), row(1), whole(wo.shape), whole((1, w)), whole((1, w)), whole((1, w))],
        out_specs=[row(w), row(w), row(w), pl.BlockSpec((w, rb), lambda i: (0, i))],
        out_shape=[
            jax.ShapeDtypeStruct((n, w), f32),
            jax.ShapeDtypeStruct((n, w), bf16),
            jax.ShapeDtypeStruct((n, w), bf16),
            jax.ShapeDtypeStruct((w, n), bf16),
        ],
        compiler_params=params(),
        cost_estimate=cost(2 * n * w * w, n * w * 20),
        name="mid_part",
    )(att, hid, cot, tw, wo, bo, g, b)


def normal_cdf_pdf(u):
    a = jnp.abs(u)
    t = 1.0 / (1.0 + a * (0.3275911 * 0.7071067811865476))
    e = jnp.exp(-0.5 * u * u)
    half = 0.5
    poly = t * (
        half * 0.254829592
        + t * (half * -0.284496736 + t * (half * 1.421413741 + t * (half * -1.453152027 + t * (half * 1.061405429))))
    )
    tail = poly * e
    return jnp.where(u < 0, tail, 1.0 - tail), e * 0.3989422804014327


def ff_kernel(n2_ref, gr_ref, grt_ref, w1_ref, b1_ref, w2_ref, acc_ref, gn_ref, dw1_ref, dw2_ref, db1_ref):
    n2 = n2_ref[...]
    w1 = w1_ref[...]
    w2 = w2_ref[...]
    pre = mm(n2, w1) + b1_ref[...].astype(f32)
    cdf, pdf = normal_cdf_pdf(pre)
    act = (pre * cdf).astype(bf16)
    slope = cdf + pre * pdf
    gpre = (mm(gr_ref[...], w2, NT) * slope).astype(bf16)
    step = pl.program_id(0)

    @pl.when(step == 0)
    def _():
        acc_ref[...] = jnp.zeros_like(acc_ref)
        gn_ref[...] = jnp.zeros_like(gn_ref)

    acc_ref[...] += mm(act, w2)
    gn_ref[...] += mm(gpre, w1, NT)
    dw2_ref[...] = mm(grt_ref[...], act)
    dw1_ref[...] = mm(gpre, n2, TN)
    db1_ref[...] = jnp.sum(gpre.astype(f32), axis=0, keepdims=True)


def ff_part(n2, gr, grt, w1, b1, w2, fc=384):
    n, w = n2.shape
    ff = w1.shape[1]
    return pl.pallas_call(
        ff_kernel,
        grid=(ff // fc,),
        in_specs=[
            whole((n, w)),
            whole((n, w)),
            whole((w, n)),
            pl.BlockSpec((w, fc), lambda i: (0, i)),
            pl.BlockSpec((1, fc), lambda i: (0, i)),
            pl.BlockSpec((fc, w), lambda i: (i, 0)),
        ],
        out_specs=[
            whole((n, w)),
            whole((n, w)),
            pl.BlockSpec((fc, w), lambda i: (i, 0)),
            pl.BlockSpec((w, fc), lambda i: (0, i)),
            pl.BlockSpec((1, fc), lambda i: (0, i)),
        ],
        out_shape=[
            jax.ShapeDtypeStruct((n, w), f32),
            jax.ShapeDtypeStruct((n, w), f32),
            jax.ShapeDtypeStruct((ff, w), f32),
            jax.ShapeDtypeStruct((w, ff), f32),
            jax.ShapeDtypeStruct((1, ff), f32),
        ],
        compiler_params=params(),
        cost_estimate=cost(12 * n * w * ff, n * w * 14 + ff * w * 12, n * ff * 2),
        name="ff_part",
    )(n2, gr, grt, w1, b1, w2)


def back_kernel(
    mid_ref, acc_ref, gn_ref, cot_ref, tw_ref, gr_ref, a_ref, wo_ref, g_ref, b2_ref, out_ref, gm_ref, ga_ref, dwo_ref, vec_ref
):
    mid = mid_ref[...]
    out_ref[...] = (mid + acc_ref[...] + b2_ref[...].astype(f32)).astype(bf16)
    std, inv = row_stats(mid)
    gn = gn_ref[...]
    gm = cot_ref[...].astype(f32) * tw_ref[...] + norm_back(gn, std, inv, g_ref[...].astype(f32))
    gm_ref[...] = gm
    gb = gm.astype(bf16)
    ga_ref[...] = mm(gb, wo_ref[...], NT).astype(bf16)
    dwo = mm(gb, a_ref[...], TN)
    add = lambda x: jnp.sum(x, axis=0, keepdims=True)
    vec = jnp.concatenate([add(gb.astype(f32)), add(gn * std), add(gn), add(gr_ref[...].astype(f32))], axis=0)
    step = pl.program_id(0)

    @pl.when(step == 0)
    def _():
        dwo_ref[...] = dwo
        vec_ref[...] = vec

    @pl.when(step > 0)
    def _():
        dwo_ref[...] += dwo
        vec_ref[...] += vec


def back_part(mid, acc, gn, cot, tw, gr, att, wo, g, b2, rb):
    n, w = mid.shape
    row = lambda cols: pl.BlockSpec((rb, cols), lambda i: (i, 0))
    return pl.pallas_call(
        back_kernel,
        grid=(n // rb,),
        in_specs=[row(w), row(w), row(w), row(w), row(1), row(w), row(w), whole(wo.shape), whole((1, w)), whole((1, w))],
        out_specs=[row(w), row(w), row(w), whole((w, w)), whole((4, w))],
        out_shape=[
            jax.ShapeDtypeStruct((n, w), bf16),
            jax.ShapeDtypeStruct((n, w), f32),
            jax.ShapeDtypeStruct((n, w), bf16),
            jax.ShapeDtypeStruct((w, w), f32),
            jax.ShapeDtypeStruct((4, w), f32),
        ],
        compiler_params=params(),
        cost_estimate=cost(4 * n * w * w, n * w * 28),
        name="back_part",
    )(mid, acc, gn, cot, tw, gr, att, wo, g, b2)


def joint_grad_kernel(gp_ref, n1_ref, out_ref):
    out_ref[0] = mm(gp_ref[0], n1_ref[...], TN)


def joint_grad(gp, n1, cb=384):
    parts, n, w = gp.shape
    return pl.pallas_call(
        joint_grad_kernel,
        grid=(parts, w // cb),
        in_specs=[pl.BlockSpec((1, n, cb), lambda p, j: (p, 0, j)), whole((n, w))],
        out_specs=pl.BlockSpec((1, cb, w), lambda p, j: (p, j, 0)),
        out_shape=jax.ShapeDtypeStruct((parts, w, w), f32),
        compiler_params=params(),
        cost_estimate=cost(2 * parts * n * w * w, n * w * 8 + parts * w * w * 4),
        name="joint_grad",
    )(gp, n1)


def tail_kernel(gp_ref, hid_ref, gm_ref, wj_ref, g_ref, gh_ref, vec_ref):
    w = hid_ref.shape[1]
    gn = mm(gp_ref[0], wj_ref[:, :w], NT) + mm(gp_ref[1], wj_ref[:, w : 2 * w], NT) + mm(gp_ref[2], wj_ref[:, 2 * w :], NT)
    std, inv = row_stats(hid_ref[...])
    gh = (gm_ref[...] + norm_back(gn, std, inv, g_ref[...].astype(f32))).astype(bf16)
    gh_ref[...] = gh
    add = lambda x: jnp.sum(x, axis=0, keepdims=True)
    vec = jnp.concatenate([add(gn * std), add(gn), add(gh.astype(f32)), jnp.zeros((1, w), f32)], axis=0)
    step = pl.program_id(0)

    @pl.when(step == 0)
    def _():
        vec_ref[...] = vec

    @pl.when(step > 0)
    def _():
        vec_ref[...] += vec


def tail_part(gp, hid, gm, wj, g, rb):
    n, w = hid.shape
    row = lambda cols: pl.BlockSpec((rb, cols), lambda i: (i, 0))
    return pl.pallas_call(
        tail_kernel,
        grid=(n // rb,),
        in_specs=[pl.BlockSpec((3, rb, w), lambda i: (0, i, 0)), row(w), row(w), whole(wj.shape), whole((1, w))],
        out_specs=[row(w), whole((4, w))],
        out_shape=[jax.ShapeDtypeStruct((n, w), bf16), jax.ShapeDtypeStruct((4, w), f32)],
        compiler_params=params(),
        cost_estimate=cost(6 * n * w * w, n * w * 16),
        name="tail_part",
    )(gp, hid, gm, wj, g)


def skip_grad_kernel(gh_ref, x_ref, s_ref, out_ref):
    w = x_ref.shape[1]
    ght = gh_ref[...].T
    out_ref[:, :w] = mm(ght, x_ref[...])
    out_ref[:, w:] = mm(ght, s_ref[...])


def skip_grad(gh, x, s, cb=384):
    n, w = gh.shape
    return pl.pallas_call(
        skip_grad_kernel,
        grid=(w // cb,),
        in_specs=[pl.BlockSpec((n, cb), lambda j: (0, j)), whole((n, w)), whole((n, w))],
        out_specs=pl.BlockSpec((cb, 2 * w), lambda j: (j, 0)),
        out_shape=jax.ShapeDtypeStruct((w, 2 * w), f32),
        compiler_params=params(),
        cost_estimate=cost(4 * n * w * w, n * w * 6 + w * w * 8),
        name="skip_grad",
    )(gh, x, s)


def in_grad_kernel(gh_ref, ws_ref, a_ref, b_ref):
    w = a_ref.shape[1]
    gh = gh_ref[...]
    a_ref[...] = mm(gh, ws_ref[:w, :], NT).astype(bf16)
    b_ref[...] = mm(gh, ws_ref[w:, :], NT).astype(bf16)


def in_grad(gh, ws, rb):
    n, w = gh.shape
    row = lambda cols: pl.BlockSpec((rb, cols), lambda i: (i, 0))
    return pl.pallas_call(
        in_grad_kernel,
        grid=(n // rb,),
        in_specs=[row(w), whole(ws.shape)],
        out_specs=[row(w), row(w)],
        out_shape=[jax.ShapeDtypeStruct((n, w), bf16)] * 2,
        compiler_params=params(),
        cost_estimate=cost(4 * n * w * w, n * w * 10),
        name="in_grad",
    )(gh, ws)


def layout(lengths, keep, group_ids, group_counts, n, tokens_total):
    groups = group_counts.shape[0]
    slots = lengths.shape[0]
    ends = jnp.cumsum(lengths)
    pos = jnp.arange(n, dtype=jnp.int32)
    segment = jnp.sum((pos[:, None] >= ends[None, :]).astype(jnp.int32), axis=1)
    chosen = group_ids[:, None] == jnp.arange(groups, dtype=jnp.int32)[None, :]
    slot_count = jnp.sum(jnp.where(chosen, group_counts[None, :], 0), axis=1).astype(f32)
    slot_weight = tokens_total // groups / slot_count
    lane = jnp.arange(PAIR, dtype=jnp.int32)[None, :]
    same = segment[:, None] == lane
    weight_row = jnp.zeros((PAIR,), f32).at[:slots].set(slot_weight)[None, :]
    tw = jnp.sum(jnp.where(same, weight_row, 0.0), axis=1, keepdims=True)
    qf = same.astype(bf16)
    kf = jnp.where(lane <= slots, jnp.where(same & (keep[:, None] == 1), 0.0, -BIG), jnp.where(lane < slots + 4, 1.0, 0.0))
    return tw, qf, kf.astype(bf16)


def local_step(args, tokens_total):
    (inputs, skips, cot, lengths, keep, group_ids, group_counts, ws, bs, g1, s1, wj, wo, bo, g2, s2, w1, b1, w2, b2) = args
    n, w = inputs.shape
    rb = n // 3
    r = lambda v: v.reshape(1, -1)
    tw, qf, kf = layout(lengths, keep, group_ids, group_counts, n, tokens_total)
    hid, n1, packed = front(inputs, skips, ws, r(bs), r(g1), r(s1), wj, rb)
    att, feat = attn_fwd(packed, qf, kf)
    mid, n2, gr, grt = mid_part(att, hid, cot, tw, wo, r(bo), r(g2), r(s2), rb)
    acc, gn2, dw1t, dw2t, db1 = ff_part(n2, gr, grt, w1, r(b1), w2)
    outcome, gm, gatt, dwot, vec2 = back_part(mid, acc, gn2, cot, tw, gr, att, wo, r(g2), r(b2), rb)
    gp = attn_bwd(packed, att, gatt, feat, kf)
    dwjt = joint_grad(gp, n1)
    gh, vec1 = tail_part(gp, hid, gm, wj, r(g1), rb)
    dwst = skip_grad(gh, inputs, skips)
    igrad, sgrad = in_grad(gh, ws, rb)
    vecs = (vec1[2], vec1[0], vec1[1], vec2[0], vec2[1], vec2[2], db1[0], vec2[3])
    return (outcome, igrad, sgrad), (dwst, dwjt.reshape(3 * w, w), dwot, dw1t, dw2t), vecs


def per_device(*args):
    n = args[0].shape[0]
    tokens_total = n * lax.axis_size("dp") * lax.axis_size("rep")
    scale = float(tokens_total) ** -0.5
    rows, mats, vecs = local_step(args, tokens_total)
    scatter = lambda x: lax.psum_scatter(x, "dp", scatter_dimension=0, tiled=True)
    mats = [scatter(m) for m in mats]
    vecs = [scatter(v) for v in vecs]
    mats, vecs = lax.psum((mats, vecs), "rep")
    ds, dj, do, d1, d2 = [m.T * scale for m in mats]
    bs, g1, s1, bo, g2, s2, b1, b2 = [v * scale for v in vecs]
    return (*rows, ds, bs, g1, s1, dj, do, bo, g2, s2, d1, b1, d2, b2)


def solution(mesh):
    both = ("dp", "rep")
    in_specs = (P(both, None),) * 3 + (P(both),) * 3 + (P(),) * 14
    cols = P(None, "dp")
    vec = P("dp")
    out_specs = (P(both, None),) * 3 + (cols, vec, vec, vec, cols, cols, vec, vec, vec, cols, vec, cols, vec)
    return jax.shard_map(per_device, mesh=mesh, in_specs=in_specs, out_specs=out_specs, check_vma=False)
```

```python
import functools

import jax
import jax.numpy as jnp
from jax import lax
from jax.experimental import pallas as pl
from jax.experimental.pallas import tpu as pltpu
from jax.sharding import PartitionSpec as P

HEAD_DIM = 64
PAIR = 2 * HEAD_DIM
EPS = 1e-05
BIG = 1e30
f32 = jnp.float32
bf16 = jnp.bfloat16
NT = (((1,), (1,)), ((), ()))
NN = (((1,), (0,)), ((), ()))
TN = (((0,), (0,)), ((), ()))


def mm(a, b, dims=NN):
    return lax.dot_general(a, b, dims, preferred_element_type=f32)


def params(mb=56):
    return pltpu.CompilerParams(vmem_limit_bytes=mb << 20)


def cost(flops, nbytes, trans=0):
    return pl.CostEstimate(flops=int(flops), bytes_accessed=int(nbytes), transcendentals=int(trans))


def whole(shape):
    return pl.BlockSpec(shape, lambda *_: (0,) * len(shape), pipeline_mode=pl.Buffered(1))


def row_stats(x):
    mean = jnp.mean(x, axis=1, keepdims=True)
    cen = x - mean
    inv = lax.rsqrt(jnp.mean(cen * cen, axis=1, keepdims=True) + EPS)
    return cen * inv, inv


def norm_back(g, std, inv, gain):
    e = g * gain
    return inv * (e - jnp.mean(e, axis=1, keepdims=True) - std * jnp.mean(e * std, axis=1, keepdims=True))


def can_split(rows, m):
    return m % 8 == 0 and rows % (2 * m) == 0


def split_store(val, refs, core, m):
    rows, cols = val.shape
    parts = val.reshape(rows // (2 * m), 2, m, cols)
    low, high = parts[:, 0], parts[:, 1]
    refs[0][...] = jnp.where(core == 0, low, high)
    refs[1][...] = jnp.where(core == 0, high, low)


def put(val, refs, core, m):
    if len(refs) == 2:
        split_store(val, refs, core, m)
    else:
        refs[0][...] = val


SMEM1 = pl.BlockSpec(memory_space=pltpu.SMEM)


def front_kernel(x_ref, s_ref, ws_ref, bs_ref, g_ref, b_ref, wj_ref, hid_ref, n1_ref, q_ref):
    w = x_ref.shape[1]
    hid = mm(x_ref[...], ws_ref[:w, :]) + mm(s_ref[...], ws_ref[w:, :]) + bs_ref[...].astype(f32)
    hid_ref[...] = hid
    std, _ = row_stats(hid)
    n1 = (std * g_ref[...].astype(f32) + b_ref[...].astype(f32)).astype(bf16)
    n1_ref[...] = n1
    q_ref[...] = mm(n1, wj_ref[...]).astype(bf16)


def front(x, s, ws, bs, g, b, wj, rb):
    n, w = x.shape
    c = wj.shape[1]
    row = lambda cols: pl.BlockSpec((rb, cols), lambda i: (i, 0))
    return pl.pallas_call(
        front_kernel,
        grid=(n // rb,),
        in_specs=[row(w), row(w), whole(ws.shape), whole((1, w)), whole((1, w)), whole((1, w)), whole(wj.shape)],
        out_specs=[row(w), row(w), row(c)],
        out_shape=[
            jax.ShapeDtypeStruct((n, w), f32),
            jax.ShapeDtypeStruct((n, w), bf16),
            jax.ShapeDtypeStruct((n, c), bf16),
        ],
        compiler_params=params(),
        cost_estimate=cost(2 * n * w * (2 * w + c), n * w * 20 + 5 * w * w * 2),
        name="front",
    )(x, s, ws, bs, g, b, wj)


def half_mask(h):
    lane = lax.broadcasted_iota(jnp.int32, (1, PAIR), 1)
    return (lane < HEAD_DIM) if h == 0 else (lane >= HEAD_DIM)


def eye_mask(t):
    return lax.broadcasted_iota(jnp.int32, (t, t), 0) == lax.broadcasted_iota(jnp.int32, (t, t), 1)


def pieces(x):
    a = x.astype(bf16)
    r = x - a.astype(f32)
    b = r.astype(bf16)
    c = (r - b.astype(f32)).astype(bf16)
    return a, b, c


def attn_fwd_kernel(q_ref, k_ref, v_ref, qf_ref, kf_ref, o_ref, feat_ref, ka_ref, vm_ref, s_ref, *, tq):
    n = q_ref.shape[0]
    ka_ref[:, :PAIR] = k_ref[...]
    ka_ref[:, PAIR:] = kf_ref[...]
    for h in range(2):
        vm_ref[h] = jnp.where(half_mask(h), v_ref[...], jnp.zeros_like(v_ref))
    eye = eye_mask(tq)
    lane = lax.broadcasted_iota(jnp.int32, (1, PAIR), 1)

    @pl.loop(0, n // tq)
    def _(i):
        start = pl.multiple_of(i * tq, tq)
        rows = pl.ds(start, tq)
        q = q_ref[rows, :] * jnp.asarray(HEAD_DIM**-0.5, bf16)
        qf = qf_ref[rows, :]
        kd = k_ref[rows, :]
        out = None
        for h in range(2):
            qm = jnp.where(half_mask(h), q, jnp.zeros_like(q))
            s_ref[h] = mm(jnp.concatenate([qm, qf], axis=1), ka_ref[...], NT)
            sd = mm(qm, kd, NT)
            s_ref[h, :, rows] = jnp.where(eye, sd, s_ref[h, :, rows])
        for h in range(2):
            s = s_ref[h]
            top = jnp.max(s, axis=1, keepdims=True)
            p = jnp.exp(s - top)
            total = jnp.sum(p, axis=1, keepdims=True)
            o = mm(p.astype(bf16), vm_ref[h]) / total
            out = o if out is None else out + o
            a, b, c = pieces(-(top + jnp.log(total)))
            feat = jnp.where(lane == 5, a, jnp.where(lane == 6, b, jnp.where(lane == 7, c, qf)))
            feat_ref[h, rows, :] = feat
        o_ref[rows, :] = out.astype(bf16)


def attn_fwd(packed, qf, kf, tq=128):
    n, c = packed.shape
    w = c // 3
    pairs = w // PAIR
    part = lambda p: pl.BlockSpec((n, PAIR), lambda j: (0, p * pairs + j))
    return pl.pallas_call(
        functools.partial(attn_fwd_kernel, tq=tq),
        grid=(pairs,),
        in_specs=[part(0), part(1), part(2), whole((n, PAIR)), whole((n, PAIR))],
        out_specs=[
            pl.BlockSpec((n, PAIR), lambda j: (0, j)),
            pl.BlockSpec((2, n, PAIR), lambda j: (j, 0, 0)),
        ],
        out_shape=[
            jax.ShapeDtypeStruct((n, w), bf16),
            jax.ShapeDtypeStruct((2 * pairs, n, PAIR), bf16),
        ],
        scratch_shapes=[
            pltpu.VMEM((n, 2 * PAIR), bf16),
            pltpu.VMEM((2, n, PAIR), bf16),
            pltpu.VMEM((2, tq, n), f32),
        ],
        compiler_params=params(),
        cost_estimate=cost(2 * n * n * (4 * PAIR) * pairs * 2, n * c * 4, n * n * 2 * pairs),
        name="attn_fwd",
    )(packed, packed, packed, qf, kf)


def attn_bwd_kernel(
    q_ref, k_ref, v_ref, o_ref, g_ref, feat_ref, kf_ref, *rest, tk
):
    out_ref, ka_ref, va_ref, qa_ref, ga_ref, dq_ref, st_ref = rest[-7:]
    n = q_ref.shape[0]
    lane = lax.broadcasted_iota(jnp.int32, (1, PAIR), 1)
    none = jnp.zeros((1, PAIR), bf16)
    scale = HEAD_DIM**-0.5
    ka_ref[:, :PAIR] = k_ref[...]
    ka_ref[:, PAIR:] = kf_ref[...]
    va_ref[:, :PAIR] = v_ref[...]
    va_ref[:, PAIR:] = jnp.broadcast_to(jnp.where(lane < 3, 1.0, 0.0).astype(bf16), (n, PAIR))
    q = q_ref[...] * jnp.asarray(scale, bf16)
    g = g_ref[...]
    prod = g.astype(f32) * o_ref[...].astype(f32)
    for h in range(2):
        own = half_mask(h)
        qa_ref[h, :, :PAIR] = jnp.where(own, q, none)
        qa_ref[h, :, PAIR:] = feat_ref[h]
        ga_ref[h, :, :PAIR] = jnp.where(own, g, none)
        delta = jnp.sum(jnp.where(own, prod, 0.0), axis=1, keepdims=True)
        a, b, c = pieces(-delta)
        ga_ref[h, :, PAIR:] = jnp.where(lane == 0, a, jnp.where(lane == 1, b, jnp.where(lane == 2, c, none)))
    dq_ref[...] = jnp.zeros_like(dq_ref)
    eye = eye_mask(tk)

    @pl.loop(0, n // tk)
    def _(i):
        start = pl.multiple_of(i * tk, tk)
        rows = pl.ds(start, tk)
        ka = ka_ref[rows, :]
        k = k_ref[rows, :]
        kplain = jnp.concatenate([k, jnp.where(lane < 5, none, kf_ref[rows, :])], axis=1)
        va = va_ref[rows, :]
        for h in range(2):
            st_ref[h] = mm(ka, qa_ref[h], NT)
            sd = mm(kplain, qa_ref[h, rows, :], NT)
            st_ref[h, :, rows] = jnp.where(eye, sd, st_ref[h, :, rows])
        dv = None
        dk = None
        dq = None
        for h in range(2):
            p = jnp.exp(st_ref[h])
            dp = mm(va, ga_ref[h], NT)
            ds = (p * dp).astype(bf16)
            km = jnp.where(half_mask(h), k, none)
            dv_h = mm(p.astype(bf16), ga_ref[h, :, :PAIR])
            dk_h = mm(ds, qa_ref[h, :, :PAIR])
            dq_h = mm(ds, km, TN)
            dv = dv_h if dv is None else dv + dv_h
            dk = dk_h if dk is None else dk + dk_h
            dq = dq_h if dq is None else dq + dq_h
        dq_ref[...] += dq
        out_ref[1, rows, :] = dk.astype(bf16)
        out_ref[2, rows, :] = dv.astype(bf16)

    out_ref[0] = (dq_ref[...] * scale).astype(bf16)


def attn_bwd(packed, att, grad, feat, kf, first, count, prev, tk=128):
    n, c = packed.shape
    w = c // 3
    pairs = w // PAIR
    part = lambda p: pl.BlockSpec((n, PAIR), lambda j: (0, p * pairs + first + j))
    extra = [] if prev is None else [prev]
    return pl.pallas_call(
        functools.partial(attn_bwd_kernel, tk=tk),
        grid=(count,),
        in_specs=[
            part(0),
            part(1),
            part(2),
            part(0),
            part(0),
            pl.BlockSpec((2, n, PAIR), lambda j: (first + j, 0, 0)),
            whole((n, PAIR)),
        ]
        + [pl.BlockSpec(memory_space=pl.ANY)] * len(extra),
        out_specs=pl.BlockSpec((3, n, PAIR), lambda j: (0, 0, first + j)),
        out_shape=jax.ShapeDtypeStruct((3, n, w), bf16),
        input_output_aliases={7: 0} if extra else {},
        scratch_shapes=[
            pltpu.VMEM((n, 2 * PAIR), bf16),
            pltpu.VMEM((n, 2 * PAIR), bf16),
            pltpu.VMEM((2, n, 2 * PAIR), bf16),
            pltpu.VMEM((2, n, 2 * PAIR), bf16),
            pltpu.VMEM((n, PAIR), f32),
            pltpu.VMEM((2, tk, n), f32),
        ],
        compiler_params=params(),
        cost_estimate=cost(2 * n * n * (9 * PAIR) * count * 2, n * PAIR * 16 * count, n * n * 2 * count),
        name="attn_bwd",
    )(packed, packed, packed, att, grad, feat, kf, *extra)


def mid_kernel(a_ref, hid_ref, cot_ref, tw_ref, wo_ref, bo_ref, g_ref, b_ref, mid_ref, n2_ref, gr_ref, grt_ref):
    mid = hid_ref[...] + mm(a_ref[...], wo_ref[...]) + bo_ref[...].astype(f32)
    mid_ref[...] = mid
    std, _ = row_stats(mid)
    n2_ref[...] = (std * g_ref[...].astype(f32) + b_ref[...].astype(f32)).astype(bf16)
    gr = (cot_ref[...].astype(f32) * tw_ref[...]).astype(bf16)
    gr_ref[...] = gr
    grt_ref[...] = gr.T


def mid_part(att, hid, cot, tw, wo, bo, g, b, rb):
    n, w = att.shape
    row = lambda cols: pl.BlockSpec((rb, cols), lambda i: (i, 0))
    return pl.pallas_call(
        mid_kernel,
        grid=(n // rb,),
        in_specs=[row(w), row(w), row(w), row(1), whole(wo.shape), whole((1, w)), whole((1, w)), whole((1, w))],
        out_specs=[row(w), row(w), row(w), pl.BlockSpec((w, rb), lambda i: (0, i))],
        out_shape=[
            jax.ShapeDtypeStruct((n, w), f32),
            jax.ShapeDtypeStruct((n, w), bf16),
            jax.ShapeDtypeStruct((n, w), bf16),
            jax.ShapeDtypeStruct((w, n), bf16),
        ],
        compiler_params=params(),
        cost_estimate=cost(2 * n * w * w, n * w * 20),
        name="mid_part",
    )(att, hid, cot, tw, wo, bo, g, b)


def normal_cdf_pdf(u):
    a = jnp.abs(u)
    t = 1.0 / (1.0 + a * (0.3275911 * 0.7071067811865476))
    e = jnp.exp(-0.5 * u * u)
    half = 0.5
    poly = t * (
        half * 0.254829592
        + t * (half * -0.284496736 + t * (half * 1.421413741 + t * (half * -1.453152027 + t * (half * 1.061405429))))
    )
    tail = poly * e
    return jnp.where(u < 0, tail, 1.0 - tail), e * 0.3989422804014327


def ff_kernel(core_ref, n2_ref, gr_ref, grt_ref, w1_ref, b1_ref, w2_ref, *rest, first, split1, split2, m1, m2):
    outs = rest if first else rest[2:]
    acc_ref, gn_ref, db1_ref = outs[:3]
    dw1_refs, dw2_refs = outs[3 : 3 + split1], outs[3 + split1 :]
    core = core_ref[0]
    n2 = n2_ref[...]
    w1 = w1_ref[...]
    w2 = w2_ref[...]
    pre = mm(n2, w1) + b1_ref[...].astype(f32)
    cdf, pdf = normal_cdf_pdf(pre)
    act = (pre * cdf).astype(bf16)
    slope = cdf + pre * pdf
    gpre = (mm(gr_ref[...], w2, NT) * slope).astype(bf16)

    @pl.when(pl.program_id(0) == 0)
    def _():
        if first:
            acc_ref[...] = jnp.zeros_like(acc_ref)
            gn_ref[...] = jnp.zeros_like(gn_ref)
        else:
            acc_ref[...] = rest[0][...]
            gn_ref[...] = rest[1][...]

    acc_ref[...] += mm(act, w2)
    gn_ref[...] += mm(gpre, w1, NT)
    put(mm(gpre, n2, TN), dw1_refs, core, m1)
    put(mm(grt_ref[...], act), dw2_refs, core, m2)
    db1_ref[...] = jnp.sum(gpre.astype(f32), axis=0, keepdims=True)


def ff_part(core, n2, gr, grt, w1, b1, w2, part, parts, prev, dp, fc=384):
    n, w = n2.shape
    ff = w1.shape[1]
    mine = ff // parts
    steps = mine // fc
    base = part * steps
    m1, m2 = ff // dp, w // dp
    first = prev is None
    if can_split(fc, m1):
        d1_spec = [pl.BlockSpec((fc // (2 * m1), m1, w), lambda i: (i, 0, 0))] * 2
        d1_shape = [jax.ShapeDtypeStruct((mine // (2 * m1), m1, w), f32)] * 2
    else:
        d1_spec = [pl.BlockSpec((fc, w), lambda i: (i, 0))]
        d1_shape = [jax.ShapeDtypeStruct((mine, w), f32)]
    if can_split(w, m2):
        d2_spec = [pl.BlockSpec((dp // 2, m2, fc), lambda i: (0, 0, i))] * 2
        d2_shape = [jax.ShapeDtypeStruct((dp // 2, m2, mine), f32)] * 2
    else:
        d2_spec = [pl.BlockSpec((w, fc), lambda i: (0, i))]
        d2_shape = [jax.ShapeDtypeStruct((w, mine), f32)]
    extra = [] if first else list(prev)
    res = pl.pallas_call(
        functools.partial(ff_kernel, first=first, split1=len(d1_spec), split2=len(d2_spec), m1=m1, m2=m2),
        grid=(steps,),
        in_specs=[
            SMEM1,
            whole((n, w)),
            whole((n, w)),
            whole((w, n)),
            pl.BlockSpec((w, fc), lambda i: (0, base + i)),
            pl.BlockSpec((1, fc), lambda i: (0, base + i)),
            pl.BlockSpec((fc, w), lambda i: (base + i, 0)),
        ]
        + [whole((n, w))] * len(extra),
        out_specs=[whole((n, w)), whole((n, w)), pl.BlockSpec((1, fc), lambda i: (0, i))] + d1_spec + d2_spec,
        out_shape=[
            jax.ShapeDtypeStruct((n, w), f32),
            jax.ShapeDtypeStruct((n, w), f32),
            jax.ShapeDtypeStruct((1, mine), f32),
        ]
        + d1_shape
        + d2_shape,
        compiler_params=params(60),
        cost_estimate=cost(12 * n * w * mine, n * w * 14 + mine * w * 12, n * mine * 2),
        name="ff_part",
    )(core, n2, gr, grt, w1, b1, w2, *extra)
    acc, gn, db1 = res[:3]
    k = 3 + len(d1_spec)
    return (acc, gn), db1, res[3:k], res[k:]


def back_kernel(
    core_ref, mid_ref, acc_ref, gn_ref, cot_ref, tw_ref, gr_ref, a_ref, wo_ref, g_ref, b2_ref, out_ref, gm_ref, ga_ref, vec_ref, *rest, m
):
    dwo_refs, dwo_ref = rest[:-1], rest[-1]
    mid = mid_ref[...]
    out_ref[...] = (mid + acc_ref[...] + b2_ref[...].astype(f32)).astype(bf16)
    std, inv = row_stats(mid)
    gn = gn_ref[...]
    gm = cot_ref[...].astype(f32) * tw_ref[...] + norm_back(gn, std, inv, g_ref[...].astype(f32))
    gm_ref[...] = gm
    gb = gm.astype(bf16)
    ga_ref[...] = mm(gb, wo_ref[...], NT).astype(bf16)
    dwo = mm(gb, a_ref[...], TN)
    add = lambda x: jnp.sum(x, axis=0, keepdims=True)
    vec = jnp.concatenate([add(gb.astype(f32)), add(gn * std), add(gn), add(gr_ref[...].astype(f32))], axis=0)
    step = pl.program_id(0)

    @pl.when(step == 0)
    def _():
        dwo_ref[...] = dwo
        vec_ref[...] = vec

    @pl.when(step > 0)
    def _():
        dwo_ref[...] += dwo
        vec_ref[...] += vec

    @pl.when(step == pl.num_programs(0) - 1)
    def _():
        put(dwo_ref[...], dwo_refs, core_ref[0], m)


def grad_outs(rows, cols, m):
    if can_split(rows, m):
        shape = (rows // (2 * m), m, cols)
        return [whole(shape)] * 2, [jax.ShapeDtypeStruct(shape, f32)] * 2
    return [whole((rows, cols))], [jax.ShapeDtypeStruct((rows, cols), f32)]


def back_part(core, dp, mid, acc, gn, cot, tw, gr, att, wo, g, b2, rb):
    n, w = mid.shape
    row = lambda cols: pl.BlockSpec((rb, cols), lambda i: (i, 0))
    specs, shapes = grad_outs(w, w, w // dp)
    res = pl.pallas_call(
        functools.partial(back_kernel, m=w // dp),
        grid=(n // rb,),
        in_specs=[SMEM1, row(w), row(w), row(w), row(w), row(1), row(w), row(w), whole(wo.shape), whole((1, w)), whole((1, w))],
        out_specs=[row(w), row(w), row(w), whole((4, w))] + specs,
        out_shape=[
            jax.ShapeDtypeStruct((n, w), bf16),
            jax.ShapeDtypeStruct((n, w), f32),
            jax.ShapeDtypeStruct((n, w), bf16),
            jax.ShapeDtypeStruct((4, w), f32),
        ]
        + shapes,
        scratch_shapes=[pltpu.VMEM((w, w), f32)],
        compiler_params=params(),
        cost_estimate=cost(4 * n * w * w, n * w * 28),
        name="back_part",
    )(core, mid, acc, gn, cot, tw, gr, att, wo, g, b2)
    return res[0], res[1], res[2], res[3], res[4:]


def joint_grad_kernel(core_ref, gp_ref, n1_ref, *rest, m):
    refs, gpt_ref = rest[:-1], rest[-1]
    parts, n, w = gp_ref.shape
    half = len(refs) // 2
    step = pl.program_id(0)

    @pl.when(step == 0)
    def _():
        for p in range(parts):
            gpt_ref[p * w : (p + 1) * w, :] = gp_ref[p].T

    for side in range(2):

        @pl.when(step == side)
        def _():
            put(mm(gpt_ref[...], n1_ref[...]), refs[side * half : (side + 1) * half], core_ref[0], m)


def joint_grad(core, dp, gp, n1):
    parts, n, w = gp.shape
    cb = w // 2
    specs, shapes = grad_outs(parts * w, cb, parts * w // dp)
    res = pl.pallas_call(
        functools.partial(joint_grad_kernel, m=parts * w // dp),
        grid=(2,),
        in_specs=[SMEM1, whole((parts, n, w)), pl.BlockSpec((n, cb), lambda j: (0, j))],
        out_specs=specs * 2,
        out_shape=shapes * 2,
        scratch_shapes=[pltpu.VMEM((parts * w, n), bf16)],
        compiler_params=params(),
        cost_estimate=cost(2 * parts * n * w * w, n * w * 8 + parts * w * w * 4),
        name="joint_grad",
    )(core, gp, n1)
    k = len(specs)
    return res[:k], res[k:]


def tail_kernel(gp_ref, hid_ref, gm_ref, wj_ref, g_ref, gh_ref, vec_ref):
    w = hid_ref.shape[1]
    gn = mm(gp_ref[0], wj_ref[:, :w], NT) + mm(gp_ref[1], wj_ref[:, w : 2 * w], NT) + mm(gp_ref[2], wj_ref[:, 2 * w :], NT)
    std, inv = row_stats(hid_ref[...])
    gh = (gm_ref[...] + norm_back(gn, std, inv, g_ref[...].astype(f32))).astype(bf16)
    gh_ref[...] = gh
    add = lambda x: jnp.sum(x, axis=0, keepdims=True)
    vec = jnp.concatenate([add(gn * std), add(gn), add(gh.astype(f32)), jnp.zeros((1, w), f32)], axis=0)
    step = pl.program_id(0)

    @pl.when(step == 0)
    def _():
        vec_ref[...] = vec

    @pl.when(step > 0)
    def _():
        vec_ref[...] += vec


def tail_part(gp, hid, gm, wj, g, rb):
    n, w = hid.shape
    row = lambda cols: pl.BlockSpec((rb, cols), lambda i: (i, 0))
    return pl.pallas_call(
        tail_kernel,
        grid=(n // rb,),
        in_specs=[pl.BlockSpec((3, rb, w), lambda i: (0, i, 0)), row(w), row(w), whole(wj.shape), whole((1, w))],
        out_specs=[row(w), whole((4, w))],
        out_shape=[jax.ShapeDtypeStruct((n, w), bf16), jax.ShapeDtypeStruct((4, w), f32)],
        compiler_params=params(),
        cost_estimate=cost(6 * n * w * w, n * w * 16),
        name="tail_part",
    )(gp, hid, gm, wj, g)


def skip_grad_kernel(core_ref, gh_ref, x_ref, s_ref, vec_ref, *refs, m):
    half = len(refs) // 2
    ght = gh_ref[...].T
    put(mm(ght, x_ref[...]), refs[:half], core_ref[0], m)
    side = jnp.concatenate([mm(ght, s_ref[...]), vec_ref[...]], axis=1)
    put(side, refs[half:], core_ref[0], m)


def skip_grad(core, dp, gh, x, s, vec):
    n, w = gh.shape
    m = w // dp
    spec_a, shape_a = grad_outs(w, w, m)
    spec_b, shape_b = grad_outs(w, w + vec.shape[1], m)
    res = pl.pallas_call(
        functools.partial(skip_grad_kernel, m=m),
        grid=(1,),
        in_specs=[SMEM1, whole((n, w)), whole((n, w)), whole((n, w)), whole(vec.shape)],
        out_specs=spec_a + spec_b,
        out_shape=shape_a + shape_b,
        compiler_params=params(),
        cost_estimate=cost(4 * n * w * w, n * w * 6 + w * w * 8),
        name="skip_grad",
    )(core, gh, x, s, vec)
    k = len(spec_a)
    return res[:k], res[k:]


def in_grad_kernel(gh_ref, ws_ref, a_ref, b_ref):
    w = a_ref.shape[1]
    gh = gh_ref[...]
    a_ref[...] = mm(gh, ws_ref[:w, :], NT).astype(bf16)
    b_ref[...] = mm(gh, ws_ref[w:, :], NT).astype(bf16)


def in_grad(gh, ws, rb):
    n, w = gh.shape
    row = lambda cols: pl.BlockSpec((rb, cols), lambda i: (i, 0))
    return pl.pallas_call(
        in_grad_kernel,
        grid=(n // rb,),
        in_specs=[row(w), whole(ws.shape)],
        out_specs=[row(w), row(w)],
        out_shape=[jax.ShapeDtypeStruct((n, w), bf16)] * 2,
        compiler_params=params(),
        cost_estimate=cost(4 * n * w * w, n * w * 10),
        name="in_grad",
    )(gh, ws)


def layout(lengths, keep, group_ids, group_counts, n, tokens_total):
    groups = group_counts.shape[0]
    slots = lengths.shape[0]
    ends = jnp.cumsum(lengths)
    pos = jnp.arange(n, dtype=jnp.int32)
    segment = jnp.sum((pos[:, None] >= ends[None, :]).astype(jnp.int32), axis=1)
    chosen = group_ids[:, None] == jnp.arange(groups, dtype=jnp.int32)[None, :]
    slot_count = jnp.sum(jnp.where(chosen, group_counts[None, :], 0), axis=1).astype(f32)
    slot_weight = tokens_total // groups / slot_count
    lane = jnp.arange(PAIR, dtype=jnp.int32)[None, :]
    same = segment[:, None] == lane
    weight_row = jnp.zeros((PAIR,), f32).at[:slots].set(slot_weight)[None, :]
    tw = jnp.sum(jnp.where(same, weight_row, 0.0), axis=1, keepdims=True)
    qf = same.astype(bf16)
    kf = jnp.where(lane <= slots, jnp.where(same & (keep[:, None] == 1), 0.0, -BIG), jnp.where(lane < slots + 4, 1.0, 0.0))
    return tw, qf, kf.astype(bf16)


def pick(x, axis, index):
    return lax.dynamic_index_in_dim(x, index, axis, keepdims=False)


class Reducer:
    def __init__(self, refs, rows, cols, dp, top=True):
        self.dp = dp
        self.bits = dp.bit_length() - 1
        self.place = lax.axis_index("dp")
        self.side = lax.axis_index("rep")
        owners = dp if top else dp // 2
        m = rows // owners
        if len(refs) == 1:
            full = refs[0].reshape(owners // 2, 2, m, cols)
            core = self.place & 1
            refs = [pick(full, 1, core), pick(full, 1, 1 - core)]
        keep, send = refs
        self.names = [b for b in range(self.bits - 1, 0, -1) if top or b != self.bits - 1] + ["x"]
        got = self.swap(send, 0)
        shape = (2,) * (len(self.names)) + (m // 2, cols)
        self.terms = [keep.reshape(shape), got.reshape(shape)]

    def swap(self, x, name):
        if name == "x":
            return lax.ppermute(x, "rep", [(0, 1), (1, 0)])
        return lax.ppermute(x, "dp", [(i, i ^ (1 << name)) for i in range(self.dp)])

    def bit(self, name):
        return self.side if name == "x" else (self.place >> name) & 1

    def halve(self, name):
        axis = self.names.index(name)
        mine = self.bit(name)
        send = sum(pick(t, axis, 1 - mine) for t in self.terms)
        got = self.swap(send, name)
        self.terms = [pick(t, axis, mine) for t in self.terms] + [got]
        self.names.pop(axis)

    def total(self):
        return sum(self.terms)


def join_top(low, high):
    name = low.bits - 1
    mine = low.bit(name)
    a, b = low.total(), high.total()
    send = jnp.where(mine == 0, b, a)
    got = low.swap(send, name)
    return jnp.where(mine == 0, a, b) + got


def both_sides(x, side):
    other = lax.ppermute(x, "rep", [(0, 1), (1, 0)])
    return jnp.concatenate([jnp.where(side == 0, x, other), jnp.where(side == 0, other, x)], axis=0)


def per_device(*args):
    (inputs, skips, cot, lengths, keep, group_ids, group_counts, ws, bs, g1, s1, wj, wo, bo, g2, s2, w1, b1, w2, b2) = args
    n, w = inputs.shape
    ff = w1.shape[1]
    dp = lax.axis_size("dp")
    tokens_total = n * dp * lax.axis_size("rep")
    scale = float(tokens_total) ** -0.5
    place = lax.axis_index("dp")
    side = lax.axis_index("rep")
    core = (place & 1).astype(jnp.int32).reshape(1)
    rb = n // 3
    r = lambda v: v.reshape(1, -1)
    bits = dp.bit_length() - 1
    later = list(range(2, bits))

    tw, qf, kf = layout(lengths, keep, group_ids, group_counts, n, tokens_total)
    hid, n1, packed = front(inputs, skips, ws, r(bs), r(g1), r(s1), wj, rb)
    att, feat = attn_fwd(packed, qf, kf)
    mid, n2, gr, grt = mid_part(att, hid, cot, tw, wo, r(bo), r(g2), r(s2), rb)

    carry = None
    red1, red2, db1 = [], [], []
    for part in range(2):
        carry, db, d1, d2 = ff_part(core, n2, gr, grt, w1, r(b1), w2, part, 2, carry, dp)
        db1.append(db)
        red1.append(Reducer(d1, ff // 2, w, dp, top=False))
        red2.append(Reducer(d2, w, ff // 2, dp))
    acc, gn2 = carry
    outcome, gm, gatt, vec2, do = back_part(core, dp, mid, acc, gn2, cot, tw, gr, att, wo, r(g2), r(b2), rb)
    redo = Reducer(do, w, w, dp)

    for part in range(2):
        for name in ["x", 1] + later[:-1]:
            red1[part].halve(name)
        for name in [1, "x"] + later:
            red2[part].halve(name)
    for name in later + ["x", 1]:
        redo.halve(name)
    out1 = both_sides(join_top(red1[0], red1[1]), side)
    out2 = both_sides(jnp.concatenate([red2[0].total(), red2[1].total()], axis=1), side)
    outo = both_sides(redo.total(), side)

    gp = None
    pairs = w // PAIR
    for first in range(0, pairs, 2):
        gp = attn_bwd(packed, att, gatt, feat, kf, first, 2, gp)
    ja, jb = joint_grad(core, dp, gp, n1)
    ja = Reducer(ja, 3 * w, w // 2, dp)
    jb = Reducer(jb, 3 * w, w // 2, dp)
    gh, vec1 = tail_part(gp, hid, gm, wj, r(g1), rb)
    db = jnp.concatenate(db1, axis=1).reshape(w, ff // w)
    vec = jnp.concatenate([vec1.T, vec2.T, db, jnp.zeros((w, PAIR - 8 - ff // w), f32)], axis=1)
    sa, sb = skip_grad(core, dp, gh, inputs, skips, vec)
    sa = Reducer(sa, w, w, dp)
    sb = Reducer(sb, w, w + PAIR, dp)
    igrad, sgrad = in_grad(gh, ws, rb)
    for a, b in ((ja, jb), (sa, sb)):
        for name in ["x", 1] + later:
            a.halve(name)
        for name in [1, "x"] + later:
            b.halve(name)
    outj = both_sides(jnp.concatenate([ja.total(), jb.total()], axis=1), side)
    outs = both_sides(jnp.concatenate([sa.total(), sb.total()], axis=1), side)

    ds, dj, do, d1, d2 = [m.T * scale for m in (outs[:, : 2 * w], outj, outo, out1, out2)]
    v = outs[:, 2 * w :] * scale
    col = lambda i: v[:, i]
    db1 = v[:, 8 : 8 + ff // w].reshape(-1)
    return (
        outcome, igrad, sgrad, ds, col(2), col(0), col(1), dj, do, col(4), col(5), col(6), d1, db1, d2, col(7),
    )


def solution(mesh):
    both = ("dp", "rep")
    in_specs = (P(both, None),) * 3 + (P(both),) * 3 + (P(),) * 14
    cols = P(None, "dp")
    vec = P("dp")
    out_specs = (P(both, None),) * 3 + (cols, vec, vec, vec, cols, cols, vec, vec, vec, cols, vec, cols, vec)
    return jax.shard_map(per_device, mesh=mesh, in_specs=in_specs, out_specs=out_specs, check_vma=False)
```

```python
import functools

import jax
import jax.numpy as jnp
from jax import lax
from jax.experimental import pallas as pl
from jax.experimental.pallas import tpu as pltpu
from jax.sharding import PartitionSpec as P

HEAD_DIM = 64
PAIR = 2 * HEAD_DIM
EPS = 1e-05
BIG = 1e30
f32 = jnp.float32
bf16 = jnp.bfloat16
NT = (((1,), (1,)), ((), ()))
NN = (((1,), (0,)), ((), ()))
TN = (((0,), (0,)), ((), ()))


def mm(a, b, dims=NN):
    return lax.dot_general(a, b, dims, preferred_element_type=f32)


def params(mb=56):
    return pltpu.CompilerParams(vmem_limit_bytes=mb << 20)


def cost(flops, nbytes, trans=0):
    return pl.CostEstimate(flops=int(flops), bytes_accessed=int(nbytes), transcendentals=int(trans))


def whole(shape):
    return pl.BlockSpec(shape, lambda *_: (0,) * len(shape), pipeline_mode=pl.Buffered(1))


def row_stats(x):
    mean = jnp.mean(x, axis=1, keepdims=True)
    cen = x - mean
    inv = lax.rsqrt(jnp.mean(cen * cen, axis=1, keepdims=True) + EPS)
    return cen * inv, inv


def norm_back(g, std, inv, gain):
    e = g * gain
    return inv * (e - jnp.mean(e, axis=1, keepdims=True) - std * jnp.mean(e * std, axis=1, keepdims=True))


def can_split(rows, m):
    return m % 8 == 0 and rows % (2 * m) == 0


def ring_order(dp):
    if dp != 16:
        return list(range(dp // 2))
    return [2 * z for z in range(4)] + [2 * z + 1 for z in reversed(range(4))]


def split_store(val, refs, core, m, order=None):
    rows, cols = val.shape
    parts = val.reshape(rows // (2 * m), 2, m, cols)
    low, high = parts[:, 0], parts[:, 1]
    keep = jnp.where(core == 0, low, high)
    send = jnp.where(core == 0, high, low)
    if order is None:
        refs[0][...] = keep
        refs[1][...] = send
    else:
        for place, owner in enumerate(order):
            refs[0][place] = keep[owner]
            refs[1][place] = send[owner]


def put(val, refs, core, m, order=None):
    if len(refs) == 2:
        split_store(val, refs, core, m, order)
    else:
        refs[0][...] = val


SMEM1 = pl.BlockSpec(memory_space=pltpu.SMEM)


def front_kernel(x_ref, s_ref, ws_ref, bs_ref, g_ref, b_ref, wj_ref, hid_ref, n1_ref, q_ref):
    w = x_ref.shape[1]
    hid = mm(x_ref[...], ws_ref[:w, :]) + mm(s_ref[...], ws_ref[w:, :]) + bs_ref[...].astype(f32)
    hid_ref[...] = hid
    std, _ = row_stats(hid)
    n1 = (std * g_ref[...].astype(f32) + b_ref[...].astype(f32)).astype(bf16)
    n1_ref[...] = n1
    q_ref[...] = mm(n1, wj_ref[...]).astype(bf16)


def front(x, s, ws, bs, g, b, wj, rb):
    n, w = x.shape
    c = wj.shape[1]
    row = lambda cols: pl.BlockSpec((rb, cols), lambda i: (i, 0))
    return pl.pallas_call(
        front_kernel,
        grid=(n // rb,),
        in_specs=[row(w), row(w), whole(ws.shape), whole((1, w)), whole((1, w)), whole((1, w)), whole(wj.shape)],
        out_specs=[row(w), row(w), row(c)],
        out_shape=[
            jax.ShapeDtypeStruct((n, w), f32),
            jax.ShapeDtypeStruct((n, w), bf16),
            jax.ShapeDtypeStruct((n, c), bf16),
        ],
        compiler_params=params(),
        cost_estimate=cost(2 * n * w * (2 * w + c), n * w * 20 + 5 * w * w * 2),
        name="front",
    )(x, s, ws, bs, g, b, wj)


def half_mask(h):
    lane = lax.broadcasted_iota(jnp.int32, (1, PAIR), 1)
    return (lane < HEAD_DIM) if h == 0 else (lane >= HEAD_DIM)


def eye_mask(t):
    return lax.broadcasted_iota(jnp.int32, (t, t), 0) == lax.broadcasted_iota(jnp.int32, (t, t), 1)


def pieces(x):
    a = x.astype(bf16)
    r = x - a.astype(f32)
    b = r.astype(bf16)
    c = (r - b.astype(f32)).astype(bf16)
    return a, b, c


def attn_fwd_kernel(q_ref, k_ref, v_ref, qf_ref, kf_ref, o_ref, feat_ref, ka_ref, vm_ref, s_ref, *, tq):
    n = q_ref.shape[0]
    ka_ref[:, :PAIR] = k_ref[...]
    ka_ref[:, PAIR:] = kf_ref[...]
    for h in range(2):
        vm_ref[h] = jnp.where(half_mask(h), v_ref[...], jnp.zeros_like(v_ref))
    eye = eye_mask(tq)
    lane = lax.broadcasted_iota(jnp.int32, (1, PAIR), 1)

    @pl.loop(0, n // tq)
    def _(i):
        start = pl.multiple_of(i * tq, tq)
        rows = pl.ds(start, tq)
        q = q_ref[rows, :] * jnp.asarray(HEAD_DIM**-0.5, bf16)
        qf = qf_ref[rows, :]
        kd = k_ref[rows, :]
        out = None
        for h in range(2):
            qm = jnp.where(half_mask(h), q, jnp.zeros_like(q))
            s_ref[h] = mm(jnp.concatenate([qm, qf], axis=1), ka_ref[...], NT)
            sd = mm(qm, kd, NT)
            s_ref[h, :, rows] = jnp.where(eye, sd, s_ref[h, :, rows])
        for h in range(2):
            s = s_ref[h]
            top = jnp.max(s, axis=1, keepdims=True)
            p = jnp.exp(s - top)
            total = jnp.sum(p, axis=1, keepdims=True)
            o = mm(p.astype(bf16), vm_ref[h]) / total
            out = o if out is None else out + o
            a, b, c = pieces(-(top + jnp.log(total)))
            feat = jnp.where(lane == 5, a, jnp.where(lane == 6, b, jnp.where(lane == 7, c, qf)))
            feat_ref[h, rows, :] = feat
        o_ref[rows, :] = out.astype(bf16)


def attn_fwd(packed, qf, kf, tq=128):
    n, c = packed.shape
    w = c // 3
    pairs = w // PAIR
    part = lambda p: pl.BlockSpec((n, PAIR), lambda j: (0, p * pairs + j))
    return pl.pallas_call(
        functools.partial(attn_fwd_kernel, tq=tq),
        grid=(pairs,),
        in_specs=[part(0), part(1), part(2), whole((n, PAIR)), whole((n, PAIR))],
        out_specs=[
            pl.BlockSpec((n, PAIR), lambda j: (0, j)),
            pl.BlockSpec((2, n, PAIR), lambda j: (j, 0, 0)),
        ],
        out_shape=[
            jax.ShapeDtypeStruct((n, w), bf16),
            jax.ShapeDtypeStruct((2 * pairs, n, PAIR), bf16),
        ],
        scratch_shapes=[
            pltpu.VMEM((n, 2 * PAIR), bf16),
            pltpu.VMEM((2, n, PAIR), bf16),
            pltpu.VMEM((2, tq, n), f32),
        ],
        compiler_params=params(),
        cost_estimate=cost(2 * n * n * (4 * PAIR) * pairs * 2, n * c * 4, n * n * 2 * pairs),
        name="attn_fwd",
    )(packed, packed, packed, qf, kf)


def attn_bwd_kernel(
    q_ref, k_ref, v_ref, o_ref, g_ref, feat_ref, kf_ref, *rest, tk
):
    out_ref, ka_ref, va_ref, qa_ref, ga_ref, dq_ref, st_ref = rest[-7:]
    n = q_ref.shape[0]
    lane = lax.broadcasted_iota(jnp.int32, (1, PAIR), 1)
    none = jnp.zeros((1, PAIR), bf16)
    scale = HEAD_DIM**-0.5
    ka_ref[:, :PAIR] = k_ref[...]
    ka_ref[:, PAIR:] = kf_ref[...]
    va_ref[:, :PAIR] = v_ref[...]
    va_ref[:, PAIR:] = jnp.broadcast_to(jnp.where(lane < 3, 1.0, 0.0).astype(bf16), (n, PAIR))
    q = q_ref[...] * jnp.asarray(scale, bf16)
    g = g_ref[...]
    prod = g.astype(f32) * o_ref[...].astype(f32)
    for h in range(2):
        own = half_mask(h)
        qa_ref[h, :, :PAIR] = jnp.where(own, q, none)
        qa_ref[h, :, PAIR:] = feat_ref[h]
        ga_ref[h, :, :PAIR] = jnp.where(own, g, none)
        delta = jnp.sum(jnp.where(own, prod, 0.0), axis=1, keepdims=True)
        a, b, c = pieces(-delta)
        ga_ref[h, :, PAIR:] = jnp.where(lane == 0, a, jnp.where(lane == 1, b, jnp.where(lane == 2, c, none)))
    dq_ref[...] = jnp.zeros_like(dq_ref)
    eye = eye_mask(tk)

    @pl.loop(0, n // tk)
    def _(i):
        start = pl.multiple_of(i * tk, tk)
        rows = pl.ds(start, tk)
        ka = ka_ref[rows, :]
        k = k_ref[rows, :]
        kplain = jnp.concatenate([k, jnp.where(lane < 5, none, kf_ref[rows, :])], axis=1)
        va = va_ref[rows, :]
        for h in range(2):
            st_ref[h] = mm(ka, qa_ref[h], NT)
            sd = mm(kplain, qa_ref[h, rows, :], NT)
            st_ref[h, :, rows] = jnp.where(eye, sd, st_ref[h, :, rows])
        dv = None
        dk = None
        dq = None
        for h in range(2):
            p = jnp.exp(st_ref[h])
            dp = mm(va, ga_ref[h], NT)
            ds = (p * dp).astype(bf16)
            km = jnp.where(half_mask(h), k, none)
            dv_h = mm(p.astype(bf16), ga_ref[h, :, :PAIR])
            dk_h = mm(ds, qa_ref[h, :, :PAIR])
            dq_h = mm(ds, km, TN)
            dv = dv_h if dv is None else dv + dv_h
            dk = dk_h if dk is None else dk + dk_h
            dq = dq_h if dq is None else dq + dq_h
        dq_ref[...] += dq
        out_ref[1, rows, :] = dk.astype(bf16)
        out_ref[2, rows, :] = dv.astype(bf16)

    out_ref[0] = (dq_ref[...] * scale).astype(bf16)


def attn_bwd(packed, att, grad, feat, kf, first, count, prev, tk=128):
    n, c = packed.shape
    w = c // 3
    pairs = w // PAIR
    part = lambda p: pl.BlockSpec((n, PAIR), lambda j: (0, p * pairs + first + j))
    extra = [] if prev is None else [prev]
    return pl.pallas_call(
        functools.partial(attn_bwd_kernel, tk=tk),
        grid=(count,),
        in_specs=[
            part(0),
            part(1),
            part(2),
            part(0),
            part(0),
            pl.BlockSpec((2, n, PAIR), lambda j: (first + j, 0, 0)),
            whole((n, PAIR)),
        ]
        + [pl.BlockSpec(memory_space=pl.ANY)] * len(extra),
        out_specs=pl.BlockSpec((3, n, PAIR), lambda j: (0, 0, first + j)),
        out_shape=jax.ShapeDtypeStruct((3, n, w), bf16),
        input_output_aliases={7: 0} if extra else {},
        scratch_shapes=[
            pltpu.VMEM((n, 2 * PAIR), bf16),
            pltpu.VMEM((n, 2 * PAIR), bf16),
            pltpu.VMEM((2, n, 2 * PAIR), bf16),
            pltpu.VMEM((2, n, 2 * PAIR), bf16),
            pltpu.VMEM((n, PAIR), f32),
            pltpu.VMEM((2, tk, n), f32),
        ],
        compiler_params=params(),
        cost_estimate=cost(2 * n * n * (9 * PAIR) * count * 2, n * PAIR * 16 * count, n * n * 2 * count),
        name="attn_bwd",
    )(packed, packed, packed, att, grad, feat, kf, *extra)


def mid_kernel(a_ref, hid_ref, cot_ref, tw_ref, wo_ref, bo_ref, g_ref, b_ref, mid_ref, n2_ref, gr_ref, grt_ref):
    mid = hid_ref[...] + mm(a_ref[...], wo_ref[...]) + bo_ref[...].astype(f32)
    mid_ref[...] = mid
    std, _ = row_stats(mid)
    n2_ref[...] = (std * g_ref[...].astype(f32) + b_ref[...].astype(f32)).astype(bf16)
    gr = (cot_ref[...].astype(f32) * tw_ref[...]).astype(bf16)
    gr_ref[...] = gr
    grt_ref[...] = gr.T


def mid_part(att, hid, cot, tw, wo, bo, g, b, rb):
    n, w = att.shape
    row = lambda cols: pl.BlockSpec((rb, cols), lambda i: (i, 0))
    return pl.pallas_call(
        mid_kernel,
        grid=(n // rb,),
        in_specs=[row(w), row(w), row(w), row(1), whole(wo.shape), whole((1, w)), whole((1, w)), whole((1, w))],
        out_specs=[row(w), row(w), row(w), pl.BlockSpec((w, rb), lambda i: (0, i))],
        out_shape=[
            jax.ShapeDtypeStruct((n, w), f32),
            jax.ShapeDtypeStruct((n, w), bf16),
            jax.ShapeDtypeStruct((n, w), bf16),
            jax.ShapeDtypeStruct((w, n), bf16),
        ],
        compiler_params=params(),
        cost_estimate=cost(2 * n * w * w, n * w * 20),
        name="mid_part",
    )(att, hid, cot, tw, wo, bo, g, b)


def normal_cdf_pdf(u):
    a = jnp.abs(u)
    t = 1.0 / (1.0 + a * (0.3275911 * 0.7071067811865476))
    e = jnp.exp(-0.5 * u * u)
    half = 0.5
    poly = t * (
        half * 0.254829592
        + t * (half * -0.284496736 + t * (half * 1.421413741 + t * (half * -1.453152027 + t * (half * 1.061405429))))
    )
    tail = poly * e
    return jnp.where(u < 0, tail, 1.0 - tail), e * 0.3989422804014327


def ff_fwd_kernel(core_ref, n2_ref, grt_ref, w1_ref, b1_ref, w2_ref, acc_ref, slope_ref, *refs, m, order):
    w2 = w2_ref[...]
    pre = mm(n2_ref[...], w1_ref[...]) + b1_ref[...].astype(f32)
    cdf, pdf = normal_cdf_pdf(pre)
    act = (pre * cdf).astype(bf16)
    slope_ref[...] = (cdf + pre * pdf).astype(bf16)

    @pl.when(pl.program_id(0) == 0)
    def _():
        acc_ref[...] = jnp.zeros_like(acc_ref)

    acc_ref[...] += mm(act, w2)
    put(mm(grt_ref[...], act), refs, core_ref[0], m, order)


def ff_fwd(core, dp, n2, grt, w1, b1, w2, fc=384):
    n, w = n2.shape
    ff = w1.shape[1]
    m = w // dp
    if can_split(w, m):
        specs = [pl.BlockSpec((dp // 2, m, fc), lambda i: (0, 0, i))] * 2
        shapes = [jax.ShapeDtypeStruct((dp // 2, m, ff), f32)] * 2
    else:
        specs = [pl.BlockSpec((w, fc), lambda i: (0, i))]
        shapes = [jax.ShapeDtypeStruct((w, ff), f32)]
    res = pl.pallas_call(
        functools.partial(ff_fwd_kernel, m=m, order=ring_order(dp)),
        grid=(ff // fc,),
        in_specs=[
            SMEM1,
            whole((n, w)),
            whole((w, n)),
            pl.BlockSpec((w, fc), lambda i: (0, i)),
            pl.BlockSpec((1, fc), lambda i: (0, i)),
            pl.BlockSpec((fc, w), lambda i: (i, 0)),
        ],
        out_specs=[whole((n, w)), pl.BlockSpec((n, fc), lambda i: (0, i))] + specs,
        out_shape=[jax.ShapeDtypeStruct((n, w), f32), jax.ShapeDtypeStruct((n, ff), bf16)] + shapes,
        compiler_params=params(),
        cost_estimate=cost(6 * n * w * ff, n * w * 10 + ff * w * 8 + n * ff * 2, n * ff * 2),
        name="ff_fwd",
    )(core, n2, grt, w1, b1, w2)
    return res[0], res[1], res[2:]


def ff_bwd_kernel(core_ref, n2_ref, gr_ref, w1_ref, slope_ref, w2_ref, *rest, first, count, m):
    outs = rest if first else rest[1 + count :]
    gn_ref, db1_ref = outs[:2]
    gpre = (mm(gr_ref[...], w2_ref[...], NT) * slope_ref[...].astype(f32)).astype(bf16)

    @pl.when(pl.program_id(0) == 0)
    def _():
        gn_ref[...] = jnp.zeros_like(gn_ref) if first else rest[0][...]

    gn_ref[...] += mm(gpre, w1_ref[...], NT)
    put(mm(gpre, n2_ref[...], TN), outs[2:], core_ref[0], m)
    db1_ref[...] = jnp.sum(gpre.astype(f32), axis=0, keepdims=True)


def ff_bwd(core, dp, n2, gr, w1, slope, w2, part, parts, prev, fc=384):
    n, w = n2.shape
    ff = w1.shape[1]
    mine = ff // parts
    steps = mine // fc
    base = part * steps
    m, mo = ff // dp, w // dp
    split = can_split(fc, m) and can_split(w, mo) and fc == 2 * m and dp == 16
    if split:
        def place(i):
            z, y = (base + i) // 2, (base + i) % 2
            return ((1 - y) * z + y * (7 - z), 0, 0)

        specs = [pl.BlockSpec((1, m, w), place)] * 2
        shapes = [jax.ShapeDtypeStruct((dp // 2, m + mo, w), f32)] * 2
    else:
        specs = [pl.BlockSpec((fc, w), lambda i: (base + i, 0))]
        shapes = [jax.ShapeDtypeStruct((ff, w), f32)]
    extra = [] if prev is None else list(prev)
    res = pl.pallas_call(
        functools.partial(ff_bwd_kernel, first=prev is None, count=len(specs), m=m),
        grid=(steps,),
        in_specs=[
            SMEM1,
            whole((n, w)),
            whole((n, w)),
            pl.BlockSpec((w, fc), lambda i: (0, base + i)),
            pl.BlockSpec((n, fc), lambda i: (0, base + i)),
            pl.BlockSpec((fc, w), lambda i: (base + i, 0)),
        ]
        + ([whole((n, w))] + [pl.BlockSpec(memory_space=pl.ANY)] * len(specs) if extra else []),
        out_specs=[whole((n, w)), pl.BlockSpec((1, fc), lambda i: (0, i))] + specs,
        out_shape=[jax.ShapeDtypeStruct((n, w), f32), jax.ShapeDtypeStruct((1, mine), f32)] + shapes,
        input_output_aliases={7 + k: 2 + k for k in range(len(specs))} if extra else {},
        compiler_params=params(),
        cost_estimate=cost(6 * n * w * mine, n * w * 10 + mine * w * 8 + n * mine * 2),
        name="ff_bwd",
    )(core, n2, gr, w1, slope, w2, *extra)
    return (res[0], *res[2:]), res[1]


def back_kernel(
    core_ref, mid_ref, acc_ref, gn_ref, cot_ref, tw_ref, gr_ref, a_ref, wo_ref, g_ref, b2_ref, *rest, m, count, order
):
    out_ref, gm_ref, ga_ref, vec_ref = rest[-5 - count : -1 - count]
    dwo_refs, dwo_ref = rest[-1 - count : -1], rest[-1]
    mid = mid_ref[...]
    out_ref[...] = (mid + acc_ref[...] + b2_ref[...].astype(f32)).astype(bf16)
    std, inv = row_stats(mid)
    gn = gn_ref[...]
    gm = cot_ref[...].astype(f32) * tw_ref[...] + norm_back(gn, std, inv, g_ref[...].astype(f32))
    gm_ref[...] = gm
    gb = gm.astype(bf16)
    ga_ref[...] = mm(gb, wo_ref[...], NT).astype(bf16)
    dwo = mm(gb, a_ref[...], TN)
    add = lambda x: jnp.sum(x, axis=0, keepdims=True)
    vec = jnp.concatenate([add(gb.astype(f32)), add(gn * std), add(gn), add(gr_ref[...].astype(f32))], axis=0)
    step = pl.program_id(0)

    @pl.when(step == 0)
    def _():
        dwo_ref[...] = dwo
        vec_ref[...] = vec

    @pl.when(step > 0)
    def _():
        dwo_ref[...] += dwo
        vec_ref[...] += vec

    @pl.when(step == pl.num_programs(0) - 1)
    def _():
        put(dwo_ref[...], dwo_refs, core_ref[0], m, order)


def grad_outs(rows, cols, m):
    if can_split(rows, m):
        shape = (rows // (2 * m), m, cols)
        return [whole(shape)] * 2, [jax.ShapeDtypeStruct(shape, f32)] * 2
    return [whole((rows, cols))], [jax.ShapeDtypeStruct((rows, cols), f32)]


def back_part(core, dp, mid, acc, gn, cot, tw, gr, att, wo, g, b2, rb, into):
    n, w = mid.shape
    row = lambda cols: pl.BlockSpec((rb, cols), lambda i: (i, 0))
    mo = w // dp
    if len(into) == 2:
        at = into[0].shape[1] // mo - 1
        specs = [pl.BlockSpec((dp // 2, mo, w), lambda i: (0, at, 0))] * 2
        shapes = [jax.ShapeDtypeStruct(into[0].shape, f32)] * 2
    else:
        into = []
        specs, shapes = [whole((w, w))], [jax.ShapeDtypeStruct((w, w), f32)]
    res = pl.pallas_call(
        functools.partial(back_kernel, m=mo, count=len(specs), order=ring_order(dp)),
        grid=(n // rb,),
        in_specs=[SMEM1, row(w), row(w), row(w), row(w), row(1), row(w), row(w), whole(wo.shape), whole((1, w)), whole((1, w))]
        + [pl.BlockSpec(memory_space=pl.ANY)] * len(into),
        out_specs=[row(w), row(w), row(w), whole((4, w))] + specs,
        out_shape=[
            jax.ShapeDtypeStruct((n, w), bf16),
            jax.ShapeDtypeStruct((n, w), f32),
            jax.ShapeDtypeStruct((n, w), bf16),
            jax.ShapeDtypeStruct((4, w), f32),
        ]
        + shapes,
        input_output_aliases={11 + k: 4 + k for k in range(len(into))},
        scratch_shapes=[pltpu.VMEM((w, w), f32)],
        compiler_params=params(),
        cost_estimate=cost(4 * n * w * w, n * w * 28),
        name="back_part",
    )(core, mid, acc, gn, cot, tw, gr, att, wo, g, b2, *into)
    return res[0], res[1], res[2], res[3], res[4:]


def joint_grad_kernel(core_ref, gp_ref, n1_ref, *rest, m):
    refs, gpt_ref = rest[:-1], rest[-1]
    parts, n, w = gp_ref.shape
    half = len(refs) // 2
    step = pl.program_id(0)

    @pl.when(step == 0)
    def _():
        for p in range(parts):
            gpt_ref[p * w : (p + 1) * w, :] = gp_ref[p].T

    for side in range(2):

        @pl.when(step == side)
        def _():
            put(mm(gpt_ref[...], n1_ref[...]), refs[side * half : (side + 1) * half], core_ref[0], m)


def joint_grad(core, dp, gp, n1):
    parts, n, w = gp.shape
    cb = w // 2
    specs, shapes = grad_outs(parts * w, cb, parts * w // dp)
    res = pl.pallas_call(
        functools.partial(joint_grad_kernel, m=parts * w // dp),
        grid=(2,),
        in_specs=[SMEM1, whole((parts, n, w)), pl.BlockSpec((n, cb), lambda j: (0, j))],
        out_specs=specs * 2,
        out_shape=shapes * 2,
        scratch_shapes=[pltpu.VMEM((parts * w, n), bf16)],
        compiler_params=params(),
        cost_estimate=cost(2 * parts * n * w * w, n * w * 8 + parts * w * w * 4),
        name="joint_grad",
    )(core, gp, n1)
    k = len(specs)
    return res[:k], res[k:]


def tail_kernel(gp_ref, hid_ref, gm_ref, wj_ref, g_ref, gh_ref, vec_ref):
    w = hid_ref.shape[1]
    gn = mm(gp_ref[0], wj_ref[:, :w], NT) + mm(gp_ref[1], wj_ref[:, w : 2 * w], NT) + mm(gp_ref[2], wj_ref[:, 2 * w :], NT)
    std, inv = row_stats(hid_ref[...])
    gh = (gm_ref[...] + norm_back(gn, std, inv, g_ref[...].astype(f32))).astype(bf16)
    gh_ref[...] = gh
    add = lambda x: jnp.sum(x, axis=0, keepdims=True)
    vec = jnp.concatenate([add(gn * std), add(gn), add(gh.astype(f32)), jnp.zeros((1, w), f32)], axis=0)
    step = pl.program_id(0)

    @pl.when(step == 0)
    def _():
        vec_ref[...] = vec

    @pl.when(step > 0)
    def _():
        vec_ref[...] += vec


def tail_part(gp, hid, gm, wj, g, rb):
    n, w = hid.shape
    row = lambda cols: pl.BlockSpec((rb, cols), lambda i: (i, 0))
    return pl.pallas_call(
        tail_kernel,
        grid=(n // rb,),
        in_specs=[pl.BlockSpec((3, rb, w), lambda i: (0, i, 0)), row(w), row(w), whole(wj.shape), whole((1, w))],
        out_specs=[row(w), whole((4, w))],
        out_shape=[jax.ShapeDtypeStruct((n, w), bf16), jax.ShapeDtypeStruct((4, w), f32)],
        compiler_params=params(),
        cost_estimate=cost(6 * n * w * w, n * w * 16),
        name="tail_part",
    )(gp, hid, gm, wj, g)


def skip_grad_kernel(core_ref, gh_ref, x_ref, s_ref, vec_ref, *refs, m):
    half = len(refs) // 2
    ght = gh_ref[...].T
    put(mm(ght, x_ref[...]), refs[:half], core_ref[0], m)
    side = jnp.concatenate([mm(ght, s_ref[...]), vec_ref[...]], axis=1)
    put(side, refs[half:], core_ref[0], m)


def skip_grad(core, dp, gh, x, s, vec):
    n, w = gh.shape
    m = w // dp
    spec_a, shape_a = grad_outs(w, w, m)
    spec_b, shape_b = grad_outs(w, w + vec.shape[1], m)
    res = pl.pallas_call(
        functools.partial(skip_grad_kernel, m=m),
        grid=(1,),
        in_specs=[SMEM1, whole((n, w)), whole((n, w)), whole((n, w)), whole(vec.shape)],
        out_specs=spec_a + spec_b,
        out_shape=shape_a + shape_b,
        compiler_params=params(),
        cost_estimate=cost(4 * n * w * w, n * w * 6 + w * w * 8),
        name="skip_grad",
    )(core, gh, x, s, vec)
    k = len(spec_a)
    return res[:k], res[k:]


def in_grad_kernel(gh_ref, ws_ref, a_ref, b_ref):
    w = a_ref.shape[1]
    gh = gh_ref[...]
    a_ref[...] = mm(gh, ws_ref[:w, :], NT).astype(bf16)
    b_ref[...] = mm(gh, ws_ref[w:, :], NT).astype(bf16)


def in_grad(gh, ws, rb):
    n, w = gh.shape
    row = lambda cols: pl.BlockSpec((rb, cols), lambda i: (i, 0))
    return pl.pallas_call(
        in_grad_kernel,
        grid=(n // rb,),
        in_specs=[row(w), whole(ws.shape)],
        out_specs=[row(w), row(w)],
        out_shape=[jax.ShapeDtypeStruct((n, w), bf16)] * 2,
        compiler_params=params(),
        cost_estimate=cost(4 * n * w * w, n * w * 10),
        name="in_grad",
    )(gh, ws)


def layout(lengths, keep, group_ids, group_counts, n, tokens_total):
    groups = group_counts.shape[0]
    slots = lengths.shape[0]
    ends = jnp.cumsum(lengths)
    pos = jnp.arange(n, dtype=jnp.int32)
    segment = jnp.sum((pos[:, None] >= ends[None, :]).astype(jnp.int32), axis=1)
    chosen = group_ids[:, None] == jnp.arange(groups, dtype=jnp.int32)[None, :]
    slot_count = jnp.sum(jnp.where(chosen, group_counts[None, :], 0), axis=1).astype(f32)
    slot_weight = tokens_total // groups / slot_count
    lane = jnp.arange(PAIR, dtype=jnp.int32)[None, :]
    same = segment[:, None] == lane
    weight_row = jnp.zeros((PAIR,), f32).at[:slots].set(slot_weight)[None, :]
    tw = jnp.sum(jnp.where(same, weight_row, 0.0), axis=1, keepdims=True)
    qf = same.astype(bf16)
    kf = jnp.where(lane <= slots, jnp.where(same & (keep[:, None] == 1), 0.0, -BIG), jnp.where(lane < slots + 4, 1.0, 0.0))
    return tw, qf, kf.astype(bf16)


def pick(x, axis, index):
    return lax.dynamic_index_in_dim(x, index, axis, keepdims=False)


class Reducer:
    def __init__(self, refs, rows, cols, dp):
        self.dp = dp
        self.bits = dp.bit_length() - 1
        self.place = lax.axis_index("dp")
        self.side = lax.axis_index("rep")
        m = rows // dp
        if len(refs) == 1:
            full = refs[0].reshape(dp // 2, 2, m, cols)
            core = self.place & 1
            refs = [pick(full, 1, core), pick(full, 1, 1 - core)]
        keep, send = refs
        self.names = list(range(self.bits - 1, 0, -1)) + ["x"]
        got = self.swap(send, 0)
        shape = (2,) * (len(self.names)) + (m // 2, cols)
        self.terms = [keep.reshape(shape), got.reshape(shape)]

    def swap(self, x, name):
        if name == "x":
            return lax.ppermute(x, "rep", [(0, 1), (1, 0)])
        return lax.ppermute(x, "dp", [(i, i ^ (1 << name)) for i in range(self.dp)])

    def bit(self, name):
        return self.side if name == "x" else (self.place >> name) & 1

    def halve(self, name):
        axis = self.names.index(name)
        mine = self.bit(name)
        send = sum(pick(t, axis, 1 - mine) for t in self.terms)
        got = self.swap(send, name)
        self.terms = [pick(t, axis, mine) for t in self.terms] + [got]
        self.names.pop(axis)

    def total(self):
        return sum(self.terms)


def pair_sum(refs, cols, dp):
    if len(refs) == 1:
        full = refs[0].reshape(dp // 2, 2, -1, cols)
        core = lax.axis_index("dp") & 1
        refs = [pick(full, 1, core), pick(full, 1, 1 - core)]
    keep, send = refs
    return keep + lax.ppermute(send, "dp", [(i, i ^ 1) for i in range(dp)])


def both_sides(x, side):
    other = lax.ppermute(x, "rep", [(0, 1), (1, 0)])
    return jnp.concatenate([jnp.where(side == 0, x, other), jnp.where(side == 0, other, x)], axis=0)


def per_device(*args):
    (inputs, skips, cot, lengths, keep, group_ids, group_counts, ws, bs, g1, s1, wj, wo, bo, g2, s2, w1, b1, w2, b2) = args
    n, w = inputs.shape
    ff = w1.shape[1]
    dp = lax.axis_size("dp")
    tokens_total = n * dp * lax.axis_size("rep")
    scale = float(tokens_total) ** -0.5
    place = lax.axis_index("dp")
    side = lax.axis_index("rep")
    core = (place & 1).astype(jnp.int32).reshape(1)
    rb = n // 3
    r = lambda v: v.reshape(1, -1)
    bits = dp.bit_length() - 1
    later = list(range(2, bits))

    tw, qf, kf = layout(lengths, keep, group_ids, group_counts, n, tokens_total)
    hid, n1, packed = front(inputs, skips, ws, r(bs), r(g1), r(s1), wj, rb)
    att, feat = attn_fwd(packed, qf, kf)
    mid, n2, gr, grt = mid_part(att, hid, cot, tw, wo, r(bo), r(g2), r(s2), rb)

    acc, slope, d2 = ff_fwd(core, dp, n2, grt, w1, r(b1), w2)
    half2 = pair_sum(d2, ff, dp)
    carry, db0 = ff_bwd(core, dp, n2, gr, w1, slope, w2, 0, 2, None)
    carry, half2 = lax.optimization_barrier((carry, half2))
    carry, db1 = ff_bwd(core, dp, n2, gr, w1, slope, w2, 1, 2, carry)
    gn2, d1 = carry[0], carry[1:]
    outcome, gm, gatt, vec2, do = back_part(core, dp, mid, acc, gn2, cot, tw, gr, att, wo, r(g2), r(b2), rb, d1)
    if len(do) == 2:
        half1 = pair_sum(do, w, dp)
    else:
        full = jnp.concatenate([d1[0].reshape(dp, ff // dp, w), do[0].reshape(dp, w // dp, w)], axis=1)
        half1 = pair_sum([full.reshape(-1, w)], w, dp)
    ring = ring_order(dp)
    groups = [[2 * i + c for i in ring] for c in range(2)]
    ring_sum = lambda h: lax.psum_scatter(h, "dp", scatter_dimension=0, tiled=True, axis_index_groups=groups)[0]
    over_rep = lambda h: h + lax.ppermute(h, "rep", [(0, 1), (1, 0)])
    out2 = over_rep(ring_sum(half2))

    gp = None
    pairs = w // PAIR
    for first in range(0, pairs, 2):
        gp = attn_bwd(packed, att, gatt, feat, kf, first, 2, gp)
        if first == 0:
            gp, half1 = lax.optimization_barrier((gp, half1))
    out1 = over_rep(ring_sum(half1))
    out1, outo = out1[: ff // dp], out1[ff // dp :]
    ja, jb = joint_grad(core, dp, gp, n1)
    ja = Reducer(ja, 3 * w, w // 2, dp)
    jb = Reducer(jb, 3 * w, w // 2, dp)
    gh, vec1 = tail_part(gp, hid, gm, wj, r(g1), rb)
    db = jnp.concatenate([db0, db1], axis=1).reshape(w, ff // w)
    vec = jnp.concatenate([vec1.T, vec2.T, db, jnp.zeros((w, PAIR - 8 - ff // w), f32)], axis=1)
    sa, sb = skip_grad(core, dp, gh, inputs, skips, vec)
    sa = Reducer(sa, w, w, dp)
    sb = Reducer(sb, w, w + PAIR, dp)
    igrad, sgrad = in_grad(gh, ws, rb)
    for a, b in ((ja, jb), (sa, sb)):
        for name in ["x", 1] + later:
            a.halve(name)
        for name in [1, "x"] + later:
            b.halve(name)
    outj = both_sides(jnp.concatenate([ja.total(), jb.total()], axis=1), side)
    outs = both_sides(jnp.concatenate([sa.total(), sb.total()], axis=1), side)

    ds, dj, do, d1, d2 = [m.T * scale for m in (outs[:, : 2 * w], outj, outo, out1, out2)]
    v = outs[:, 2 * w :] * scale
    col = lambda i: v[:, i]
    db1 = v[:, 8 : 8 + ff // w].reshape(-1)
    return (
        outcome, igrad, sgrad, ds, col(2), col(0), col(1), dj, do, col(4), col(5), col(6), d1, db1, d2, col(7),
    )


def solution(mesh):
    both = ("dp", "rep")
    in_specs = (P(both, None),) * 3 + (P(both),) * 3 + (P(),) * 14
    cols = P(None, "dp")
    vec = P("dp")
    out_specs = (P(both, None),) * 3 + (cols, vec, vec, vec, cols, cols, vec, vec, vec, cols, vec, cols, vec)
    return jax.shard_map(per_device, mesh=mesh, in_specs=in_specs, out_specs=out_specs, check_vma=False)
```

```python
import functools

import jax
import jax.numpy as jnp
from jax import lax
from jax.experimental import pallas as pl
from jax.experimental.pallas import tpu as pltpu
from jax.sharding import PartitionSpec as P

HEAD_DIM = 64
PAIR = 2 * HEAD_DIM
EPS = 1e-05
BIG = 1e30
f32 = jnp.float32
bf16 = jnp.bfloat16
NT = (((1,), (1,)), ((), ()))
NN = (((1,), (0,)), ((), ()))
TN = (((0,), (0,)), ((), ()))


def mm(a, b, dims=NN):
    return lax.dot_general(a, b, dims, preferred_element_type=f32)


def params(mb=56):
    return pltpu.CompilerParams(vmem_limit_bytes=mb << 20)


def cost(flops, nbytes, trans=0):
    return pl.CostEstimate(flops=int(flops), bytes_accessed=int(nbytes), transcendentals=int(trans))


def whole(shape):
    return pl.BlockSpec(shape, lambda *_: (0,) * len(shape), pipeline_mode=pl.Buffered(1))


def row_stats(x):
    mean = jnp.mean(x, axis=1, keepdims=True)
    cen = x - mean
    inv = lax.rsqrt(jnp.mean(cen * cen, axis=1, keepdims=True) + EPS)
    return cen * inv, inv


def norm_back(g, std, inv, gain):
    e = g * gain
    return inv * (e - jnp.mean(e, axis=1, keepdims=True) - std * jnp.mean(e * std, axis=1, keepdims=True))


def can_split(rows, m):
    return m % 8 == 0 and rows % (2 * m) == 0


def ring_order(dp):
    if dp != 16:
        return list(range(dp // 2))
    return [2 * z for z in range(4)] + [2 * z + 1 for z in reversed(range(4))]


def split_store(val, refs, core, m, order=None):
    rows, cols = val.shape
    parts = val.reshape(rows // (2 * m), 2, m, cols)
    low, high = parts[:, 0], parts[:, 1]
    keep = jnp.where(core == 0, low, high)
    send = jnp.where(core == 0, high, low)
    if order is None:
        refs[0][...] = keep
        refs[1][...] = send
    else:
        for place, owner in enumerate(order):
            refs[0][place] = keep[owner]
            refs[1][place] = send[owner]


def put(val, refs, core, m, order=None):
    if len(refs) == 2:
        split_store(val, refs, core, m, order)
    else:
        refs[0][...] = val


SMEM1 = pl.BlockSpec(memory_space=pltpu.SMEM)


def eye_mask(t):
    return lax.broadcasted_iota(jnp.int32, (t, t), 0) == lax.broadcasted_iota(jnp.int32, (t, t), 1)


def line(ref):
    return ref[...].astype(f32).reshape(1, -1)


def front_kernel(
    len_ref, gid_ref, cnt_ref, keep_ref, x_ref, s_ref, ws_ref, bs_ref, g_ref, b_ref, wj_ref,
    hid_ref, n1_ref, q_ref, qf_ref, kf_ref, tw_ref, *, group_tokens,
):
    rb, w = x_ref.shape
    hid = mm(x_ref[...], ws_ref[:w, :]) + mm(s_ref[...], ws_ref[w:, :]) + line(bs_ref)
    hid_ref[...] = hid
    std, _ = row_stats(hid)
    n1 = (std * line(g_ref) + line(b_ref)).astype(bf16)
    n1_ref[...] = n1
    q_ref[...] = mm(n1, wj_ref[...]).astype(bf16)

    slots = len_ref.shape[0]
    base = pl.program_id(0) * rb
    lane = lax.broadcasted_iota(jnp.int32, (1, PAIR), 1)
    pos = lax.broadcasted_iota(jnp.int32, (rb, 1), 0) + base
    segment = jnp.zeros((rb, 1), jnp.int32)
    count = jnp.ones((1, PAIR), f32)
    end = 0
    for i in range(slots):
        end = end + len_ref[i]
        segment = segment + (pos >= end).astype(jnp.int32)
        count = jnp.where(lane == i, cnt_ref[gid_ref[i]].astype(f32), count)
    same = segment == lane
    weight = jnp.where(lane < slots, group_tokens / count, 0.0)
    tw_ref[...] = jnp.sum(jnp.where(same, weight, 0.0), axis=1, keepdims=True)
    qf_ref[...] = jnp.where(same, 1.0, 0.0).astype(bf16)
    eye = eye_mask(PAIR)
    for t in range(rb // PAIR):
        rows = slice(t * PAIR, (t + 1) * PAIR)
        keep = keep_ref[pl.ds(pl.multiple_of(base + t * PAIR, PAIR), PAIR)].astype(f32).reshape(1, PAIR)
        kept = jnp.sum(jnp.where(eye, keep, 0.0), axis=1, keepdims=True) == 1.0
        bias = jnp.where(same[rows] & kept, 0.0, -BIG)
        kf_ref[rows, :] = jnp.where(lane <= slots, bias, jnp.where(lane < slots + 4, 1.0, 0.0)).astype(bf16)


def front(lengths, gids, counts, keep, x, s, ws, bs, g, b, wj, rb, group_tokens):
    n, w = x.shape
    c = wj.shape[1]
    row = lambda cols: pl.BlockSpec((rb, cols), lambda i: (i, 0))
    return pl.pallas_call(
        functools.partial(front_kernel, group_tokens=float(group_tokens)),
        grid=(n // rb,),
        in_specs=[SMEM1, SMEM1, SMEM1, whole((n,)), row(w), row(w), whole(ws.shape), whole((w,)), whole((w,)), whole((w,)), whole(wj.shape)],
        out_specs=[row(w), row(w), row(c), row(PAIR), row(PAIR), row(1)],
        out_shape=[
            jax.ShapeDtypeStruct((n, w), f32),
            jax.ShapeDtypeStruct((n, w), bf16),
            jax.ShapeDtypeStruct((n, c), bf16),
            jax.ShapeDtypeStruct((n, PAIR), bf16),
            jax.ShapeDtypeStruct((n, PAIR), bf16),
            jax.ShapeDtypeStruct((n, 1), f32),
        ],
        compiler_params=params(),
        cost_estimate=cost(2 * n * w * (2 * w + c), n * w * 20 + 5 * w * w * 2),
        name="front",
    )(lengths, gids, counts, keep, x, s, ws, bs, g, b, wj)


def half_mask(h):
    lane = lax.broadcasted_iota(jnp.int32, (1, PAIR), 1)
    return (lane < HEAD_DIM) if h == 0 else (lane >= HEAD_DIM)


def pieces(x):
    a = x.astype(bf16)
    r = x - a.astype(f32)
    b = r.astype(bf16)
    c = (r - b.astype(f32)).astype(bf16)
    return a, b, c


def attn_fwd_kernel(q_ref, k_ref, v_ref, qf_ref, kf_ref, o_ref, feat_ref, ka_ref, vm_ref, s_ref, *, tq):
    n = q_ref.shape[0]
    none = jnp.zeros((1, PAIR), bf16)
    one = jnp.ones((1, PAIR), bf16)
    lane = lax.broadcasted_iota(jnp.int32, (1, PAIR), 1)
    ka_ref[:, :PAIR] = k_ref[...]
    ka_ref[:, PAIR:] = kf_ref[...]
    spare = [HEAD_DIM, 0]
    for h in range(2):
        vm_ref[h] = jnp.where(half_mask(h), v_ref[...], jnp.where(lane == spare[h], one, none))
    eye = eye_mask(PAIR)
    units = [(i, h) for i in range(n // tq) for h in range(2)]

    def scores(u):
        i, h = units[u]
        rows = slice(i * tq, (i + 1) * tq)
        qm = jnp.where(half_mask(h), q_ref[rows, :] * jnp.asarray(HEAD_DIM**-0.5, bf16), none)
        slot = u % 2
        s_ref[slot] = mm(jnp.concatenate([qm, qf_ref[rows, :]], axis=1), ka_ref[...], NT)
        for j in range(tq // PAIR):
            a = slice(j * PAIR, (j + 1) * PAIR)
            c = slice(i * tq + j * PAIR, i * tq + (j + 1) * PAIR)
            s_ref[slot, a, c] = jnp.where(eye, mm(qm[a], k_ref[c, :], NT), s_ref[slot, a, c])

    scores(0)
    outs = [None, None]
    for u, (i, h) in enumerate(units):
        if u + 1 < len(units):
            scores(u + 1)
        rows = slice(i * tq, (i + 1) * tq)
        s = s_ref[u % 2]
        top = jnp.max(s, axis=1, keepdims=True)
        pv = mm(jnp.exp(s - top).astype(bf16), vm_ref[h])
        total = pv[:, spare[h] : spare[h] + 1]
        outs[h] = pv / total
        a, b, c = pieces(-(top + jnp.log(total)))
        feat_ref[h, rows, :] = jnp.where(lane == 5, a, jnp.where(lane == 6, b, jnp.where(lane == 7, c, qf_ref[rows, :])))
        if h == 1:
            o_ref[rows, :] = jnp.where(lane < HEAD_DIM, outs[0], outs[1]).astype(bf16)


def attn_fwd(packed, qf, kf, tq=384):
    n, c = packed.shape
    w = c // 3
    pairs = w // PAIR
    part = lambda p: pl.BlockSpec((n, PAIR), lambda j: (0, p * pairs + j))
    return pl.pallas_call(
        functools.partial(attn_fwd_kernel, tq=tq),
        grid=(pairs,),
        in_specs=[part(0), part(1), part(2), whole((n, PAIR)), whole((n, PAIR))],
        out_specs=[
            pl.BlockSpec((n, PAIR), lambda j: (0, j)),
            pl.BlockSpec((2, n, PAIR), lambda j: (j, 0, 0)),
        ],
        out_shape=[
            jax.ShapeDtypeStruct((n, w), bf16),
            jax.ShapeDtypeStruct((2 * pairs, n, PAIR), bf16),
        ],
        scratch_shapes=[
            pltpu.VMEM((n, 2 * PAIR), bf16),
            pltpu.VMEM((2, n, PAIR), bf16),
            pltpu.VMEM((2, tq, n), f32),
        ],
        compiler_params=params(),
        cost_estimate=cost(2 * n * n * (4 * PAIR) * pairs * 2, n * c * 4, n * n * 2 * pairs),
        name="attn_fwd",
    )(packed, packed, packed, qf, kf)


def attn_bwd_kernel(q_ref, k_ref, v_ref, o_ref, g_ref, feat_ref, kf_ref, *rest, tk):
    out_ref, ka_ref, va_ref, qa_ref, ga_ref, kt_ref, dq_ref, st_ref, dp_ref = rest[-9:]
    n = q_ref.shape[0]
    lane = lax.broadcasted_iota(jnp.int32, (1, PAIR), 1)
    none = jnp.zeros((1, PAIR), bf16)
    scale = HEAD_DIM**-0.5
    ka_ref[:, :PAIR] = k_ref[...]
    ka_ref[:, PAIR:] = kf_ref[...]
    va_ref[:, :PAIR] = v_ref[...]
    va_ref[:, PAIR:] = jnp.broadcast_to(jnp.where(lane < 3, 1.0, 0.0).astype(bf16), (n, PAIR))
    kt_ref[...] = k_ref[...].T
    q = q_ref[...] * jnp.asarray(scale, bf16)
    g = g_ref[...]
    prod = g.astype(f32) * o_ref[...].astype(f32)
    for h in range(2):
        own = half_mask(h)
        delta = jnp.sum(jnp.where(own, prod, 0.0), axis=1, keepdims=True)
        a, b, c = pieces(-delta)
        qa_ref[h, :, :PAIR] = jnp.where(own, q, none)
        qa_ref[h, :, PAIR:] = feat_ref[h]
        ga_ref[h, :, :PAIR] = jnp.where(own, g, none)
        ga_ref[h, :, PAIR:] = jnp.where(lane == 0, a, jnp.where(lane == 1, b, jnp.where(lane == 2, c, none)))
    eye = eye_mask(PAIR)
    units = [(i, h) for i in range(n // tk) for h in range(2)]

    def scores(u):
        i, h = units[u]
        rows = slice(i * tk, (i + 1) * tk)
        slot = u % 2
        st_ref[slot] = mm(ka_ref[rows, :], qa_ref[h], NT)
        for j in range(tk // PAIR):
            a = slice(j * PAIR, (j + 1) * PAIR)
            c = slice(i * tk + j * PAIR, i * tk + (j + 1) * PAIR)
            plain = jnp.concatenate([k_ref[c, :], jnp.where(lane < 5, none, kf_ref[c, :])], axis=1)
            st_ref[slot, a, c] = jnp.where(eye, mm(plain, qa_ref[h, c, :], NT), st_ref[slot, a, c])
        dp_ref[slot] = mm(va_ref[rows, :], ga_ref[h], NT)

    scores(0)
    dv = [None, None]
    dk = [None, None]
    for u, (i, h) in enumerate(units):
        if u + 1 < len(units):
            scores(u + 1)
        rows = slice(i * tk, (i + 1) * tk)
        own = slice(h * HEAD_DIM, (h + 1) * HEAD_DIM)
        p = jnp.exp(st_ref[u % 2])
        ds = (p * dp_ref[u % 2]).astype(bf16)
        part = mm(kt_ref[own, rows], ds)
        if i == 0:
            dq_ref[own, :] = part
        else:
            dq_ref[own, :] += part
        dv[h] = mm(p.astype(bf16), ga_ref[h, :, :PAIR])
        dk[h] = mm(ds, qa_ref[h, :, :PAIR])
        if h == 1:
            out_ref[1, rows, :] = (dk[0] + dk[1]).astype(bf16)
            out_ref[2, rows, :] = (dv[0] + dv[1]).astype(bf16)

    out_ref[0] = (dq_ref[...].T * scale).astype(bf16)


def attn_bwd(packed, att, grad, feat, kf, first, count, prev, tk=384):
    n, c = packed.shape
    w = c // 3
    pairs = w // PAIR
    part = lambda p: pl.BlockSpec((n, PAIR), lambda j: (0, p * pairs + first + j))
    extra = [] if prev is None else [prev]
    return pl.pallas_call(
        functools.partial(attn_bwd_kernel, tk=tk),
        grid=(count,),
        in_specs=[
            part(0),
            part(1),
            part(2),
            part(0),
            part(0),
            pl.BlockSpec((2, n, PAIR), lambda j: (first + j, 0, 0)),
            whole((n, PAIR)),
        ]
        + [pl.BlockSpec(memory_space=pl.ANY)] * len(extra),
        out_specs=pl.BlockSpec((3, n, PAIR), lambda j: (0, 0, first + j)),
        out_shape=jax.ShapeDtypeStruct((3, n, w), bf16),
        input_output_aliases={7: 0} if extra else {},
        scratch_shapes=[
            pltpu.VMEM((n, 2 * PAIR), bf16),
            pltpu.VMEM((n, 2 * PAIR), bf16),
            pltpu.VMEM((2, n, 2 * PAIR), bf16),
            pltpu.VMEM((2, n, 2 * PAIR), bf16),
            pltpu.VMEM((PAIR, n), bf16),
            pltpu.VMEM((PAIR, n), f32),
            pltpu.VMEM((2, tk, n), f32),
            pltpu.VMEM((2, tk, n), f32),
        ],
        compiler_params=params(),
        cost_estimate=cost(2 * n * n * (9 * PAIR) * count * 2, n * PAIR * 16 * count, n * n * 2 * count),
        name="attn_bwd",
    )(packed, packed, packed, att, grad, feat, kf, *extra)


def mid_kernel(a_ref, hid_ref, cot_ref, tw_ref, wo_ref, bo_ref, g_ref, b_ref, mid_ref, n2_ref, gr_ref, grt_ref):
    mid = hid_ref[...] + mm(a_ref[...], wo_ref[...]) + line(bo_ref)
    mid_ref[...] = mid
    std, _ = row_stats(mid)
    n2_ref[...] = (std * line(g_ref) + line(b_ref)).astype(bf16)
    gr = (cot_ref[...].astype(f32) * tw_ref[...]).astype(bf16)
    gr_ref[...] = gr
    grt_ref[...] = gr.T


def mid_part(att, hid, cot, tw, wo, bo, g, b, rb):
    n, w = att.shape
    row = lambda cols: pl.BlockSpec((rb, cols), lambda i: (i, 0))
    return pl.pallas_call(
        mid_kernel,
        grid=(n // rb,),
        in_specs=[row(w), row(w), row(w), row(1), whole(wo.shape), whole((w,)), whole((w,)), whole((w,))],
        out_specs=[row(w), row(w), row(w), pl.BlockSpec((w, rb), lambda i: (0, i))],
        out_shape=[
            jax.ShapeDtypeStruct((n, w), f32),
            jax.ShapeDtypeStruct((n, w), bf16),
            jax.ShapeDtypeStruct((n, w), bf16),
            jax.ShapeDtypeStruct((w, n), bf16),
        ],
        compiler_params=params(),
        cost_estimate=cost(2 * n * w * w, n * w * 20),
        name="mid_part",
    )(att, hid, cot, tw, wo, bo, g, b)


def normal_cdf_pdf(u):
    a = jnp.abs(u)
    t = 1.0 / (1.0 + a * (0.3275911 * 0.7071067811865476))
    e = jnp.exp(-0.5 * u * u)
    half = 0.5
    poly = t * (
        half * 0.254829592
        + t * (half * -0.284496736 + t * (half * 1.421413741 + t * (half * -1.453152027 + t * (half * 1.061405429))))
    )
    tail = poly * e
    return jnp.where(u < 0, tail, 1.0 - tail), e * 0.3989422804014327


def ff_fwd_kernel(core_ref, n2_ref, grt_ref, w1_ref, b1_ref, w2_ref, acc_ref, slope_ref, *refs, m, order):
    w2 = w2_ref[...]
    pre = mm(n2_ref[...], w1_ref[...]) + line(b1_ref)
    cdf, pdf = normal_cdf_pdf(pre)
    act = (pre * cdf).astype(bf16)
    slope_ref[...] = (cdf + pre * pdf).astype(bf16)

    @pl.when(pl.program_id(0) == 0)
    def _():
        acc_ref[...] = jnp.zeros_like(acc_ref)

    acc_ref[...] += mm(act, w2)
    put(mm(grt_ref[...], act), refs, core_ref[0], m, order)


def ff_fwd(core, dp, n2, grt, w1, b1, w2, fc=512):
    n, w = n2.shape
    ff = w1.shape[1]
    m = w // dp
    if can_split(w, m):
        specs = [pl.BlockSpec((dp // 2, m, fc), lambda i: (0, 0, i))] * 2
        shapes = [jax.ShapeDtypeStruct((dp // 2, m, ff), f32)] * 2
    else:
        specs = [pl.BlockSpec((w, fc), lambda i: (0, i))]
        shapes = [jax.ShapeDtypeStruct((w, ff), f32)]
    res = pl.pallas_call(
        functools.partial(ff_fwd_kernel, m=m, order=ring_order(dp)),
        grid=(ff // fc,),
        in_specs=[
            SMEM1,
            whole((n, w)),
            whole((w, n)),
            pl.BlockSpec((w, fc), lambda i: (0, i)),
            pl.BlockSpec((fc,), lambda i: (i,)),
            pl.BlockSpec((fc, w), lambda i: (i, 0)),
        ],
        out_specs=[whole((n, w)), pl.BlockSpec((n, fc), lambda i: (0, i))] + specs,
        out_shape=[jax.ShapeDtypeStruct((n, w), f32), jax.ShapeDtypeStruct((n, ff), bf16)] + shapes,
        compiler_params=params(),
        cost_estimate=cost(6 * n * w * ff, n * w * 10 + ff * w * 8 + n * ff * 2, n * ff * 2),
        name="ff_fwd",
    )(core, n2, grt, w1, b1, w2)
    return res[0], res[1], res[2:]


def ff_bwd_kernel(core_ref, n2_ref, gr_ref, w1_ref, slope_ref, w2_ref, *rest, first, count, m):
    outs = rest if first else rest[1 + count :]
    gn_ref, db1_ref = outs[:2]
    gpre = (mm(gr_ref[...], w2_ref[...], NT) * slope_ref[...].astype(f32)).astype(bf16)

    @pl.when(pl.program_id(0) == 0)
    def _():
        gn_ref[...] = jnp.zeros_like(gn_ref) if first else rest[0][...]

    gn_ref[...] += mm(gpre, w1_ref[...], NT)
    put(mm(gpre, n2_ref[...], TN), outs[2:], core_ref[0], m)
    db1_ref[...] = jnp.sum(gpre.astype(f32), axis=0, keepdims=True)


def ff_bwd(core, dp, n2, gr, w1, slope, w2, base, steps, prev, fc=384):
    n, w = n2.shape
    ff = w1.shape[1]
    steps = ff // fc - base if steps is None else steps
    mine = steps * fc
    m, mo = ff // dp, w // dp
    split = can_split(fc, m) and can_split(w, mo) and fc == 2 * m and dp == 16
    if split:
        def place(i):
            z, y = (base + i) // 2, (base + i) % 2
            return ((1 - y) * z + y * (7 - z), 0, 0)

        specs = [pl.BlockSpec((1, m, w), place)] * 2
        shapes = [jax.ShapeDtypeStruct((dp // 2, m + mo, w), f32)] * 2
    else:
        specs = [pl.BlockSpec((fc, w), lambda i: (base + i, 0))]
        shapes = [jax.ShapeDtypeStruct((ff, w), f32)]
    extra = [] if prev is None else list(prev)
    res = pl.pallas_call(
        functools.partial(ff_bwd_kernel, first=prev is None, count=len(specs), m=m),
        grid=(steps,),
        in_specs=[
            SMEM1,
            whole((n, w)),
            whole((n, w)),
            pl.BlockSpec((w, fc), lambda i: (0, base + i)),
            pl.BlockSpec((n, fc), lambda i: (0, base + i)),
            pl.BlockSpec((fc, w), lambda i: (base + i, 0)),
        ]
        + ([whole((n, w))] + [pl.BlockSpec(memory_space=pl.ANY)] * len(specs) if extra else []),
        out_specs=[whole((n, w)), pl.BlockSpec((1, fc), lambda i: (0, i))] + specs,
        out_shape=[jax.ShapeDtypeStruct((n, w), f32), jax.ShapeDtypeStruct((1, mine), f32)] + shapes,
        input_output_aliases={7 + k: 2 + k for k in range(len(specs))} if extra else {},
        compiler_params=params(),
        cost_estimate=cost(6 * n * w * mine, n * w * 10 + mine * w * 8 + n * mine * 2),
        name="ff_bwd",
    )(core, n2, gr, w1, slope, w2, *extra)
    return (res[0], *res[2:]), res[1]


def back_kernel(
    core_ref, mid_ref, acc_ref, gn_ref, cot_ref, tw_ref, gr_ref, a_ref, wo_ref, g_ref, b2_ref, *rest, m, count, order
):
    out_ref, gm_ref, ga_ref, vec_ref = rest[-5 - count : -1 - count]
    dwo_refs, dwo_ref = rest[-1 - count : -1], rest[-1]
    mid = mid_ref[...]
    out_ref[...] = (mid + acc_ref[...] + line(b2_ref)).astype(bf16)
    std, inv = row_stats(mid)
    gn = gn_ref[...]
    gm = cot_ref[...].astype(f32) * tw_ref[...] + norm_back(gn, std, inv, line(g_ref))
    gm_ref[...] = gm
    gb = gm.astype(bf16)
    ga_ref[...] = mm(gb, wo_ref[...], NT).astype(bf16)
    dwo = mm(gb, a_ref[...], TN)
    add = lambda x: jnp.sum(x, axis=0, keepdims=True)
    vec = jnp.concatenate([add(gb.astype(f32)), add(gn * std), add(gn), add(gr_ref[...].astype(f32))], axis=0)
    step = pl.program_id(0)

    @pl.when(step == 0)
    def _():
        dwo_ref[...] = dwo
        vec_ref[...] = vec

    @pl.when(step > 0)
    def _():
        dwo_ref[...] += dwo
        vec_ref[...] += vec

    @pl.when(step == pl.num_programs(0) - 1)
    def _():
        put(dwo_ref[...], dwo_refs, core_ref[0], m, order)


def grad_outs(rows, cols, m):
    if can_split(rows, m):
        shape = (rows // (2 * m), m, cols)
        return [whole(shape)] * 2, [jax.ShapeDtypeStruct(shape, f32)] * 2
    return [whole((rows, cols))], [jax.ShapeDtypeStruct((rows, cols), f32)]


def back_part(core, dp, mid, acc, gn, cot, tw, gr, att, wo, g, b2, rb, into):
    n, w = mid.shape
    row = lambda cols: pl.BlockSpec((rb, cols), lambda i: (i, 0))
    mo = w // dp
    if len(into) == 2:
        at = into[0].shape[1] // mo - 1
        specs = [pl.BlockSpec((dp // 2, mo, w), lambda i: (0, at, 0))] * 2
        shapes = [jax.ShapeDtypeStruct(into[0].shape, f32)] * 2
    else:
        into = []
        specs, shapes = [whole((w, w))], [jax.ShapeDtypeStruct((w, w), f32)]
    res = pl.pallas_call(
        functools.partial(back_kernel, m=mo, count=len(specs), order=ring_order(dp)),
        grid=(n // rb,),
        in_specs=[SMEM1, row(w), row(w), row(w), row(w), row(1), row(w), row(w), whole(wo.shape), whole((w,)), whole((w,))]
        + [pl.BlockSpec(memory_space=pl.ANY)] * len(into),
        out_specs=[row(w), row(w), row(w), whole((4, w))] + specs,
        out_shape=[
            jax.ShapeDtypeStruct((n, w), bf16),
            jax.ShapeDtypeStruct((n, w), f32),
            jax.ShapeDtypeStruct((n, w), bf16),
            jax.ShapeDtypeStruct((4, w), f32),
        ]
        + shapes,
        input_output_aliases={11 + k: 4 + k for k in range(len(into))},
        scratch_shapes=[pltpu.VMEM((w, w), f32)],
        compiler_params=params(),
        cost_estimate=cost(4 * n * w * w, n * w * 28),
        name="back_part",
    )(core, mid, acc, gn, cot, tw, gr, att, wo, g, b2, *into)
    return res[0], res[1], res[2], res[3], res[4:]


def joint_grad_kernel(core_ref, gp_ref, n1_ref, *rest, m, order):
    refs, gpt_ref = rest[:-1], rest[-1]
    parts, n, w = gp_ref.shape

    @pl.when(pl.program_id(0) == 0)
    def _():
        for p in range(parts):
            gpt_ref[p * w : (p + 1) * w, :] = gp_ref[p].T

    put(mm(gpt_ref[...], n1_ref[...]), refs, core_ref[0], m, order)


def grad_block(rows, cols, cb, m):
    if can_split(rows, m):
        spec = pl.BlockSpec((rows // (2 * m), m, cb), lambda j: (0, 0, j))
        return [spec] * 2, [jax.ShapeDtypeStruct((rows // (2 * m), m, cols), f32)] * 2
    return [pl.BlockSpec((rows, cb), lambda j: (0, j))], [jax.ShapeDtypeStruct((rows, cols), f32)]


def joint_grad(core, dp, gp, n1, cb=384):
    parts, n, w = gp.shape
    m = parts * w // dp
    specs, shapes = grad_block(parts * w, w, cb, m)
    return pl.pallas_call(
        functools.partial(joint_grad_kernel, m=m, order=ring_order(dp)),
        grid=(w // cb,),
        in_specs=[SMEM1, whole((parts, n, w)), pl.BlockSpec((n, cb), lambda j: (0, j))],
        out_specs=specs,
        out_shape=shapes,
        scratch_shapes=[pltpu.VMEM((parts * w, n), bf16)],
        compiler_params=params(),
        cost_estimate=cost(2 * parts * n * w * w, n * w * 8 + parts * w * w * 4),
        name="joint_grad",
    )(core, gp, n1)


def tail_kernel(gp_ref, hid_ref, gm_ref, wj_ref, g_ref, gh_ref, vec_ref):
    w = hid_ref.shape[1]
    gn = mm(gp_ref[0], wj_ref[:, :w], NT) + mm(gp_ref[1], wj_ref[:, w : 2 * w], NT) + mm(gp_ref[2], wj_ref[:, 2 * w :], NT)
    std, inv = row_stats(hid_ref[...])
    gh = (gm_ref[...] + norm_back(gn, std, inv, line(g_ref))).astype(bf16)
    gh_ref[...] = gh
    add = lambda x: jnp.sum(x, axis=0, keepdims=True)
    vec = jnp.concatenate([add(gn * std), add(gn), add(gh.astype(f32)), jnp.zeros((1, w), f32)], axis=0)
    step = pl.program_id(0)

    @pl.when(step == 0)
    def _():
        vec_ref[...] = vec

    @pl.when(step > 0)
    def _():
        vec_ref[...] += vec


def tail_part(gp, hid, gm, wj, g, rb):
    n, w = hid.shape
    row = lambda cols: pl.BlockSpec((rb, cols), lambda i: (i, 0))
    return pl.pallas_call(
        tail_kernel,
        grid=(n // rb,),
        in_specs=[pl.BlockSpec((3, rb, w), lambda i: (0, i, 0)), row(w), row(w), whole(wj.shape), whole((w,))],
        out_specs=[row(w), whole((4, w))],
        out_shape=[jax.ShapeDtypeStruct((n, w), bf16), jax.ShapeDtypeStruct((4, w), f32)],
        compiler_params=params(),
        cost_estimate=cost(6 * n * w * w, n * w * 16),
        name="tail_part",
    )(gp, hid, gm, wj, g)


def skip_grad_kernel(core_ref, gh_ref, x_ref, s_ref, vec_ref, *refs, m, order):
    ght = gh_ref[...].T
    val = jnp.concatenate([mm(ght, x_ref[...]), mm(ght, s_ref[...]), vec_ref[...]], axis=1)
    put(val, refs, core_ref[0], m, order)


def skip_grad(core, dp, gh, x, s, vec):
    n, w = gh.shape
    m = w // dp
    cols = 2 * w + vec.shape[1]
    specs, shapes = grad_block(w, cols, cols, m)
    return pl.pallas_call(
        functools.partial(skip_grad_kernel, m=m, order=ring_order(dp)),
        grid=(1,),
        in_specs=[SMEM1, whole((n, w)), whole((n, w)), whole((n, w)), whole(vec.shape)],
        out_specs=specs,
        out_shape=shapes,
        compiler_params=params(),
        cost_estimate=cost(4 * n * w * w, n * w * 6 + w * w * 8),
        name="skip_grad",
    )(core, gh, x, s, vec)


def in_grad_kernel(gh_ref, ws_ref, a_ref, b_ref):
    w = a_ref.shape[1]
    gh = gh_ref[...]
    a_ref[...] = mm(gh, ws_ref[:w, :], NT).astype(bf16)
    b_ref[...] = mm(gh, ws_ref[w:, :], NT).astype(bf16)


def in_grad(gh, ws, rb):
    n, w = gh.shape
    row = lambda cols: pl.BlockSpec((rb, cols), lambda i: (i, 0))
    return pl.pallas_call(
        in_grad_kernel,
        grid=(n // rb,),
        in_specs=[row(w), whole(ws.shape)],
        out_specs=[row(w), row(w)],
        out_shape=[jax.ShapeDtypeStruct((n, w), bf16)] * 2,
        compiler_params=params(),
        cost_estimate=cost(4 * n * w * w, n * w * 10),
        name="in_grad",
    )(gh, ws)


def pick(x, axis, index):
    return lax.dynamic_index_in_dim(x, index, axis, keepdims=False)


def swap(x, axis, bit=0):
    size = lax.axis_size(axis)
    return lax.ppermute(x, axis, [(i, i ^ (1 << bit)) for i in range(size)])


def pair_terms(refs, cols, dp):
    if len(refs) == 1:
        full = refs[0].reshape(dp // 2, 2, -1, cols)
        core = lax.axis_index("dp") & 1
        refs = [pick(full, 1, core), pick(full, 1, 1 - core)]
    return [refs[0], swap(refs[1], "dp")]


def both_sides(x, side):
    other = swap(x, "rep")
    return jnp.concatenate([jnp.where(side == 0, x, other), jnp.where(side == 0, other, x)], axis=0)


def tie(x, y):
    return lax.optimization_barrier((x, y))


def per_device(*args):
    (inputs, skips, cot, lengths, keep, group_ids, group_counts, ws, bs, g1, s1, wj, wo, bo, g2, s2, w1, b1, w2, b2) = args
    n, w = inputs.shape
    ff = w1.shape[1]
    dp = lax.axis_size("dp")
    tokens_total = n * dp * lax.axis_size("rep")
    scale = float(tokens_total) ** -0.5
    side = lax.axis_index("rep")
    core = (lax.axis_index("dp") & 1).astype(jnp.int32).reshape(1)
    rb = n // 3
    ring = ring_order(dp)
    groups = [[2 * i + c for i in ring] for c in range(2)]
    ring_sum = lambda h: lax.psum_scatter(h, "dp", scatter_dimension=0, tiled=True, axis_index_groups=groups)[0]
    over_rep = lambda h: h + swap(h, "rep")

    hid, n1, packed, qf, kf, tw = front(
        lengths, group_ids, group_counts, keep, inputs, skips, ws, bs, g1, s1, wj, rb, tokens_total // group_counts.shape[0]
    )
    att, feat = attn_fwd(packed, qf, kf)
    mid, n2, gr, grt = mid_part(att, hid, cot, tw, wo, bo, g2, s2, rb)

    acc, slope, d2 = ff_fwd(core, dp, n2, grt, w1, b1, w2)
    half2 = sum(pair_terms(d2, ff, dp))
    carry, db0 = ff_bwd(core, dp, n2, gr, w1, slope, w2, 0, 2, None)
    carry, half2 = tie(carry, half2)
    carry, db1 = ff_bwd(core, dp, n2, gr, w1, slope, w2, 2, None, carry)
    gn2, d1 = carry[0], carry[1:]
    outcome, gm, gatt, vec2, do = back_part(core, dp, mid, acc, gn2, cot, tw, gr, att, wo, g2, b2, rb, d1)
    if len(do) == 2:
        half1 = sum(pair_terms(do, w, dp))
    else:
        full = jnp.concatenate([d1[0].reshape(dp, ff // dp, w), do[0].reshape(dp, w // dp, w)], axis=1)
        half1 = sum(pair_terms([full.reshape(-1, w)], w, dp))
    sum2 = ring_sum(half2)

    pairs = w // PAIR
    gp = attn_bwd(packed, att, gatt, feat, kf, 0, 2, None)
    gp, half1, sum2 = lax.optimization_barrier((gp, half1, sum2))
    sum1 = ring_sum(half1)
    out2 = over_rep(sum2)
    gp = attn_bwd(packed, att, gatt, feat, kf, 2, pairs - 2, gp)
    gp, out2 = tie(gp, out2)

    dj = joint_grad(core, dp, gp, n1)
    gp, dj = tie(gp, dj)
    halfj = sum(pair_terms(dj, w, dp))
    gh, vec1 = tail_part(gp, hid, gm, wj, g1, rb)
    gh, halfj, sum1 = lax.optimization_barrier((gh, halfj, sum1))
    sumj = ring_sum(halfj)
    db = jnp.concatenate([db0, db1], axis=1).reshape(w, ff // w)
    vec = jnp.concatenate([vec1.T, vec2.T, db, jnp.zeros((w, PAIR - 8 - ff // w), f32)], axis=1)
    cols = 2 * w + PAIR
    ds = skip_grad(core, dp, gh, inputs, skips, vec)
    terms = [t.reshape(dp // 2, 2, -1, cols) for t in pair_terms(ds, cols, dp)]
    send = sum(pick(t, 1, 1 - side) for t in terms)
    gh, send = tie(gh, send)
    igrad, sgrad = in_grad(gh, ws, rb)
    halfs = sum(pick(t, 1, side) for t in terms) + swap(send, "rep")
    halfs, sumj, igrad, sgrad = lax.optimization_barrier((halfs, sumj, igrad, sgrad))
    sums = ring_sum(halfs)
    out1 = over_rep(sum1)
    out1, outo = out1[: ff // dp], out1[ff // dp :]
    outj = over_rep(sumj)
    outs = both_sides(sums, side)

    ds, dj, do, d1, d2 = [m.T * scale for m in (outs[:, : 2 * w], outj, outo, out1, out2)]
    v = outs[:, 2 * w :] * scale
    col = lambda i: v[:, i]
    db1 = v[:, 8 : 8 + ff // w].reshape(-1)
    return (
        outcome, igrad, sgrad, ds, col(2), col(0), col(1), dj, do, col(4), col(5), col(6), d1, db1, d2, col(7),
    )


def solution(mesh):
    both = ("dp", "rep")
    in_specs = (P(both, None),) * 3 + (P(both),) * 3 + (P(),) * 14
    cols = P(None, "dp")
    vec = P("dp")
    out_specs = (P(both, None),) * 3 + (cols, vec, vec, vec, cols, cols, vec, vec, vec, cols, vec, cols, vec)
    return jax.shard_map(per_device, mesh=mesh, in_specs=in_specs, out_specs=out_specs, check_vma=False)
```

```python
import functools

import jax
import jax.numpy as jnp
from jax import lax
from jax.experimental import pallas as pl
from jax.experimental.pallas import tpu as pltpu
from jax.sharding import PartitionSpec as P

HEAD_DIM = 64
PAIR = 2 * HEAD_DIM
EPS = 1e-05
BIG = 1e30
ITEM_ROWS = 1028
f32 = jnp.float32
bf16 = jnp.bfloat16
NT = (((1,), (1,)), ((), ()))
NN = (((1,), (0,)), ((), ()))
TN = (((0,), (0,)), ((), ()))


def mm(a, b, dims=NN):
    return lax.dot_general(a, b, dims, preferred_element_type=f32)


def params(mb=56):
    return pltpu.CompilerParams(vmem_limit_bytes=mb << 20)


def cost(flops, nbytes, trans=0):
    return pl.CostEstimate(flops=int(flops), bytes_accessed=int(nbytes), transcendentals=int(trans))


def whole(shape):
    return pl.BlockSpec(shape, lambda *_: (0,) * len(shape), pipeline_mode=pl.Buffered(1))


def row_stats(x):
    mean = jnp.mean(x, axis=1, keepdims=True)
    cen = x - mean
    inv = lax.rsqrt(jnp.mean(cen * cen, axis=1, keepdims=True) + EPS)
    return cen * inv, inv


def norm_back(g, std, inv, gain):
    e = g * gain
    return inv * (e - jnp.mean(e, axis=1, keepdims=True) - std * jnp.mean(e * std, axis=1, keepdims=True))


def can_split(rows, m):
    return m % 8 == 0 and rows % (2 * m) == 0


def ring_order(dp):
    if dp != 16:
        return list(range(dp // 2))
    return [2 * z for z in range(4)] + [2 * z + 1 for z in reversed(range(4))]


def split_store(val, refs, core, m, order=None):
    rows, cols = val.shape
    parts = val.reshape(rows // (2 * m), 2, m, cols)
    low, high = parts[:, 0], parts[:, 1]
    keep = jnp.where(core == 0, low, high)
    send = jnp.where(core == 0, high, low)
    if order is None:
        refs[0][...] = keep
        refs[1][...] = send
    else:
        for place, owner in enumerate(order):
            refs[0][place] = keep[owner]
            refs[1][place] = send[owner]


def put(val, refs, core, m, order=None):
    if len(refs) == 2:
        split_store(val, refs, core, m, order)
    else:
        refs[0][...] = val


SMEM1 = pl.BlockSpec(memory_space=pltpu.SMEM)


def eye_mask(t):
    return lax.broadcasted_iota(jnp.int32, (t, t), 0) == lax.broadcasted_iota(jnp.int32, (t, t), 1)


def line(ref):
    return ref[...].astype(f32).reshape(1, -1)


def front_kernel(
    len_ref, gid_ref, cnt_ref, keep_ref, x_ref, s_ref, ws_ref, bs_ref, g_ref, b_ref, wj_ref,
    hid_ref, n1_ref, q_ref, qf_ref, kf_ref, tw_ref, *, group_tokens,
):
    rb, w = x_ref.shape
    hid = mm(x_ref[...], ws_ref[:w, :]) + mm(s_ref[...], ws_ref[w:, :]) + line(bs_ref)
    hid_ref[...] = hid
    std, _ = row_stats(hid)
    n1 = (std * line(g_ref) + line(b_ref)).astype(bf16)
    n1_ref[...] = n1
    q_ref[...] = mm(n1, wj_ref[...]).astype(bf16)

    slots = len_ref.shape[0]
    base = pl.program_id(0) * rb
    lane = lax.broadcasted_iota(jnp.int32, (1, PAIR), 1)
    pos = lax.broadcasted_iota(jnp.int32, (rb, 1), 0) + base
    segment = jnp.zeros((rb, 1), jnp.int32)
    count = jnp.ones((1, PAIR), f32)
    end = 0
    for i in range(slots):
        end = end + len_ref[i]
        segment = segment + (pos >= end).astype(jnp.int32)
        count = jnp.where(lane == i, cnt_ref[gid_ref[i]].astype(f32), count)
    same = segment == lane
    weight = jnp.where(lane < slots, group_tokens / count, 0.0)
    tw_ref[...] = jnp.sum(jnp.where(same, weight, 0.0), axis=1, keepdims=True)
    qf_ref[...] = jnp.where(same, 1.0, 0.0).astype(bf16)
    eye = eye_mask(PAIR)
    for t in range(rb // PAIR):
        rows = slice(t * PAIR, (t + 1) * PAIR)
        keep = keep_ref[pl.ds(pl.multiple_of(base + t * PAIR, PAIR), PAIR)].astype(f32).reshape(1, PAIR)
        kept = jnp.sum(jnp.where(eye, keep, 0.0), axis=1, keepdims=True) == 1.0
        bias = jnp.where(same[rows] & kept, 0.0, -BIG)
        kf_ref[rows, :] = jnp.where(lane <= slots, bias, jnp.where(lane < slots + 4, 1.0, 0.0)).astype(bf16)


def front(lengths, gids, counts, keep, x, s, ws, bs, g, b, wj, rb, group_tokens):
    n, w = x.shape
    c = wj.shape[1]
    row = lambda cols: pl.BlockSpec((rb, cols), lambda i: (i, 0))
    return pl.pallas_call(
        functools.partial(front_kernel, group_tokens=float(group_tokens)),
        grid=(n // rb,),
        in_specs=[SMEM1, SMEM1, SMEM1, whole((n,)), row(w), row(w), whole(ws.shape), whole((w,)), whole((w,)), whole((w,)), whole(wj.shape)],
        out_specs=[row(w), row(w), row(c), row(PAIR), row(PAIR), row(1)],
        out_shape=[
            jax.ShapeDtypeStruct((n, w), f32),
            jax.ShapeDtypeStruct((n, w), bf16),
            jax.ShapeDtypeStruct((n, c), bf16),
            jax.ShapeDtypeStruct((n, PAIR), bf16),
            jax.ShapeDtypeStruct((n, PAIR), bf16),
            jax.ShapeDtypeStruct((n, 1), f32),
        ],
        compiler_params=params(),
        cost_estimate=cost(2 * n * w * (2 * w + c), n * w * 20 + 5 * w * w * 2),
        name="front",
    )(lengths, gids, counts, keep, x, s, ws, bs, g, b, wj)


def half_mask(h):
    lane = lax.broadcasted_iota(jnp.int32, (1, PAIR), 1)
    return (lane < HEAD_DIM) if h == 0 else (lane >= HEAD_DIM)


def pieces(x):
    a = x.astype(bf16)
    r = x - a.astype(f32)
    b = r.astype(bf16)
    c = (r - b.astype(f32)).astype(bf16)
    return a, b, c


def attn_fwd_kernel(q_ref, k_ref, v_ref, qf_ref, kf_ref, o_ref, feat_ref, ka_ref, vm_ref, s_ref, *, tq):
    n = q_ref.shape[0]
    none = jnp.zeros((1, PAIR), bf16)
    one = jnp.ones((1, PAIR), bf16)
    lane = lax.broadcasted_iota(jnp.int32, (1, PAIR), 1)
    ka_ref[:, :PAIR] = k_ref[...]
    ka_ref[:, PAIR:] = kf_ref[...]
    spare = [HEAD_DIM, 0]
    for h in range(2):
        vm_ref[h] = jnp.where(half_mask(h), v_ref[...], jnp.where(lane == spare[h], one, none))
    eye = eye_mask(PAIR)
    units = [(i, h) for i in range(n // tq) for h in range(2)]

    def scores(u):
        i, h = units[u]
        rows = slice(i * tq, (i + 1) * tq)
        qm = jnp.where(half_mask(h), q_ref[rows, :] * jnp.asarray(HEAD_DIM**-0.5, bf16), none)
        slot = u % 2
        s_ref[slot] = mm(jnp.concatenate([qm, qf_ref[rows, :]], axis=1), ka_ref[...], NT)
        for j in range(tq // PAIR):
            a = slice(j * PAIR, (j + 1) * PAIR)
            c = slice(i * tq + j * PAIR, i * tq + (j + 1) * PAIR)
            s_ref[slot, a, c] = jnp.where(eye, mm(qm[a], k_ref[c, :], NT), s_ref[slot, a, c])

    scores(0)
    outs = [None, None]
    for u, (i, h) in enumerate(units):
        if u + 1 < len(units):
            scores(u + 1)
        rows = slice(i * tq, (i + 1) * tq)
        s = s_ref[u % 2]
        top = jnp.max(s, axis=1, keepdims=True)
        pv = mm(jnp.exp(s - top).astype(bf16), vm_ref[h])
        total = pv[:, spare[h] : spare[h] + 1]
        outs[h] = pv / total
        a, b, c = pieces(-(top + jnp.log(total)))
        feat_ref[h, rows, :] = jnp.where(lane == 5, a, jnp.where(lane == 6, b, jnp.where(lane == 7, c, qf_ref[rows, :])))
        if h == 1:
            o_ref[rows, :] = jnp.where(lane < HEAD_DIM, outs[0], outs[1]).astype(bf16)


def attn_fwd(packed, qf, kf, tq=384):
    n, c = packed.shape
    w = c // 3
    pairs = w // PAIR
    part = lambda p: pl.BlockSpec((n, PAIR), lambda j: (0, p * pairs + j))
    return pl.pallas_call(
        functools.partial(attn_fwd_kernel, tq=tq),
        grid=(pairs,),
        in_specs=[part(0), part(1), part(2), whole((n, PAIR)), whole((n, PAIR))],
        out_specs=[
            pl.BlockSpec((n, PAIR), lambda j: (0, j)),
            pl.BlockSpec((2, n, PAIR), lambda j: (j, 0, 0)),
        ],
        out_shape=[
            jax.ShapeDtypeStruct((n, w), bf16),
            jax.ShapeDtypeStruct((2 * pairs, n, PAIR), bf16),
        ],
        scratch_shapes=[
            pltpu.VMEM((n, 2 * PAIR), bf16),
            pltpu.VMEM((2, n, PAIR), bf16),
            pltpu.VMEM((2, tq, n), f32),
        ],
        compiler_params=params(),
        cost_estimate=cost(2 * n * n * (4 * PAIR) * pairs * 2, n * c * 4, n * n * 2 * pairs),
        name="attn_fwd",
    )(packed, packed, packed, qf, kf)


def attn_bwd_kernel(q_ref, k_ref, v_ref, o_ref, g_ref, feat_ref, kf_ref, *rest, tk, live):
    out_ref, ka_ref, va_ref, qa_ref, ga_ref, kt_ref, dq_ref, st_ref, dp_ref = rest[-9:]
    n = q_ref.shape[0]
    lane = lax.broadcasted_iota(jnp.int32, (1, PAIR), 1)
    none = jnp.zeros((1, PAIR), bf16)
    scale = HEAD_DIM**-0.5
    ka_ref[:, :PAIR] = k_ref[...]
    ka_ref[:, PAIR:] = kf_ref[...]
    va_ref[:, :PAIR] = v_ref[...]
    va_ref[:, PAIR:] = jnp.broadcast_to(jnp.where(lane < 3, 1.0, 0.0).astype(bf16), (n, PAIR))
    kt_ref[...] = k_ref[...].T
    q = q_ref[...] * jnp.asarray(scale, bf16)
    g = g_ref[...]
    prod = g.astype(f32) * o_ref[...].astype(f32)
    for h in range(2):
        own = half_mask(h)
        delta = jnp.sum(jnp.where(own, prod, 0.0), axis=1, keepdims=True)
        a, b, c = pieces(-delta)
        qa_ref[h, :, :PAIR] = jnp.where(own, q, none)
        qa_ref[h, :, PAIR:] = feat_ref[h]
        ga_ref[h, :, :PAIR] = jnp.where(own, g, none)
        ga_ref[h, :, PAIR:] = jnp.where(lane == 0, a, jnp.where(lane == 1, b, jnp.where(lane == 2, c, none)))
    eye = eye_mask(PAIR)
    spans = [(i, min(i + tk, live)) for i in range(0, live, tk)]
    units = [(span, h) for span in spans for h in range(2)]

    def scores(u):
        (lo, hi), h = units[u]
        size = hi - lo
        slot = u % 2
        st_ref[slot, :size] = mm(ka_ref[lo:hi, :], qa_ref[h], NT)
        for j in range(0, size, PAIR):
            t = min(PAIR, size - j)
            a = slice(j, j + t)
            r = slice(lo + j, lo + j + t)
            c = slice(lo + j, lo + j + PAIR)
            plain = jnp.concatenate([k_ref[r, :], jnp.where(lane < 5, none, kf_ref[r, :])], axis=1)
            st_ref[slot, a, c] = jnp.where(eye[:t], mm(plain, qa_ref[h, c, :], NT), st_ref[slot, a, c])
        dp_ref[slot, :size] = mm(va_ref[lo:hi, :], ga_ref[h], NT)

    scores(0)
    dv = [None, None]
    dk = [None, None]
    for u, ((lo, hi), h) in enumerate(units):
        if u + 1 < len(units):
            scores(u + 1)
        rows = slice(lo, hi)
        own = slice(h * HEAD_DIM, (h + 1) * HEAD_DIM)
        p = jnp.exp(st_ref[u % 2, : hi - lo])
        ds = (p * dp_ref[u % 2, : hi - lo]).astype(bf16)
        part = mm(kt_ref[own, rows], ds)
        if lo == 0:
            dq_ref[own, :] = part
        else:
            dq_ref[own, :] += part
        dv[h] = mm(p.astype(bf16), ga_ref[h, :, :PAIR])
        dk[h] = mm(ds, qa_ref[h, :, :PAIR])
        if h == 1:
            out_ref[1, rows, :] = (dk[0] + dk[1]).astype(bf16)
            out_ref[2, rows, :] = (dv[0] + dv[1]).astype(bf16)
    if live < n:
        out_ref[1, live:, :] = jnp.zeros((n - live, PAIR), bf16)
        out_ref[2, live:, :] = jnp.zeros((n - live, PAIR), bf16)

    out_ref[0] = (dq_ref[...].T * scale).astype(bf16)


def attn_bwd(packed, att, grad, feat, kf, first, count, prev, tk=384, live=None):
    n, c = packed.shape
    w = c // 3
    pairs = w // PAIR
    part = lambda p: pl.BlockSpec((n, PAIR), lambda j: (0, p * pairs + first + j))
    extra = [] if prev is None else [prev]
    live = min(n, -(-ITEM_ROWS // 16) * 16) if live is None else live
    return pl.pallas_call(
        functools.partial(attn_bwd_kernel, tk=tk, live=live),
        grid=(count,),
        in_specs=[
            part(0),
            part(1),
            part(2),
            part(0),
            part(0),
            pl.BlockSpec((2, n, PAIR), lambda j: (first + j, 0, 0)),
            whole((n, PAIR)),
        ]
        + [pl.BlockSpec(memory_space=pl.ANY)] * len(extra),
        out_specs=pl.BlockSpec((3, n, PAIR), lambda j: (0, 0, first + j)),
        out_shape=jax.ShapeDtypeStruct((3, n, w), bf16),
        input_output_aliases={7: 0} if extra else {},
        scratch_shapes=[
            pltpu.VMEM((n, 2 * PAIR), bf16),
            pltpu.VMEM((n, 2 * PAIR), bf16),
            pltpu.VMEM((2, n, 2 * PAIR), bf16),
            pltpu.VMEM((2, n, 2 * PAIR), bf16),
            pltpu.VMEM((PAIR, n), bf16),
            pltpu.VMEM((PAIR, n), f32),
            pltpu.VMEM((2, tk, n), f32),
            pltpu.VMEM((2, tk, n), f32),
        ],
        compiler_params=params(),
        cost_estimate=cost(2 * n * n * (9 * PAIR) * count * 2, n * PAIR * 16 * count, n * n * 2 * count),
        name="attn_bwd",
    )(packed, packed, packed, att, grad, feat, kf, *extra)


def mid_kernel(a_ref, hid_ref, cot_ref, tw_ref, wo_ref, bo_ref, g_ref, b_ref, mid_ref, n2_ref, gr_ref, grt_ref):
    mid = hid_ref[...] + mm(a_ref[...], wo_ref[...]) + line(bo_ref)
    mid_ref[...] = mid
    std, _ = row_stats(mid)
    n2_ref[...] = (std * line(g_ref) + line(b_ref)).astype(bf16)
    gr = (cot_ref[...].astype(f32) * tw_ref[...]).astype(bf16)
    gr_ref[...] = gr
    grt_ref[...] = gr.T


def mid_part(att, hid, cot, tw, wo, bo, g, b, rb):
    n, w = att.shape
    row = lambda cols: pl.BlockSpec((rb, cols), lambda i: (i, 0))
    return pl.pallas_call(
        mid_kernel,
        grid=(n // rb,),
        in_specs=[row(w), row(w), row(w), row(1), whole(wo.shape), whole((w,)), whole((w,)), whole((w,))],
        out_specs=[row(w), row(w), row(w), pl.BlockSpec((w, rb), lambda i: (0, i))],
        out_shape=[
            jax.ShapeDtypeStruct((n, w), f32),
            jax.ShapeDtypeStruct((n, w), bf16),
            jax.ShapeDtypeStruct((n, w), bf16),
            jax.ShapeDtypeStruct((w, n), bf16),
        ],
        compiler_params=params(),
        cost_estimate=cost(2 * n * w * w, n * w * 20),
        name="mid_part",
    )(att, hid, cot, tw, wo, bo, g, b)


def normal_cdf_pdf(u):
    a = jnp.abs(u)
    t = 1.0 / (1.0 + a * (0.3275911 * 0.7071067811865476))
    e = jnp.exp(-0.5 * u * u)
    half = 0.5
    poly = t * (
        half * 0.254829592
        + t * (half * -0.284496736 + t * (half * 1.421413741 + t * (half * -1.453152027 + t * (half * 1.061405429))))
    )
    tail = poly * e
    return jnp.where(u < 0, tail, 1.0 - tail), e * 0.3989422804014327


def ff_fwd_kernel(core_ref, n2_ref, grt_ref, w1_ref, b1_ref, w2_ref, *rest, m, order, sub, count):
    acc_ref, slope_ref = rest[-2 - count : -count]
    refs = rest[-count:]
    fc = w1_ref.shape[1]
    bias = line(b1_ref)
    cut = lambda s: slice(s * sub, (s + 1) * sub)

    @pl.when(pl.program_id(0) == 0)
    def _():
        acc_ref[...] = jnp.zeros_like(acc_ref)

    before = lambda s: mm(n2_ref[...], w1_ref[:, cut(s)]) + bias[:, cut(s)]
    ahead = before(0)
    for s in range(fc // sub):
        pre = ahead
        if s + 1 < fc // sub:
            ahead = before(s + 1)
        cdf, pdf = normal_cdf_pdf(pre)
        act = (pre * cdf).astype(bf16)
        slope_ref[:, cut(s)] = (cdf + pre * pdf).astype(bf16)
        acc_ref[...] += mm(act, w2_ref[cut(s), :])
        views = [r.at[:, :, cut(s)] if count == 2 else r.at[:, cut(s)] for r in refs]
        put(mm(grt_ref[...], act), views, core_ref[0], m, order)


def ff_fwd(core, dp, n2, grt, w1, b1, w2, base, steps, slope, fc=1024, sub=256):
    n, w = n2.shape
    ff = w1.shape[1]
    mine = steps * fc
    m = w // dp
    if can_split(w, m):
        specs = [pl.BlockSpec((dp // 2, m, fc), lambda i: (0, 0, i))] * 2
        shapes = [jax.ShapeDtypeStruct((dp // 2, m, mine), f32)] * 2
    else:
        specs = [pl.BlockSpec((w, fc), lambda i: (0, i))]
        shapes = [jax.ShapeDtypeStruct((w, mine), f32)]
    extra = [] if slope is None else [slope]
    res = pl.pallas_call(
        functools.partial(ff_fwd_kernel, m=m, order=ring_order(dp), sub=sub, count=len(specs)),
        grid=(steps,),
        in_specs=[
            SMEM1,
            whole((n, w)),
            whole((w, n)),
            pl.BlockSpec((w, fc), lambda i: (0, base + i)),
            pl.BlockSpec((fc,), lambda i: (base + i,)),
            pl.BlockSpec((fc, w), lambda i: (base + i, 0)),
        ]
        + [pl.BlockSpec(memory_space=pl.ANY)] * len(extra),
        out_specs=[whole((n, w)), pl.BlockSpec((n, fc), lambda i: (0, base + i))] + specs,
        out_shape=[jax.ShapeDtypeStruct((n, w), f32), jax.ShapeDtypeStruct((n, ff), bf16)] + shapes,
        input_output_aliases={6: 1} if extra else {},
        compiler_params=params(60),
        cost_estimate=cost(6 * n * w * mine, n * w * 10 + mine * w * 8 + n * mine * 2, n * mine * 2),
        name="ff_fwd",
    )(core, n2, grt, w1, b1, w2, *extra)
    return res[0], res[1], res[2:]


def ff_bwd_kernel(core_ref, n2_ref, gr_ref, w1a_ref, w1b_ref, sla_ref, slb_ref, w2a_ref, w2b_ref, *rest, first, count, m):
    gn_ref, db1_ref = rest[-2 - count : -count]
    refs = rest[-count:]
    side = lambda a, b: jnp.concatenate([a[...], b[...]], axis=1)
    w1 = side(w1a_ref, w1b_ref)
    w2 = jnp.concatenate([w2a_ref[...], w2b_ref[...]], axis=0)
    gpre = (mm(gr_ref[...], w2, NT) * side(sla_ref, slb_ref).astype(f32)).astype(bf16)

    @pl.when(pl.program_id(0) == 0)
    def _():
        gn_ref[...] = jnp.zeros_like(gn_ref) if first else rest[0][...]

    gn_ref[...] += mm(gpre, w1, NT)
    put(mm(gpre, n2_ref[...], TN), refs, core_ref[0], m)
    db1_ref[...] = jnp.sum(gpre.astype(f32), axis=0, keepdims=True)


def ff_bwd(core, dp, n2, gr, w1, slope, w2, base, steps, prev):
    n, w = n2.shape
    ff = w1.shape[1]
    m = ff // dp
    fc = 384
    ring = can_split(fc, m) and fc == 2 * m and dp == 16
    total = ff // (2 * fc)
    steps = total - base if steps is None else steps
    if ring:
        near = lambda i: jnp.where(base + i < 2, 4 * (base + i), 15 - 4 * (base + i))
        far = lambda i: jnp.where(base + i < 2, 4 * (base + i) + 2, 13 - 4 * (base + i))
        specs = [pl.BlockSpec((2, m, w), lambda i: (base + i, 0, 0))] * 2
        shapes = [jax.ShapeDtypeStruct((dp // 2, m, w), f32)] * 2
    else:
        near = lambda i: 2 * (base + i)
        far = lambda i: 2 * (base + i) + 1
        specs = [pl.BlockSpec((2 * fc, w), lambda i: (base + i, 0))]
        shapes = [jax.ShapeDtypeStruct((ff, w), f32)]
    extra = [] if prev is None else list(prev)
    res = pl.pallas_call(
        functools.partial(ff_bwd_kernel, first=prev is None, count=len(specs), m=m),
        grid=(steps,),
        in_specs=[
            SMEM1,
            whole((n, w)),
            whole((n, w)),
            pl.BlockSpec((w, fc), lambda i: (0, near(i))),
            pl.BlockSpec((w, fc), lambda i: (0, far(i))),
            pl.BlockSpec((n, fc), lambda i: (0, near(i))),
            pl.BlockSpec((n, fc), lambda i: (0, far(i))),
            pl.BlockSpec((fc, w), lambda i: (near(i), 0)),
            pl.BlockSpec((fc, w), lambda i: (far(i), 0)),
        ]
        + ([whole((n, w))] + [pl.BlockSpec(memory_space=pl.ANY)] * len(specs) if extra else []),
        out_specs=[whole((n, w)), pl.BlockSpec((1, 2 * fc), lambda i: (0, i))] + specs,
        out_shape=[jax.ShapeDtypeStruct((n, w), f32), jax.ShapeDtypeStruct((1, 2 * fc * steps), f32)] + shapes,
        input_output_aliases={10 + k: 2 + k for k in range(len(specs))} if extra else {},
        compiler_params=params(60),
        cost_estimate=cost(12 * n * w * fc * steps, n * w * 10 + fc * steps * w * 16 + n * fc * steps * 4),
        name="ff_bwd",
    )(core, n2, gr, w1, w1, slope, slope, w2, w2, *extra)
    return (res[0], *res[2:]), res[1]


def back_kernel(
    core_ref, mid_ref, acc_ref, gn_ref, cot_ref, tw_ref, gr_ref, a_ref, wo_ref, g_ref, b2_ref, *rest, m, count, order
):
    out_ref, gm_ref, ga_ref, vec_ref = rest[-5 - count : -1 - count]
    dwo_refs, dwo_ref = rest[-1 - count : -1], rest[-1]
    mid = mid_ref[...]
    out_ref[...] = (mid + acc_ref[...] + line(b2_ref)).astype(bf16)
    std, inv = row_stats(mid)
    gn = gn_ref[...]
    gm = cot_ref[...].astype(f32) * tw_ref[...] + norm_back(gn, std, inv, line(g_ref))
    gm_ref[...] = gm
    gb = gm.astype(bf16)
    ga_ref[...] = mm(gb, wo_ref[...], NT).astype(bf16)
    dwo = mm(gb, a_ref[...], TN)
    add = lambda x: jnp.sum(x, axis=0, keepdims=True)
    vec = jnp.concatenate([add(gb.astype(f32)), add(gn * std), add(gn), add(gr_ref[...].astype(f32))], axis=0)
    step = pl.program_id(0)

    @pl.when(step == 0)
    def _():
        dwo_ref[...] = dwo
        vec_ref[...] = vec

    @pl.when(step > 0)
    def _():
        dwo_ref[...] += dwo
        vec_ref[...] += vec

    @pl.when(step == pl.num_programs(0) - 1)
    def _():
        put(dwo_ref[...], dwo_refs, core_ref[0], m, order)


def grad_outs(rows, cols, m):
    if can_split(rows, m):
        shape = (rows // (2 * m), m, cols)
        return [whole(shape)] * 2, [jax.ShapeDtypeStruct(shape, f32)] * 2
    return [whole((rows, cols))], [jax.ShapeDtypeStruct((rows, cols), f32)]


def back_part(core, dp, mid, acc, gn, cot, tw, gr, att, wo, g, b2, rb):
    n, w = mid.shape
    row = lambda cols: pl.BlockSpec((rb, cols), lambda i: (i, 0))
    mo, mj = w // dp, 3 * w // dp
    if can_split(w, mo) and can_split(3 * w, mj):
        specs = [pl.BlockSpec((dp // 2, mo, w), lambda i: (0, mj // mo, 0))] * 2
        shapes = [jax.ShapeDtypeStruct((dp // 2, mj + mo, w), f32)] * 2
    else:
        specs, shapes = [whole((w, w))], [jax.ShapeDtypeStruct((w, w), f32)]
    res = pl.pallas_call(
        functools.partial(back_kernel, m=mo, count=len(specs), order=ring_order(dp)),
        grid=(n // rb,),
        in_specs=[SMEM1, row(w), row(w), row(w), row(w), row(1), row(w), row(w), whole(wo.shape), whole((w,)), whole((w,))],
        out_specs=[row(w), row(w), row(w), whole((4, w))] + specs,
        out_shape=[
            jax.ShapeDtypeStruct((n, w), bf16),
            jax.ShapeDtypeStruct((n, w), f32),
            jax.ShapeDtypeStruct((n, w), bf16),
            jax.ShapeDtypeStruct((4, w), f32),
        ]
        + shapes,
        scratch_shapes=[pltpu.VMEM((w, w), f32)],
        compiler_params=params(),
        cost_estimate=cost(4 * n * w * w, n * w * 28),
        name="back_part",
    )(core, mid, acc, gn, cot, tw, gr, att, wo, g, b2)
    return res[0], res[1], res[2], res[3], res[4:]


def joint_grad_kernel(core_ref, gp_ref, n1_ref, *rest, m, count, order):
    refs, gpt_ref = rest[-1 - count : -1], rest[-1]
    parts, n, w = gp_ref.shape

    @pl.when(pl.program_id(0) == 0)
    def _():
        for p in range(parts):
            gpt_ref[p * w : (p + 1) * w, :] = gp_ref[p].T

    put(mm(gpt_ref[...], n1_ref[...]), refs, core_ref[0], m, order)


def grad_block(rows, cols, cb, m):
    if can_split(rows, m):
        spec = pl.BlockSpec((rows // (2 * m), m, cb), lambda j: (0, 0, j))
        return [spec] * 2, [jax.ShapeDtypeStruct((rows // (2 * m), m, cols), f32)] * 2
    return [pl.BlockSpec((rows, cb), lambda j: (0, j))], [jax.ShapeDtypeStruct((rows, cols), f32)]


def joint_grad(core, dp, gp, n1, into, cb=256):
    parts, n, w = gp.shape
    m = parts * w // dp
    specs, shapes = grad_block(parts * w, w, cb, m)
    if len(into) == 2:
        shapes = [jax.ShapeDtypeStruct(x.shape, f32) for x in into]
    else:
        into = []
    return pl.pallas_call(
        functools.partial(joint_grad_kernel, m=m, count=len(specs), order=ring_order(dp)),
        grid=(w // cb,),
        in_specs=[SMEM1, whole((parts, n, w)), pl.BlockSpec((n, cb), lambda j: (0, j))]
        + [pl.BlockSpec(memory_space=pl.ANY)] * len(into),
        out_specs=specs,
        out_shape=shapes,
        input_output_aliases={3 + k: k for k in range(len(into))},
        scratch_shapes=[pltpu.VMEM((parts * w, n), bf16)],
        compiler_params=params(),
        cost_estimate=cost(2 * parts * n * w * w, n * w * 8 + parts * w * w * 4),
        name="joint_grad",
    )(core, gp, n1, *into)


def tail_kernel(gp_ref, hid_ref, gm_ref, wj_ref, g_ref, gh_ref, vec_ref):
    w = hid_ref.shape[1]
    gn = mm(gp_ref[0], wj_ref[:, :w], NT) + mm(gp_ref[1], wj_ref[:, w : 2 * w], NT) + mm(gp_ref[2], wj_ref[:, 2 * w :], NT)
    std, inv = row_stats(hid_ref[...])
    gh = (gm_ref[...] + norm_back(gn, std, inv, line(g_ref))).astype(bf16)
    gh_ref[...] = gh
    add = lambda x: jnp.sum(x, axis=0, keepdims=True)
    vec = jnp.concatenate([add(gn * std), add(gn), add(gh.astype(f32)), jnp.zeros((1, w), f32)], axis=0)
    step = pl.program_id(0)

    @pl.when(step == 0)
    def _():
        vec_ref[...] = vec

    @pl.when(step > 0)
    def _():
        vec_ref[...] += vec


def tail_part(gp, hid, gm, wj, g, rb):
    n, w = hid.shape
    row = lambda cols: pl.BlockSpec((rb, cols), lambda i: (i, 0))
    return pl.pallas_call(
        tail_kernel,
        grid=(n // rb,),
        in_specs=[pl.BlockSpec((3, rb, w), lambda i: (0, i, 0)), row(w), row(w), whole(wj.shape), whole((w,))],
        out_specs=[row(w), whole((4, w))],
        out_shape=[jax.ShapeDtypeStruct((n, w), bf16), jax.ShapeDtypeStruct((4, w), f32)],
        compiler_params=params(),
        cost_estimate=cost(6 * n * w * w, n * w * 16),
        name="tail_part",
    )(gp, hid, gm, wj, g)


def skip_grad_kernel(core_ref, gh_ref, x_ref, s_ref, vec_ref, *refs, m, order):
    ght = gh_ref[...].T
    val = jnp.concatenate([mm(ght, x_ref[...]), mm(ght, s_ref[...]), vec_ref[...]], axis=1)
    put(val, refs, core_ref[0], m, order)


def skip_grad(core, dp, gh, x, s, vec):
    n, w = gh.shape
    m = w // dp
    cols = 2 * w + vec.shape[1]
    specs, shapes = grad_block(w, cols, cols, m)
    return pl.pallas_call(
        functools.partial(skip_grad_kernel, m=m, order=ring_order(dp)),
        grid=(1,),
        in_specs=[SMEM1, whole((n, w)), whole((n, w)), whole((n, w)), whole(vec.shape)],
        out_specs=specs,
        out_shape=shapes,
        compiler_params=params(),
        cost_estimate=cost(4 * n * w * w, n * w * 6 + w * w * 8),
        name="skip_grad",
    )(core, gh, x, s, vec)


def in_grad_kernel(gh_ref, ws_ref, a_ref, b_ref):
    w = a_ref.shape[1]
    gh = gh_ref[...]
    a_ref[...] = mm(gh, ws_ref[:w, :], NT).astype(bf16)
    b_ref[...] = mm(gh, ws_ref[w:, :], NT).astype(bf16)


def in_grad(gh, ws, rb):
    n, w = gh.shape
    row = lambda cols: pl.BlockSpec((rb, cols), lambda i: (i, 0))
    return pl.pallas_call(
        in_grad_kernel,
        grid=(n // rb,),
        in_specs=[row(w), whole(ws.shape)],
        out_specs=[row(w), row(w)],
        out_shape=[jax.ShapeDtypeStruct((n, w), bf16)] * 2,
        compiler_params=params(),
        cost_estimate=cost(4 * n * w * w, n * w * 10),
        name="in_grad",
    )(gh, ws)


def pick(x, axis, index):
    return lax.dynamic_index_in_dim(x, index, axis, keepdims=False)


def swap(x, axis, bit=0):
    size = lax.axis_size(axis)
    return lax.ppermute(x, axis, [(i, i ^ (1 << bit)) for i in range(size)])


def pair_terms(refs, cols, dp):
    if len(refs) == 1:
        full = refs[0].reshape(dp // 2, 2, -1, cols)
        core = lax.axis_index("dp") & 1
        refs = [pick(full, 1, core), pick(full, 1, 1 - core)]
    return [refs[0], swap(refs[1], "dp")]


def both_sides(x, side):
    other = swap(x, "rep")
    return jnp.concatenate([jnp.where(side == 0, x, other), jnp.where(side == 0, other, x)], axis=0)


def tie(x, y):
    return lax.optimization_barrier((x, y))


def per_device(*args):
    (inputs, skips, cot, lengths, keep, group_ids, group_counts, ws, bs, g1, s1, wj, wo, bo, g2, s2, w1, b1, w2, b2) = args
    n, w = inputs.shape
    ff = w1.shape[1]
    dp = lax.axis_size("dp")
    tokens_total = n * dp * lax.axis_size("rep")
    scale = float(tokens_total) ** -0.5
    side = lax.axis_index("rep")
    core = (lax.axis_index("dp") & 1).astype(jnp.int32).reshape(1)
    rb = n // 3
    ring = ring_order(dp)
    groups = [[2 * i + c for i in ring] for c in range(2)]
    ring_sum = lambda h: lax.psum_scatter(h, "dp", scatter_dimension=0, tiled=True, axis_index_groups=groups)[0]
    over_rep = lambda h: h + swap(h, "rep")

    hid, n1, packed, qf, kf, tw = front(
        lengths, group_ids, group_counts, keep, inputs, skips, ws, bs, g1, s1, wj, rb, tokens_total // group_counts.shape[0]
    )
    att, feat = attn_fwd(packed, qf, kf)
    mid, n2, gr, grt = mid_part(att, hid, cot, tw, wo, bo, g2, s2, rb)

    acc, slope, d2 = ff_fwd(core, dp, n2, grt, w1, b1, w2, 0, ff // 1024, None)
    half2 = sum(pair_terms(d2, ff, dp))
    carry, db0 = ff_bwd(core, dp, n2, gr, w1, slope, w2, 0, 1, None)
    carry, half2 = tie(carry, half2)
    carry, db1 = ff_bwd(core, dp, n2, gr, w1, slope, w2, 1, None, carry)
    gn2, d1 = carry[0], carry[1:]
    outcome, gm, gatt, vec2, do = back_part(core, dp, mid, acc, gn2, cot, tw, gr, att, wo, g2, b2, rb)
    half1 = sum(pair_terms(d1, w, dp))
    gatt, half1 = tie(gatt, half1)
    sum2 = ring_sum(half2)
    sum1 = ring_sum(half1)

    pairs = w // PAIR
    gp = attn_bwd(packed, att, gatt, feat, kf, 0, 2, None)
    gp, sum2 = tie(gp, sum2)
    gp = attn_bwd(packed, att, gatt, feat, kf, 2, pairs - 2, gp)

    dj = joint_grad(core, dp, gp, n1, do)
    gp, dj = tie(gp, dj)
    if len(dj) == 2:
        halfj = sum(pair_terms(dj, w, dp))
    else:
        full = jnp.concatenate([dj[0].reshape(dp, 3 * w // dp, w), do[0].reshape(dp, w // dp, w)], axis=1)
        halfj = sum(pair_terms([full.reshape(-1, w)], w, dp))
    gh, vec1 = tail_part(gp, hid, gm, wj, g1, rb)
    gh, halfj, sum1 = lax.optimization_barrier((gh, halfj, sum1))
    sumj = ring_sum(halfj)
    db = jnp.concatenate([db0, db1], axis=1).reshape(8, ff // 8)
    if len(d1) == 2:
        db = jnp.stack([db[ring.index(i)] for i in range(8)])
    db = db.reshape(w, ff // w)
    vec = jnp.concatenate([vec1.T, vec2.T, db, jnp.zeros((w, PAIR - 8 - ff // w), f32)], axis=1)
    cols = 2 * w + PAIR
    ds = skip_grad(core, dp, gh, inputs, skips, vec)
    ds, sum2 = tie(ds, sum2)
    got2 = swap(sum2, "rep")
    terms = [t.reshape(dp // 2, 2, -1, cols) for t in pair_terms(ds, cols, dp)]
    send = sum(pick(t, 1, 1 - side) for t in terms)
    gh, send = tie(gh, send)
    igrad, sgrad = in_grad(gh, ws, rb)
    halfs = sum(pick(t, 1, side) for t in terms) + swap(send, "rep")
    halfs, sumj, sum1, got2, igrad, sgrad = lax.optimization_barrier((halfs, sumj, sum1, got2, igrad, sgrad))
    sums = ring_sum(halfs)
    out2 = sum2 + got2
    out1 = over_rep(sum1)
    outj = over_rep(sumj)
    outj, outo = outj[: 3 * w // dp], outj[3 * w // dp :]
    outs = both_sides(sums, side)

    ds, dj, do, d1, d2 = [m.T * scale for m in (outs[:, : 2 * w], outj, outo, out1, out2)]
    v = outs[:, 2 * w :] * scale
    col = lambda i: v[:, i]
    db1 = v[:, 8 : 8 + ff // w].reshape(-1)
    return (
        outcome, igrad, sgrad, ds, col(2), col(0), col(1), dj, do, col(4), col(5), col(6), d1, db1, d2, col(7),
    )


def solution(mesh):
    both = ("dp", "rep")
    in_specs = (P(both, None),) * 3 + (P(both),) * 3 + (P(),) * 14
    cols = P(None, "dp")
    vec = P("dp")
    out_specs = (P(both, None),) * 3 + (cols, vec, vec, vec, cols, cols, vec, vec, vec, cols, vec, cols, vec)
    return jax.shard_map(per_device, mesh=mesh, in_specs=in_specs, out_specs=out_specs, check_vma=False)
```

```python
import functools

import jax
import jax.numpy as jnp
from jax import lax
from jax.experimental import pallas as pl
from jax.experimental.pallas import tpu as pltpu
from jax.sharding import PartitionSpec as P

HEAD_DIM = 64
PAIR = 2 * HEAD_DIM
EPS = 1e-05
BIG = 1e30
ITEM_ROWS = 1028
f32 = jnp.float32
bf16 = jnp.bfloat16
NT = (((1,), (1,)), ((), ()))
NN = (((1,), (0,)), ((), ()))
TN = (((0,), (0,)), ((), ()))


def mm(a, b, dims=NN):
    return lax.dot_general(a, b, dims, preferred_element_type=f32)


def params(mb=56):
    return pltpu.CompilerParams(vmem_limit_bytes=mb << 20)


def cost(flops, nbytes, trans=0):
    return pl.CostEstimate(flops=int(flops), bytes_accessed=int(nbytes), transcendentals=int(trans))


def whole(shape):
    return pl.BlockSpec(shape, lambda *_: (0,) * len(shape), pipeline_mode=pl.Buffered(1))


def row_stats(x):
    mean = jnp.mean(x, axis=1, keepdims=True)
    cen = x - mean
    inv = lax.rsqrt(jnp.mean(cen * cen, axis=1, keepdims=True) + EPS)
    return cen * inv, inv


def norm_back(g, std, inv, gain):
    e = g * gain
    return inv * (e - jnp.mean(e, axis=1, keepdims=True) - std * jnp.mean(e * std, axis=1, keepdims=True))


def can_split(rows, m):
    return m % 8 == 0 and rows % (2 * m) == 0


def ring_order(dp):
    if dp != 16:
        return list(range(dp // 2))
    return [2 * z for z in range(4)] + [2 * z + 1 for z in reversed(range(4))]


def split_store(val, refs, core, m, order=None):
    rows, cols = val.shape
    parts = val.reshape(rows // (2 * m), 2, m, cols)
    low, high = parts[:, 0], parts[:, 1]
    keep = jnp.where(core == 0, low, high)
    send = jnp.where(core == 0, high, low)
    if order is None:
        refs[0][...] = keep
        refs[1][...] = send
    else:
        for place, owner in enumerate(order):
            refs[0][place] = keep[owner]
            refs[1][place] = send[owner]


def put(val, refs, core, m, order=None):
    if len(refs) == 2:
        split_store(val, refs, core, m, order)
    else:
        refs[0][...] = val


SMEM1 = pl.BlockSpec(memory_space=pltpu.SMEM)


def eye_mask(t):
    return lax.broadcasted_iota(jnp.int32, (t, t), 0) == lax.broadcasted_iota(jnp.int32, (t, t), 1)


def line(ref):
    return ref[...].astype(f32).reshape(1, -1)


def front_kernel(
    len_ref, gid_ref, cnt_ref, keep_ref, x_ref, s_ref, ws_ref, bs_ref, g_ref, b_ref, wj_ref,
    hid_ref, n1_ref, q_ref, qf_ref, kf_ref, tw_ref, *, group_tokens, sub,
):
    rb, w = x_ref.shape

    def project(r):
        return mm(x_ref[r, :], ws_ref[:w, :]) + mm(s_ref[r, :], ws_ref[w:, :]) + line(bs_ref)

    parts = [slice(lo, lo + sub) for lo in range(0, rb, sub)]
    ahead = project(parts[0])
    for i, r in enumerate(parts):
        hid = ahead
        if i + 1 < len(parts):
            ahead = project(parts[i + 1])
        hid_ref[r, :] = hid
        std, _ = row_stats(hid)
        n1 = (std * line(g_ref) + line(b_ref)).astype(bf16)
        n1_ref[r, :] = n1
        q_ref[r, :] = mm(n1, wj_ref[...]).astype(bf16)

    slots = len_ref.shape[0]
    base = pl.program_id(0) * rb
    lane = lax.broadcasted_iota(jnp.int32, (1, PAIR), 1)
    pos = lax.broadcasted_iota(jnp.int32, (rb, 1), 0) + base
    segment = jnp.zeros((rb, 1), jnp.int32)
    count = jnp.ones((1, PAIR), f32)
    end = 0
    for i in range(slots):
        end = end + len_ref[i]
        segment = segment + (pos >= end).astype(jnp.int32)
        count = jnp.where(lane == i, cnt_ref[gid_ref[i]].astype(f32), count)
    same = segment == lane
    weight = jnp.where(lane < slots, group_tokens / count, 0.0)
    tw_ref[...] = jnp.sum(jnp.where(same, weight, 0.0), axis=1, keepdims=True)
    qf_ref[...] = jnp.where(same, 1.0, 0.0).astype(bf16)
    eye = eye_mask(PAIR)
    for t in range(rb // PAIR):
        rows = slice(t * PAIR, (t + 1) * PAIR)
        keep = keep_ref[pl.ds(pl.multiple_of(base + t * PAIR, PAIR), PAIR)].astype(f32).reshape(1, PAIR)
        kept = jnp.sum(jnp.where(eye, keep, 0.0), axis=1, keepdims=True) == 1.0
        bias = jnp.where(same[rows] & kept, 0.0, -BIG)
        kf_ref[rows, :] = jnp.where(lane <= slots, bias, jnp.where(lane < slots + 4, 1.0, 0.0)).astype(bf16)


def front(lengths, gids, counts, keep, x, s, ws, bs, g, b, wj, rb, group_tokens, sub=192):
    n, w = x.shape
    c = wj.shape[1]
    row = lambda cols: pl.BlockSpec((rb, cols), lambda i: (i, 0))
    return pl.pallas_call(
        functools.partial(front_kernel, group_tokens=float(group_tokens), sub=sub),
        grid=(n // rb,),
        in_specs=[SMEM1, SMEM1, SMEM1, whole((n,)), row(w), row(w), whole(ws.shape), whole((w,)), whole((w,)), whole((w,)), whole(wj.shape)],
        out_specs=[row(w), row(w), row(c), row(PAIR), row(PAIR), row(1)],
        out_shape=[
            jax.ShapeDtypeStruct((n, w), f32),
            jax.ShapeDtypeStruct((n, w), bf16),
            jax.ShapeDtypeStruct((n, c), bf16),
            jax.ShapeDtypeStruct((n, PAIR), bf16),
            jax.ShapeDtypeStruct((n, PAIR), bf16),
            jax.ShapeDtypeStruct((n, 1), f32),
        ],
        compiler_params=params(),
        cost_estimate=cost(2 * n * w * (2 * w + c), n * w * 20 + 5 * w * w * 2),
        name="front",
    )(lengths, gids, counts, keep, x, s, ws, bs, g, b, wj)


def half_mask(h):
    lane = lax.broadcasted_iota(jnp.int32, (1, PAIR), 1)
    return (lane < HEAD_DIM) if h == 0 else (lane >= HEAD_DIM)


def pieces(x):
    a = x.astype(bf16)
    r = x - a.astype(f32)
    b = r.astype(bf16)
    c = (r - b.astype(f32)).astype(bf16)
    return a, b, c


def attn_fwd_kernel(
    q_ref, k_ref, v_ref, qf_ref, kf_ref, cot_ref, tw_ref, o_ref, feat_ref, gr_ref, grt_ref, gsum_ref, ka_ref, vm_ref, s_ref, *, tq, per
):
    n = q_ref.shape[0]
    none = jnp.zeros((1, PAIR), bf16)
    one = jnp.ones((1, PAIR), bf16)
    lane = lax.broadcasted_iota(jnp.int32, (1, PAIR), 1)
    spare = [HEAD_DIM, 0]
    cols = [slice(d * PAIR, (d + 1) * PAIR) for d in range(per)]
    for d in range(per):
        ka_ref[d, :, :PAIR] = k_ref[:, cols[d]]
        ka_ref[d, :, PAIR:] = kf_ref[...]
        for h in range(2):
            vm_ref[d, h] = jnp.where(half_mask(h), v_ref[:, cols[d]], jnp.where(lane == spare[h], one, none))
    eye = eye_mask(PAIR)
    units = [(d, i, h) for d in range(per) for i in range(n // tq) for h in range(2)]

    def scores(u):
        d, i, h = units[u]
        rows = slice(i * tq, (i + 1) * tq)
        qm = jnp.where(half_mask(h), q_ref[rows, cols[d]] * jnp.asarray(HEAD_DIM**-0.5, bf16), none)
        slot = u % 2
        s_ref[slot] = mm(jnp.concatenate([qm, qf_ref[rows, :]], axis=1), ka_ref[d], NT)
        for j in range(tq // PAIR):
            a = slice(j * PAIR, (j + 1) * PAIR)
            c = slice(i * tq + j * PAIR, i * tq + (j + 1) * PAIR)
            s_ref[slot, a, c] = jnp.where(eye, mm(qm[a], k_ref[c, cols[d]], NT), s_ref[slot, a, c])

    scores(0)
    outs = [None, None]
    gsum = [None] * per
    for u, (d, i, h) in enumerate(units):
        if u + 1 < len(units):
            scores(u + 1)
        rows = slice(i * tq, (i + 1) * tq)
        s = s_ref[u % 2]
        top = jnp.max(s, axis=1, keepdims=True)
        pv = mm(jnp.exp(s - top).astype(bf16), vm_ref[d, h])
        total = pv[:, spare[h] : spare[h] + 1]
        outs[h] = pv / total
        a, b, c = pieces(-(top + jnp.log(total)))
        feat_ref[2 * d + h, rows, :] = jnp.where(
            lane == 5, a, jnp.where(lane == 6, b, jnp.where(lane == 7, c, qf_ref[rows, :]))
        )
        if h == 0:
            gr = (cot_ref[rows, cols[d]].astype(f32) * tw_ref[rows, :]).astype(bf16)
            gr_ref[rows, cols[d]] = gr
            grt_ref[cols[d], rows] = gr.T
            part = jnp.sum(gr.astype(f32), axis=0, keepdims=True)
            gsum[d] = part if i == 0 else gsum[d] + part
        else:
            o_ref[rows, cols[d]] = jnp.where(lane < HEAD_DIM, outs[0], outs[1]).astype(bf16)
    for d in range(per):
        gsum_ref[:, cols[d]] = gsum[d]


def attn_fwd(packed, qf, kf, cot, tw, tq=384, per=1):
    n, c = packed.shape
    w = c // 3
    pairs = w // PAIR
    wide = per * PAIR
    part = lambda p: pl.BlockSpec((n, wide), lambda j: (0, p * (pairs // per) + j))
    return pl.pallas_call(
        functools.partial(attn_fwd_kernel, tq=tq, per=per),
        grid=(pairs // per,),
        in_specs=[part(0), part(1), part(2), whole((n, PAIR)), whole((n, PAIR)), part(0), whole((n, 1))],
        out_specs=[
            pl.BlockSpec((n, wide), lambda j: (0, j)),
            pl.BlockSpec((2 * per, n, PAIR), lambda j: (j, 0, 0)),
            pl.BlockSpec((n, wide), lambda j: (0, j)),
            pl.BlockSpec((wide, n), lambda j: (j, 0)),
            pl.BlockSpec((1, wide), lambda j: (0, j)),
        ],
        out_shape=[
            jax.ShapeDtypeStruct((n, w), bf16),
            jax.ShapeDtypeStruct((2 * pairs, n, PAIR), bf16),
            jax.ShapeDtypeStruct((n, w), bf16),
            jax.ShapeDtypeStruct((w, n), bf16),
            jax.ShapeDtypeStruct((1, w), f32),
        ],
        scratch_shapes=[
            pltpu.VMEM((per, n, 2 * PAIR), bf16),
            pltpu.VMEM((per, 2, n, PAIR), bf16),
            pltpu.VMEM((2, tq, n), f32),
        ],
        compiler_params=params(),
        cost_estimate=cost(2 * n * n * (4 * PAIR) * pairs * 2, n * c * 4, n * n * 2 * pairs),
        name="attn_fwd",
    )(packed, packed, packed, qf, kf, cot, tw)


def attn_bwd_kernel(
    q_ref, k_ref, v_ref, o_ref, g_ref, feat_ref, kf_ref, out_ref, ka_ref, va_ref, qa_ref, ga_ref, kt_ref, dq_ref, st_ref, dp_ref,
    *, tk, live, per,
):
    n = q_ref.shape[0]
    lane = lax.broadcasted_iota(jnp.int32, (1, PAIR), 1)
    none = jnp.zeros((1, PAIR), bf16)
    scale = HEAD_DIM**-0.5
    cols = [slice(d * PAIR, (d + 1) * PAIR) for d in range(per)]

    def prepare(d):
        ka_ref[d, :, :PAIR] = k_ref[:, cols[d]]
        ka_ref[d, :, PAIR:] = kf_ref[...]
        va_ref[d, :, :PAIR] = v_ref[:, cols[d]]
        va_ref[d, :, PAIR:] = jnp.broadcast_to(jnp.where(lane < 3, 1.0, 0.0).astype(bf16), (n, PAIR))
        kt_ref[d] = k_ref[:, cols[d]].T
        q = q_ref[:, cols[d]] * jnp.asarray(scale, bf16)
        g = g_ref[:, cols[d]]
        prod = g.astype(f32) * o_ref[:, cols[d]].astype(f32)
        for h in range(2):
            own = half_mask(h)
            delta = jnp.sum(jnp.where(own, prod, 0.0), axis=1, keepdims=True)
            a, b, c = pieces(-delta)
            qa_ref[d, h, :, :PAIR] = jnp.where(own, q, none)
            qa_ref[d, h, :, PAIR:] = feat_ref[2 * d + h]
            ga_ref[d, h, :, :PAIR] = jnp.where(own, g, none)
            ga_ref[d, h, :, PAIR:] = jnp.where(lane == 0, a, jnp.where(lane == 1, b, jnp.where(lane == 2, c, none)))

    eye = eye_mask(PAIR)
    spans = [(i, min(i + tk, live)) for i in range(0, live, tk)]
    units = [(d, span, h) for d in range(per) for span in spans for h in range(2)]

    def scores(u):
        d, (lo, hi), h = units[u]
        size = hi - lo
        slot = u % 2
        st_ref[slot, :size] = mm(ka_ref[d, lo:hi, :], qa_ref[d, h], NT)
        for j in range(0, size, PAIR):
            t = min(PAIR, size - j)
            a = slice(j, j + t)
            r = slice(lo + j, lo + j + t)
            c = slice(lo + j, lo + j + PAIR)
            plain = jnp.concatenate([k_ref[r, cols[d]], jnp.where(lane < 5, none, kf_ref[r, :])], axis=1)
            st_ref[slot, a, c] = jnp.where(eye[:t], mm(plain, qa_ref[d, h, c, :], NT), st_ref[slot, a, c])
        dp_ref[slot, :size] = mm(va_ref[d, lo:hi, :], ga_ref[d, h], NT)

    prepare(0)
    scores(0)
    dv = [None, None]
    dk = [None, None]
    for u, (d, (lo, hi), h) in enumerate(units):
        if (lo, h) == (0, 0) and d + 1 < per:
            prepare(d + 1)
        if u + 1 < len(units):
            scores(u + 1)
        rows = slice(lo, hi)
        own = slice(h * HEAD_DIM, (h + 1) * HEAD_DIM)
        p = jnp.exp(st_ref[u % 2, : hi - lo])
        ds = (p * dp_ref[u % 2, : hi - lo]).astype(bf16)
        part = mm(kt_ref[d, own, rows], ds)
        if lo == 0:
            dq_ref[d, own, :] = part
        else:
            dq_ref[d, own, :] += part
        dv[h] = mm(p.astype(bf16), ga_ref[d, h, :, :PAIR])
        dk[h] = mm(ds, qa_ref[d, h, :, :PAIR])
        if h == 1:
            out_ref[1, rows, cols[d]] = (dk[0] + dk[1]).astype(bf16)
            out_ref[2, rows, cols[d]] = (dv[0] + dv[1]).astype(bf16)
            if hi == live:
                out_ref[0, :, cols[d]] = (dq_ref[d].T * scale).astype(bf16)
    if live < n:
        out_ref[1, live:, :] = jnp.zeros((n - live, per * PAIR), bf16)
        out_ref[2, live:, :] = jnp.zeros((n - live, per * PAIR), bf16)


def attn_bwd(packed, att, grad, feat, kf, tk=384, per=1):
    n, c = packed.shape
    w = c // 3
    pairs = w // PAIR
    wide = per * PAIR
    part = lambda p: pl.BlockSpec((n, wide), lambda j: (0, p * (pairs // per) + j))
    live = min(n, -(-ITEM_ROWS // 16) * 16)
    return pl.pallas_call(
        functools.partial(attn_bwd_kernel, tk=tk, live=live, per=per),
        grid=(pairs // per,),
        in_specs=[
            part(0),
            part(1),
            part(2),
            part(0),
            part(0),
            pl.BlockSpec((2 * per, n, PAIR), lambda j: (j, 0, 0)),
            whole((n, PAIR)),
        ],
        out_specs=pl.BlockSpec((3, n, wide), lambda j: (0, 0, j)),
        out_shape=jax.ShapeDtypeStruct((3, n, w), bf16),
        scratch_shapes=[
            pltpu.VMEM((per, n, 2 * PAIR), bf16),
            pltpu.VMEM((per, n, 2 * PAIR), bf16),
            pltpu.VMEM((per, 2, n, 2 * PAIR), bf16),
            pltpu.VMEM((per, 2, n, 2 * PAIR), bf16),
            pltpu.VMEM((per, PAIR, n), bf16),
            pltpu.VMEM((per, PAIR, n), f32),
            pltpu.VMEM((2, tk, n), f32),
            pltpu.VMEM((2, tk, n), f32),
        ],
        compiler_params=params(),
        cost_estimate=cost(2 * n * n * (9 * PAIR) * pairs * 2, n * c * 8, n * n * 2 * pairs),
        name="attn_bwd",
    )(packed, packed, packed, att, grad, feat, kf)


def mid_kernel(a_ref, hid_ref, wo_ref, bo_ref, g_ref, b_ref, mid_ref, n2_ref):
    mid = hid_ref[...] + mm(a_ref[...], wo_ref[...]) + line(bo_ref)
    mid_ref[...] = mid
    std, _ = row_stats(mid)
    n2_ref[...] = (std * line(g_ref) + line(b_ref)).astype(bf16)


def mid_part(att, hid, wo, bo, g, b, rb):
    n, w = att.shape
    row = lambda cols: pl.BlockSpec((rb, cols), lambda i: (i, 0))
    return pl.pallas_call(
        mid_kernel,
        grid=(n // rb,),
        in_specs=[row(w), row(w), whole(wo.shape), whole((w,)), whole((w,)), whole((w,))],
        out_specs=[row(w), row(w)],
        out_shape=[jax.ShapeDtypeStruct((n, w), f32), jax.ShapeDtypeStruct((n, w), bf16)],
        compiler_params=params(),
        cost_estimate=cost(2 * n * w * w, n * w * 12),
        name="mid_part",
    )(att, hid, wo, bo, g, b)


def normal_cdf_pdf(u):
    a = jnp.abs(u)
    t = 1.0 / (1.0 + a * (0.3275911 * 0.7071067811865476))
    e = jnp.exp(-0.5 * u * u)
    half = 0.5
    poly = t * (
        half * 0.254829592
        + t * (half * -0.284496736 + t * (half * 1.421413741 + t * (half * -1.453152027 + t * (half * 1.061405429))))
    )
    tail = poly * e
    return jnp.where(u < 0, tail, 1.0 - tail), e * 0.3989422804014327


def ff_fwd_kernel(core_ref, n2_ref, grt_ref, w1_ref, b1_ref, w2_ref, *rest, m, order, sub, count):
    acc_ref, slope_ref = rest[-2 - count : -count]
    refs = rest[-count:]
    fc = w1_ref.shape[1]
    bias = line(b1_ref)
    cut = lambda s: slice(s * sub, (s + 1) * sub)

    @pl.when(pl.program_id(0) == 0)
    def _():
        acc_ref[...] = jnp.zeros_like(acc_ref)

    before = lambda s: mm(n2_ref[...], w1_ref[:, cut(s)]) + bias[:, cut(s)]
    ahead = before(0)
    for s in range(fc // sub):
        pre = ahead
        if s + 1 < fc // sub:
            ahead = before(s + 1)
        cdf, pdf = normal_cdf_pdf(pre)
        act = (pre * cdf).astype(bf16)
        slope_ref[:, cut(s)] = (cdf + pre * pdf).astype(bf16)
        acc_ref[...] += mm(act, w2_ref[cut(s), :])
        views = [r.at[:, :, cut(s)] if count == 2 else r.at[:, cut(s)] for r in refs]
        put(mm(grt_ref[...], act), views, core_ref[0], m, order)


def ff_fwd(core, dp, n2, grt, w1, b1, w2, base, steps, slope, fc=1024, sub=256):
    n, w = n2.shape
    ff = w1.shape[1]
    mine = steps * fc
    m = w // dp
    if can_split(w, m):
        specs = [pl.BlockSpec((dp // 2, m, fc), lambda i: (0, 0, i))] * 2
        shapes = [jax.ShapeDtypeStruct((dp // 2, m, mine), f32)] * 2
    else:
        specs = [pl.BlockSpec((w, fc), lambda i: (0, i))]
        shapes = [jax.ShapeDtypeStruct((w, mine), f32)]
    extra = [] if slope is None else [slope]
    res = pl.pallas_call(
        functools.partial(ff_fwd_kernel, m=m, order=ring_order(dp), sub=sub, count=len(specs)),
        grid=(steps,),
        in_specs=[
            SMEM1,
            whole((n, w)),
            whole((w, n)),
            pl.BlockSpec((w, fc), lambda i: (0, base + i)),
            pl.BlockSpec((fc,), lambda i: (base + i,)),
            pl.BlockSpec((fc, w), lambda i: (base + i, 0)),
        ]
        + [pl.BlockSpec(memory_space=pl.ANY)] * len(extra),
        out_specs=[whole((n, w)), pl.BlockSpec((n, fc), lambda i: (0, base + i))] + specs,
        out_shape=[jax.ShapeDtypeStruct((n, w), f32), jax.ShapeDtypeStruct((n, ff), bf16)] + shapes,
        input_output_aliases={6: 1} if extra else {},
        compiler_params=params(60),
        cost_estimate=cost(6 * n * w * mine, n * w * 10 + mine * w * 8 + n * mine * 2, n * mine * 2),
        name="ff_fwd",
    )(core, n2, grt, w1, b1, w2, *extra)
    return res[0], res[1], res[2:]


def ff_bwd_kernel(core_ref, n2_ref, gr_ref, w1a_ref, w1b_ref, sla_ref, slb_ref, w2a_ref, w2b_ref, *rest, first, count, m):
    gn_ref, db1_ref = rest[-2 - count : -count]
    refs = rest[-count:]
    side = lambda a, b: jnp.concatenate([a[...], b[...]], axis=1)
    w1 = side(w1a_ref, w1b_ref)
    w2 = jnp.concatenate([w2a_ref[...], w2b_ref[...]], axis=0)
    gpre = (mm(gr_ref[...], w2, NT) * side(sla_ref, slb_ref).astype(f32)).astype(bf16)

    @pl.when(pl.program_id(0) == 0)
    def _():
        gn_ref[...] = jnp.zeros_like(gn_ref) if first else rest[0][...]

    gn_ref[...] += mm(gpre, w1, NT)
    put(mm(gpre, n2_ref[...], TN), refs, core_ref[0], m)
    db1_ref[...] = jnp.sum(gpre.astype(f32), axis=0, keepdims=True)


def ff_bwd(core, dp, n2, gr, w1, slope, w2, base, steps, prev):
    n, w = n2.shape
    ff = w1.shape[1]
    m = ff // dp
    fc = 384
    ring = can_split(fc, m) and fc == 2 * m and dp == 16
    total = ff // (2 * fc)
    steps = total - base if steps is None else steps
    if ring:
        near = lambda i: jnp.where(base + i < 2, 4 * (base + i), 15 - 4 * (base + i))
        far = lambda i: jnp.where(base + i < 2, 4 * (base + i) + 2, 13 - 4 * (base + i))
        specs = [pl.BlockSpec((2, m, w), lambda i: (base + i, 0, 0))] * 2
        shapes = [jax.ShapeDtypeStruct((dp // 2, m, w), f32)] * 2
    else:
        near = lambda i: 2 * (base + i)
        far = lambda i: 2 * (base + i) + 1
        specs = [pl.BlockSpec((2 * fc, w), lambda i: (base + i, 0))]
        shapes = [jax.ShapeDtypeStruct((ff, w), f32)]
    extra = [] if prev is None else list(prev)
    res = pl.pallas_call(
        functools.partial(ff_bwd_kernel, first=prev is None, count=len(specs), m=m),
        grid=(steps,),
        in_specs=[
            SMEM1,
            whole((n, w)),
            whole((n, w)),
            pl.BlockSpec((w, fc), lambda i: (0, near(i))),
            pl.BlockSpec((w, fc), lambda i: (0, far(i))),
            pl.BlockSpec((n, fc), lambda i: (0, near(i))),
            pl.BlockSpec((n, fc), lambda i: (0, far(i))),
            pl.BlockSpec((fc, w), lambda i: (near(i), 0)),
            pl.BlockSpec((fc, w), lambda i: (far(i), 0)),
        ]
        + ([whole((n, w))] + [pl.BlockSpec(memory_space=pl.ANY)] * len(specs) if extra else []),
        out_specs=[whole((n, w)), pl.BlockSpec((1, 2 * fc), lambda i: (0, i))] + specs,
        out_shape=[jax.ShapeDtypeStruct((n, w), f32), jax.ShapeDtypeStruct((1, 2 * fc * steps), f32)] + shapes,
        input_output_aliases={10 + k: 2 + k for k in range(len(specs))} if extra else {},
        compiler_params=params(60),
        cost_estimate=cost(12 * n * w * fc * steps, n * w * 10 + fc * steps * w * 16 + n * fc * steps * 4),
        name="ff_bwd",
    )(core, n2, gr, w1, w1, slope, slope, w2, w2, *extra)
    return (res[0], *res[2:]), res[1]


def back_kernel(core_ref, mid_ref, acc_ref, gn_ref, cot_ref, tw_ref, a_ref, wo_ref, g_ref, b2_ref, *rest, m, count, order, sub):
    out_ref, gm_ref, ga_ref, vec_ref = rest[-5 - count : -1 - count]
    dwo_refs, dwo_ref = rest[-1 - count : -1], rest[-1]
    rb, w = mid_ref.shape
    step = pl.program_id(0)
    add = lambda x: jnp.sum(x, axis=0, keepdims=True)
    parts = [slice(lo, lo + sub) for lo in range(0, rb, sub)]

    @pl.when(step == 0)
    def _():
        dwo_ref[...] = jnp.zeros_like(dwo_ref)
        vec_ref[...] = jnp.zeros_like(vec_ref)

    def norm_part(r):
        mid = mid_ref[r, :]
        out_ref[r, :] = (mid + acc_ref[r, :] + line(b2_ref)).astype(bf16)
        std, inv = row_stats(mid)
        gn = gn_ref[r, :]
        gm = cot_ref[r, :].astype(f32) * tw_ref[r, :] + norm_back(gn, std, inv, line(g_ref))
        gm_ref[r, :] = gm
        gb = gm.astype(bf16)
        vec_ref[...] += jnp.concatenate([add(gb.astype(f32)), add(gn * std), add(gn), jnp.zeros((1, w), f32)], axis=0)
        return gb

    ahead = norm_part(parts[0])
    for i, r in enumerate(parts):
        gb = ahead
        if i + 1 < len(parts):
            ahead = norm_part(parts[i + 1])
        ga_ref[r, :] = mm(gb, wo_ref[...], NT).astype(bf16)
        dwo_ref[...] += mm(gb, a_ref[r, :], TN)

    @pl.when(step == pl.num_programs(0) - 1)
    def _():
        put(dwo_ref[...], dwo_refs, core_ref[0], m, order)


def grad_outs(rows, cols, m):
    if can_split(rows, m):
        shape = (rows // (2 * m), m, cols)
        return [whole(shape)] * 2, [jax.ShapeDtypeStruct(shape, f32)] * 2
    return [whole((rows, cols))], [jax.ShapeDtypeStruct((rows, cols), f32)]


def back_part(core, dp, mid, acc, gn, cot, tw, att, wo, g, b2, rb, sub=384):
    n, w = mid.shape
    row = lambda cols: pl.BlockSpec((rb, cols), lambda i: (i, 0))
    mo, mj = w // dp, 3 * w // dp
    if can_split(w, mo) and can_split(3 * w, mj):
        specs = [pl.BlockSpec((dp // 2, mo, w), lambda i: (0, mj // mo, 0))] * 2
        shapes = [jax.ShapeDtypeStruct((dp // 2, mj + mo, w), f32)] * 2
    else:
        specs, shapes = [whole((w, w))], [jax.ShapeDtypeStruct((w, w), f32)]
    res = pl.pallas_call(
        functools.partial(back_kernel, m=mo, count=len(specs), order=ring_order(dp), sub=sub),
        grid=(n // rb,),
        in_specs=[SMEM1, row(w), row(w), row(w), row(w), row(1), row(w), whole(wo.shape), whole((w,)), whole((w,))],
        out_specs=[row(w), row(w), row(w), whole((4, w))] + specs,
        out_shape=[
            jax.ShapeDtypeStruct((n, w), bf16),
            jax.ShapeDtypeStruct((n, w), f32),
            jax.ShapeDtypeStruct((n, w), bf16),
            jax.ShapeDtypeStruct((4, w), f32),
        ]
        + shapes,
        scratch_shapes=[pltpu.VMEM((w, w), f32)],
        compiler_params=params(),
        cost_estimate=cost(4 * n * w * w, n * w * 28),
        name="back_part",
    )(core, mid, acc, gn, cot, tw, att, wo, g, b2)
    return res[0], res[1], res[2], res[3], res[4:]


def joint_grad_kernel(core_ref, gp_ref, n1_ref, *rest, m, count, order):
    refs, gpt_ref = rest[-1 - count : -1], rest[-1]
    parts, n, w = gp_ref.shape

    @pl.when(pl.program_id(0) == 0)
    def _():
        for p in range(parts):
            gpt_ref[p * w : (p + 1) * w, :] = gp_ref[p].T

    put(mm(gpt_ref[...], n1_ref[...]), refs, core_ref[0], m, order)


def grad_block(rows, cols, cb, m):
    if can_split(rows, m):
        spec = pl.BlockSpec((rows // (2 * m), m, cb), lambda j: (0, 0, j))
        return [spec] * 2, [jax.ShapeDtypeStruct((rows // (2 * m), m, cols), f32)] * 2
    return [pl.BlockSpec((rows, cb), lambda j: (0, j))], [jax.ShapeDtypeStruct((rows, cols), f32)]


def joint_grad(core, dp, gp, n1, into, cb=256):
    parts, n, w = gp.shape
    m = parts * w // dp
    specs, shapes = grad_block(parts * w, w, cb, m)
    if len(into) == 2:
        shapes = [jax.ShapeDtypeStruct(x.shape, f32) for x in into]
    else:
        into = []
    return pl.pallas_call(
        functools.partial(joint_grad_kernel, m=m, count=len(specs), order=ring_order(dp)),
        grid=(w // cb,),
        in_specs=[SMEM1, whole((parts, n, w)), pl.BlockSpec((n, cb), lambda j: (0, j))]
        + [pl.BlockSpec(memory_space=pl.ANY)] * len(into),
        out_specs=specs,
        out_shape=shapes,
        input_output_aliases={3 + k: k for k in range(len(into))},
        scratch_shapes=[pltpu.VMEM((parts * w, n), bf16)],
        compiler_params=params(),
        cost_estimate=cost(2 * parts * n * w * w, n * w * 8 + parts * w * w * 4),
        name="joint_grad",
    )(core, gp, n1, *into)


def tail_kernel(gp_ref, hid_ref, gm_ref, wj_ref, g_ref, gh_ref, vec_ref, *, sub):
    rb, w = hid_ref.shape
    parts = [slice(lo, lo + sub) for lo in range(0, rb, sub)]
    add = lambda x: jnp.sum(x, axis=0, keepdims=True)

    def project(r):
        return sum(mm(gp_ref[p, r, :], wj_ref[:, p * w : (p + 1) * w], NT) for p in range(3))

    ahead = project(parts[0])
    vec = jnp.zeros((4, w), f32)
    for i, r in enumerate(parts):
        gn = ahead
        if i + 1 < len(parts):
            ahead = project(parts[i + 1])
        std, inv = row_stats(hid_ref[r, :])
        gh = (gm_ref[r, :] + norm_back(gn, std, inv, line(g_ref))).astype(bf16)
        gh_ref[r, :] = gh
        vec = vec + jnp.concatenate([add(gn * std), add(gn), add(gh.astype(f32)), jnp.zeros((1, w), f32)], axis=0)
    step = pl.program_id(0)

    @pl.when(step == 0)
    def _():
        vec_ref[...] = vec

    @pl.when(step > 0)
    def _():
        vec_ref[...] += vec


def tail_part(gp, hid, gm, wj, g, rb, sub=384):
    n, w = hid.shape
    row = lambda cols: pl.BlockSpec((rb, cols), lambda i: (i, 0))
    return pl.pallas_call(
        functools.partial(tail_kernel, sub=sub),
        grid=(n // rb,),
        in_specs=[pl.BlockSpec((3, rb, w), lambda i: (0, i, 0)), row(w), row(w), whole(wj.shape), whole((w,))],
        out_specs=[row(w), whole((4, w))],
        out_shape=[jax.ShapeDtypeStruct((n, w), bf16), jax.ShapeDtypeStruct((4, w), f32)],
        compiler_params=params(),
        cost_estimate=cost(6 * n * w * w, n * w * 16),
        name="tail_part",
    )(gp, hid, gm, wj, g)


def skip_grad_kernel(core_ref, gh_ref, x_ref, s_ref, vec_ref, *refs, m, order):
    ght = gh_ref[...].T
    val = jnp.concatenate([mm(ght, x_ref[...]), mm(ght, s_ref[...]), vec_ref[...]], axis=1)
    put(val, refs, core_ref[0], m, order)


def skip_grad(core, dp, gh, x, s, vec):
    n, w = gh.shape
    m = w // dp
    cols = 2 * w + vec.shape[1]
    specs, shapes = grad_block(w, cols, cols, m)
    return pl.pallas_call(
        functools.partial(skip_grad_kernel, m=m, order=ring_order(dp)),
        grid=(1,),
        in_specs=[SMEM1, whole((n, w)), whole((n, w)), whole((n, w)), whole(vec.shape)],
        out_specs=specs,
        out_shape=shapes,
        compiler_params=params(),
        cost_estimate=cost(4 * n * w * w, n * w * 6 + w * w * 8),
        name="skip_grad",
    )(core, gh, x, s, vec)


def in_grad_kernel(gh_ref, ws_ref, a_ref, b_ref):
    w = a_ref.shape[1]
    gh = gh_ref[...]
    a_ref[...] = mm(gh, ws_ref[:w, :], NT).astype(bf16)
    b_ref[...] = mm(gh, ws_ref[w:, :], NT).astype(bf16)


def in_grad(gh, ws, rb):
    n, w = gh.shape
    row = lambda cols: pl.BlockSpec((rb, cols), lambda i: (i, 0))
    return pl.pallas_call(
        in_grad_kernel,
        grid=(n // rb,),
        in_specs=[row(w), whole(ws.shape)],
        out_specs=[row(w), row(w)],
        out_shape=[jax.ShapeDtypeStruct((n, w), bf16)] * 2,
        compiler_params=params(),
        cost_estimate=cost(4 * n * w * w, n * w * 10),
        name="in_grad",
    )(gh, ws)


def pick(x, axis, index):
    return lax.dynamic_index_in_dim(x, index, axis, keepdims=False)


def swap(x, axis, bit=0):
    size = lax.axis_size(axis)
    return lax.ppermute(x, axis, [(i, i ^ (1 << bit)) for i in range(size)])


def pair_terms(refs, cols, dp):
    if len(refs) == 1:
        full = refs[0].reshape(dp // 2, 2, -1, cols)
        core = lax.axis_index("dp") & 1
        refs = [pick(full, 1, core), pick(full, 1, 1 - core)]
    return [refs[0], swap(refs[1], "dp")]


def both_sides(x, side):
    other = swap(x, "rep")
    return jnp.concatenate([jnp.where(side == 0, x, other), jnp.where(side == 0, other, x)], axis=0)


def tie(x, y):
    return lax.optimization_barrier((x, y))


def per_device(*args):
    (inputs, skips, cot, lengths, keep, group_ids, group_counts, ws, bs, g1, s1, wj, wo, bo, g2, s2, w1, b1, w2, b2) = args
    n, w = inputs.shape
    ff = w1.shape[1]
    dp = lax.axis_size("dp")
    tokens_total = n * dp * lax.axis_size("rep")
    scale = float(tokens_total) ** -0.5
    side = lax.axis_index("rep")
    core = (lax.axis_index("dp") & 1).astype(jnp.int32).reshape(1)
    rb = n // 3
    ring = ring_order(dp)
    groups = [[2 * i + c for i in ring] for c in range(2)]
    ring_sum = lambda h: lax.psum_scatter(h, "dp", scatter_dimension=0, tiled=True, axis_index_groups=groups)[0]
    over_rep = lambda h: h + swap(h, "rep")

    hid, n1, packed, qf, kf, tw = front(
        lengths, group_ids, group_counts, keep, inputs, skips, ws, bs, g1, s1, wj, rb, tokens_total // group_counts.shape[0]
    )
    att, feat, gr, grt, gsum = attn_fwd(packed, qf, kf, cot, tw)
    mid, n2 = mid_part(att, hid, wo, bo, g2, s2, rb)

    acc, slope, d2 = ff_fwd(core, dp, n2, grt, w1, b1, w2, 0, ff // 1024, None)
    half2 = sum(pair_terms(d2, ff, dp))
    carry, db0 = ff_bwd(core, dp, n2, gr, w1, slope, w2, 0, 1, None)
    carry, half2 = tie(carry, half2)
    carry, db1 = ff_bwd(core, dp, n2, gr, w1, slope, w2, 1, None, carry)
    gn2, d1 = carry[0], carry[1:]
    outcome, gm, gatt, vec2, do = back_part(core, dp, mid, acc, gn2, cot, tw, att, wo, g2, b2, rb)
    half1 = sum(pair_terms(d1, w, dp))
    gatt, half1 = tie(gatt, half1)
    sum2 = ring_sum(half2)
    sum1 = ring_sum(half1)

    gp = attn_bwd(packed, att, gatt, feat, kf)
    gp, sum2 = tie(gp, sum2)
    got2 = swap(sum2, "rep")

    dj = joint_grad(core, dp, gp, n1, do)
    gp, dj = tie(gp, dj)
    if len(dj) == 2:
        halfj = sum(pair_terms(dj, w, dp))
    else:
        full = jnp.concatenate([dj[0].reshape(dp, 3 * w // dp, w), do[0].reshape(dp, w // dp, w)], axis=1)
        halfj = sum(pair_terms([full.reshape(-1, w)], w, dp))
    gh, vec1 = tail_part(gp, hid, gm, wj, g1, rb)
    gh, halfj, sum1, got2 = lax.optimization_barrier((gh, halfj, sum1, got2))
    sumj = ring_sum(halfj)
    db = jnp.concatenate([db0, db1], axis=1).reshape(8, ff // 8)
    if len(d1) == 2:
        db = jnp.stack([db[ring.index(i)] for i in range(8)])
    db = db.reshape(w, ff // w)
    vec = jnp.concatenate([vec1.T, vec2[:3].T, gsum.T, db, jnp.zeros((w, PAIR - 8 - ff // w), f32)], axis=1)
    cols = 2 * w + PAIR
    ds = skip_grad(core, dp, gh, inputs, skips, vec)
    terms = [t.reshape(dp // 2, 2, -1, cols) for t in pair_terms(ds, cols, dp)]
    send = sum(pick(t, 1, 1 - side) for t in terms)
    gh, send = tie(gh, send)
    igrad, sgrad = in_grad(gh, ws, rb)
    halfs = sum(pick(t, 1, side) for t in terms) + swap(send, "rep")
    halfs, sumj, sum1, igrad, sgrad = lax.optimization_barrier((halfs, sumj, sum1, igrad, sgrad))
    sums = ring_sum(halfs)
    out2 = sum2 + got2
    out1 = over_rep(sum1)
    outj = over_rep(sumj)
    outj, outo = outj[: 3 * w // dp], outj[3 * w // dp :]
    outs = both_sides(sums, side)

    ds, dj, do, d1, d2 = [m.T * scale for m in (outs[:, : 2 * w], outj, outo, out1, out2)]
    v = outs[:, 2 * w :] * scale
    col = lambda i: v[:, i]
    db1 = v[:, 8 : 8 + ff // w].reshape(-1)
    return (
        outcome, igrad, sgrad, ds, col(2), col(0), col(1), dj, do, col(4), col(5), col(6), d1, db1, d2, col(7),
    )


def solution(mesh):
    both = ("dp", "rep")
    in_specs = (P(both, None),) * 3 + (P(both),) * 3 + (P(),) * 14
    cols = P(None, "dp")
    vec = P("dp")
    out_specs = (P(both, None),) * 3 + (cols, vec, vec, vec, cols, cols, vec, vec, vec, cols, vec, cols, vec)
    return jax.shard_map(per_device, mesh=mesh, in_specs=in_specs, out_specs=out_specs, check_vma=False)
```

```python
import functools

import jax
import jax.numpy as jnp
from jax import lax
from jax.experimental import pallas as pl
from jax.experimental.pallas import tpu as pltpu
from jax.sharding import PartitionSpec as P

HEAD_DIM = 64
PAIR = 2 * HEAD_DIM
EPS = 1e-05
BIG = 1e30
ITEM_ROWS = 1028
f32 = jnp.float32
bf16 = jnp.bfloat16
NT = (((1,), (1,)), ((), ()))
NN = (((1,), (0,)), ((), ()))
TN = (((0,), (0,)), ((), ()))


def mm(a, b, dims=NN):
    return lax.dot_general(a, b, dims, preferred_element_type=f32)


def params(mb=56):
    return pltpu.CompilerParams(vmem_limit_bytes=mb << 20)


def cost(flops, nbytes, trans=0):
    return pl.CostEstimate(flops=int(flops), bytes_accessed=int(nbytes), transcendentals=int(trans))


def whole(shape):
    return pl.BlockSpec(shape, lambda *_: (0,) * len(shape), pipeline_mode=pl.Buffered(1))


def row_stats(x):
    mean = jnp.mean(x, axis=1, keepdims=True)
    cen = x - mean
    inv = lax.rsqrt(jnp.mean(cen * cen, axis=1, keepdims=True) + EPS)
    return cen * inv, inv


def norm_back(g, std, inv, gain):
    e = g * gain
    return inv * (e - jnp.mean(e, axis=1, keepdims=True) - std * jnp.mean(e * std, axis=1, keepdims=True))


def can_split(rows, m):
    return m % 8 == 0 and rows % (2 * m) == 0


def ring_order(dp):
    if dp != 16:
        return list(range(dp // 2))
    return [2 * z for z in range(4)] + [2 * z + 1 for z in reversed(range(4))]


def split_store(val, refs, core, m, order=None):
    rows, cols = val.shape
    parts = val.reshape(rows // (2 * m), 2, m, cols)
    low, high = parts[:, 0], parts[:, 1]
    keep = jnp.where(core == 0, low, high)
    send = jnp.where(core == 0, high, low)
    if order is None:
        refs[0][...] = keep
        refs[1][...] = send
    else:
        for place, owner in enumerate(order):
            refs[0][place] = keep[owner]
            refs[1][place] = send[owner]


def put(val, refs, core, m, order=None):
    if len(refs) == 2:
        split_store(val, refs, core, m, order)
    else:
        refs[0][...] = val


SMEM1 = pl.BlockSpec(memory_space=pltpu.SMEM)


def eye_mask(t):
    return lax.broadcasted_iota(jnp.int32, (t, t), 0) == lax.broadcasted_iota(jnp.int32, (t, t), 1)


def line(ref):
    return ref[...].astype(f32).reshape(1, -1)


def front_kernel(
    len_ref, gid_ref, cnt_ref, keep_ref, x_ref, s_ref, ws_ref, bs_ref, g_ref, b_ref, wj_ref,
    hid_ref, n1_ref, q_ref, qf_ref, kf_ref, tw_ref, *, group_tokens, sub,
):
    rb, w = x_ref.shape

    def project(r):
        return mm(x_ref[r, :], ws_ref[:w, :]) + mm(s_ref[r, :], ws_ref[w:, :]) + line(bs_ref)

    parts = [slice(lo, lo + sub) for lo in range(0, rb, sub)]
    ahead = project(parts[0])
    for i, r in enumerate(parts):
        hid = ahead
        if i + 1 < len(parts):
            ahead = project(parts[i + 1])
        hid_ref[r, :] = hid
        std, _ = row_stats(hid)
        n1 = (std * line(g_ref) + line(b_ref)).astype(bf16)
        n1_ref[r, :] = n1
        q_ref[r, :] = mm(n1, wj_ref[...]).astype(bf16)

    slots = len_ref.shape[0]
    base = pl.program_id(0) * rb
    lane = lax.broadcasted_iota(jnp.int32, (1, PAIR), 1)
    pos = lax.broadcasted_iota(jnp.int32, (rb, 1), 0) + base
    segment = jnp.zeros((rb, 1), jnp.int32)
    count = jnp.ones((1, PAIR), f32)
    end = 0
    for i in range(slots):
        end = end + len_ref[i]
        segment = segment + (pos >= end).astype(jnp.int32)
        count = jnp.where(lane == i, cnt_ref[gid_ref[i]].astype(f32), count)
    same = segment == lane
    weight = jnp.where(lane < slots, group_tokens / count, 0.0)
    tw_ref[...] = jnp.sum(jnp.where(same, weight, 0.0), axis=1, keepdims=True)
    qf_ref[...] = jnp.where(same, 1.0, 0.0).astype(bf16)
    eye = eye_mask(PAIR)
    for t in range(rb // PAIR):
        rows = slice(t * PAIR, (t + 1) * PAIR)
        keep = keep_ref[pl.ds(pl.multiple_of(base + t * PAIR, PAIR), PAIR)].astype(f32).reshape(1, PAIR)
        kept = jnp.sum(jnp.where(eye, keep, 0.0), axis=1, keepdims=True) == 1.0
        bias = jnp.where(same[rows] & kept, 0.0, -BIG)
        kf_ref[rows, :] = jnp.where(lane <= slots, bias, jnp.where(lane < slots + 4, 1.0, 0.0)).astype(bf16)


def front(lengths, gids, counts, keep, x, s, ws, bs, g, b, wj, rb, group_tokens, sub=192):
    n, w = x.shape
    c = wj.shape[1]
    row = lambda cols: pl.BlockSpec((rb, cols), lambda i: (i, 0))
    return pl.pallas_call(
        functools.partial(front_kernel, group_tokens=float(group_tokens), sub=sub),
        grid=(n // rb,),
        in_specs=[SMEM1, SMEM1, SMEM1, whole((n,)), row(w), row(w), whole(ws.shape), whole((w,)), whole((w,)), whole((w,)), whole(wj.shape)],
        out_specs=[row(w), row(w), row(c), row(PAIR), row(PAIR), row(1)],
        out_shape=[
            jax.ShapeDtypeStruct((n, w), f32),
            jax.ShapeDtypeStruct((n, w), bf16),
            jax.ShapeDtypeStruct((n, c), bf16),
            jax.ShapeDtypeStruct((n, PAIR), bf16),
            jax.ShapeDtypeStruct((n, PAIR), bf16),
            jax.ShapeDtypeStruct((n, 1), f32),
        ],
        compiler_params=params(),
        cost_estimate=cost(2 * n * w * (2 * w + c), n * w * 20 + 5 * w * w * 2),
        name="front",
    )(lengths, gids, counts, keep, x, s, ws, bs, g, b, wj)


def half_mask(h):
    lane = lax.broadcasted_iota(jnp.int32, (1, PAIR), 1)
    return (lane < HEAD_DIM) if h == 0 else (lane >= HEAD_DIM)


def pieces(x):
    a = x.astype(bf16)
    r = x - a.astype(f32)
    b = r.astype(bf16)
    c = (r - b.astype(f32)).astype(bf16)
    return a, b, c


def attn_fwd_kernel(
    q_ref, k_ref, v_ref, qf_ref, kf_ref, cot_ref, tw_ref, o_ref, feat_ref, gr_ref, grt_ref, gsum_ref, ka_ref, vm_ref, s_ref, *, tq, per
):
    n = q_ref.shape[0]
    none = jnp.zeros((1, PAIR), bf16)
    one = jnp.ones((1, PAIR), bf16)
    lane = lax.broadcasted_iota(jnp.int32, (1, PAIR), 1)
    spare = [HEAD_DIM, 0]
    cols = [slice(d * PAIR, (d + 1) * PAIR) for d in range(per)]
    for d in range(per):
        ka_ref[d, :, :PAIR] = k_ref[:, cols[d]]
        ka_ref[d, :, PAIR:] = kf_ref[...]
        for h in range(2):
            vm_ref[d, h] = jnp.where(half_mask(h), v_ref[:, cols[d]], jnp.where(lane == spare[h], one, none))
    eye = eye_mask(PAIR)
    units = [(d, i, h) for d in range(per) for i in range(n // tq) for h in range(2)]

    def scores(u):
        d, i, h = units[u]
        rows = slice(i * tq, (i + 1) * tq)
        qm = jnp.where(half_mask(h), q_ref[rows, cols[d]] * jnp.asarray(HEAD_DIM**-0.5, bf16), none)
        slot = u % 2
        s_ref[slot] = mm(jnp.concatenate([qm, qf_ref[rows, :]], axis=1), ka_ref[d], NT)
        for j in range(tq // PAIR):
            a = slice(j * PAIR, (j + 1) * PAIR)
            c = slice(i * tq + j * PAIR, i * tq + (j + 1) * PAIR)
            s_ref[slot, a, c] = jnp.where(eye, mm(qm[a], k_ref[c, cols[d]], NT), s_ref[slot, a, c])

    scores(0)
    outs = [None, None]
    gsum = [None] * per
    for u, (d, i, h) in enumerate(units):
        if u + 1 < len(units):
            scores(u + 1)
        rows = slice(i * tq, (i + 1) * tq)
        s = s_ref[u % 2]
        top = jnp.max(s, axis=1, keepdims=True)
        pv = mm(jnp.exp(s - top).astype(bf16), vm_ref[d, h])
        total = pv[:, spare[h] : spare[h] + 1]
        outs[h] = pv / total
        a, b, c = pieces(-(top + jnp.log(total)))
        feat_ref[2 * d + h, rows, :] = jnp.where(
            lane == 5, a, jnp.where(lane == 6, b, jnp.where(lane == 7, c, qf_ref[rows, :]))
        )
        if h == 0:
            gr = (cot_ref[rows, cols[d]].astype(f32) * tw_ref[rows, :]).astype(bf16)
            gr_ref[rows, cols[d]] = gr
            grt_ref[cols[d], rows] = gr.T
            part = jnp.sum(gr.astype(f32), axis=0, keepdims=True)
            gsum[d] = part if i == 0 else gsum[d] + part
        else:
            o_ref[rows, cols[d]] = jnp.where(lane < HEAD_DIM, outs[0], outs[1]).astype(bf16)
    for d in range(per):
        gsum_ref[:, cols[d]] = gsum[d]


def attn_fwd(packed, qf, kf, cot, tw, tq=384, per=1):
    n, c = packed.shape
    w = c // 3
    pairs = w // PAIR
    wide = per * PAIR
    part = lambda p: pl.BlockSpec((n, wide), lambda j: (0, p * (pairs // per) + j))
    return pl.pallas_call(
        functools.partial(attn_fwd_kernel, tq=tq, per=per),
        grid=(pairs // per,),
        in_specs=[part(0), part(1), part(2), whole((n, PAIR)), whole((n, PAIR)), part(0), whole((n, 1))],
        out_specs=[
            pl.BlockSpec((n, wide), lambda j: (0, j)),
            pl.BlockSpec((2 * per, n, PAIR), lambda j: (j, 0, 0)),
            pl.BlockSpec((n, wide), lambda j: (0, j)),
            pl.BlockSpec((wide, n), lambda j: (j, 0)),
            pl.BlockSpec((1, wide), lambda j: (0, j)),
        ],
        out_shape=[
            jax.ShapeDtypeStruct((n, w), bf16),
            jax.ShapeDtypeStruct((2 * pairs, n, PAIR), bf16),
            jax.ShapeDtypeStruct((n, w), bf16),
            jax.ShapeDtypeStruct((w, n), bf16),
            jax.ShapeDtypeStruct((1, w), f32),
        ],
        scratch_shapes=[
            pltpu.VMEM((per, n, 2 * PAIR), bf16),
            pltpu.VMEM((per, 2, n, PAIR), bf16),
            pltpu.VMEM((2, tq, n), f32),
        ],
        compiler_params=params(),
        cost_estimate=cost(2 * n * n * (4 * PAIR) * pairs * 2, n * c * 4, n * n * 2 * pairs),
        name="attn_fwd",
    )(packed, packed, packed, qf, kf, cot, tw)


def attn_bwd_kernel(
    q_ref, k_ref, v_ref, o_ref, g_ref, feat_ref, kf_ref, out_ref, ka_ref, va_ref, qa_ref, ga_ref, kt_ref, dq_ref, st_ref, dp_ref,
    *, tk, live, per,
):
    n = q_ref.shape[0]
    lane = lax.broadcasted_iota(jnp.int32, (1, PAIR), 1)
    none = jnp.zeros((1, PAIR), bf16)
    scale = HEAD_DIM**-0.5
    cols = [slice(d * PAIR, (d + 1) * PAIR) for d in range(per)]

    def prepare(d):
        ka_ref[d, :, :PAIR] = k_ref[:, cols[d]]
        ka_ref[d, :, PAIR:] = kf_ref[...]
        va_ref[d, :, :PAIR] = v_ref[:, cols[d]]
        va_ref[d, :, PAIR:] = jnp.broadcast_to(jnp.where(lane < 3, 1.0, 0.0).astype(bf16), (n, PAIR))
        kt_ref[d] = k_ref[:, cols[d]].T
        q = q_ref[:, cols[d]] * jnp.asarray(scale, bf16)
        g = g_ref[:, cols[d]]
        prod = g.astype(f32) * o_ref[:, cols[d]].astype(f32)
        for h in range(2):
            own = half_mask(h)
            delta = jnp.sum(jnp.where(own, prod, 0.0), axis=1, keepdims=True)
            a, b, c = pieces(-delta)
            qa_ref[d, h, :, :PAIR] = jnp.where(own, q, none)
            qa_ref[d, h, :, PAIR:] = feat_ref[2 * d + h]
            ga_ref[d, h, :, :PAIR] = jnp.where(own, g, none)
            ga_ref[d, h, :, PAIR:] = jnp.where(lane == 0, a, jnp.where(lane == 1, b, jnp.where(lane == 2, c, none)))

    eye = eye_mask(PAIR)
    spans = [(i, min(i + tk, live)) for i in range(0, live, tk)]
    units = [(d, span, h) for d in range(per) for span in spans for h in range(2)]

    def scores(u):
        d, (lo, hi), h = units[u]
        size = hi - lo
        slot = u % 2
        st_ref[slot, :size] = mm(ka_ref[d, lo:hi, :], qa_ref[d, h], NT)
        for j in range(0, size, PAIR):
            t = min(PAIR, size - j)
            a = slice(j, j + t)
            r = slice(lo + j, lo + j + t)
            c = slice(lo + j, lo + j + PAIR)
            plain = jnp.concatenate([k_ref[r, cols[d]], jnp.where(lane < 5, none, kf_ref[r, :])], axis=1)
            st_ref[slot, a, c] = jnp.where(eye[:t], mm(plain, qa_ref[d, h, c, :], NT), st_ref[slot, a, c])
        dp_ref[slot, :size] = mm(va_ref[d, lo:hi, :], ga_ref[d, h], NT)

    prepare(0)
    scores(0)
    dv = [None, None]
    dk = [None, None]
    for u, (d, (lo, hi), h) in enumerate(units):
        if (lo, h) == (0, 0) and d + 1 < per:
            prepare(d + 1)
        if u + 1 < len(units):
            scores(u + 1)
        rows = slice(lo, hi)
        own = slice(h * HEAD_DIM, (h + 1) * HEAD_DIM)
        p = jnp.exp(st_ref[u % 2, : hi - lo])
        ds = (p * dp_ref[u % 2, : hi - lo]).astype(bf16)
        part = mm(kt_ref[d, own, rows], ds)
        if lo == 0:
            dq_ref[d, own, :] = part
        else:
            dq_ref[d, own, :] += part
        dv[h] = mm(p.astype(bf16), ga_ref[d, h, :, :PAIR])
        dk[h] = mm(ds, qa_ref[d, h, :, :PAIR])
        if h == 1:
            out_ref[1, rows, cols[d]] = (dk[0] + dk[1]).astype(bf16)
            out_ref[2, rows, cols[d]] = (dv[0] + dv[1]).astype(bf16)
            if hi == live:
                out_ref[0, :, cols[d]] = (dq_ref[d].T * scale).astype(bf16)
    if live < n:
        out_ref[1, live:, :] = jnp.zeros((n - live, per * PAIR), bf16)
        out_ref[2, live:, :] = jnp.zeros((n - live, per * PAIR), bf16)


def attn_bwd(packed, att, grad, feat, kf, tk=384, per=1):
    n, c = packed.shape
    w = c // 3
    pairs = w // PAIR
    wide = per * PAIR
    part = lambda p: pl.BlockSpec((n, wide), lambda j: (0, p * (pairs // per) + j))
    live = min(n, -(-ITEM_ROWS // 16) * 16)
    return pl.pallas_call(
        functools.partial(attn_bwd_kernel, tk=tk, live=live, per=per),
        grid=(pairs // per,),
        in_specs=[
            part(0),
            part(1),
            part(2),
            part(0),
            part(0),
            pl.BlockSpec((2 * per, n, PAIR), lambda j: (j, 0, 0)),
            whole((n, PAIR)),
        ],
        out_specs=pl.BlockSpec((3, n, wide), lambda j: (0, 0, j)),
        out_shape=jax.ShapeDtypeStruct((3, n, w), bf16),
        scratch_shapes=[
            pltpu.VMEM((per, n, 2 * PAIR), bf16),
            pltpu.VMEM((per, n, 2 * PAIR), bf16),
            pltpu.VMEM((per, 2, n, 2 * PAIR), bf16),
            pltpu.VMEM((per, 2, n, 2 * PAIR), bf16),
            pltpu.VMEM((per, PAIR, n), bf16),
            pltpu.VMEM((per, PAIR, n), f32),
            pltpu.VMEM((2, tk, n), f32),
            pltpu.VMEM((2, tk, n), f32),
        ],
        compiler_params=params(),
        cost_estimate=cost(2 * n * n * (9 * PAIR) * pairs * 2, n * c * 8, n * n * 2 * pairs),
        name="attn_bwd",
    )(packed, packed, packed, att, grad, feat, kf)


def normal_cdf_pdf(u):
    a = jnp.abs(u)
    t = 1.0 / (1.0 + a * (0.3275911 * 0.7071067811865476))
    e = jnp.exp(-0.5 * u * u)
    half = 0.5
    poly = t * (
        half * 0.254829592
        + t * (half * -0.284496736 + t * (half * 1.421413741 + t * (half * -1.453152027 + t * (half * 1.061405429))))
    )
    tail = poly * e
    return jnp.where(u < 0, tail, 1.0 - tail), e * 0.3989422804014327


def ff_fwd_kernel(
    core_ref, a_ref, hid_ref, wo_ref, bo_ref, g_ref, b_ref, grt_ref, w1_ref, b1_ref, w2_ref,
    mid_out, n2_out, acc_ref, slope_ref, *rest, m, order, sub, count, rb,
):
    refs, (mid_ref, n2_ref, sems) = rest[:count], rest[count:]
    n = a_ref.shape[0]
    step = pl.program_id(0)
    copies = [pltpu.make_async_copy(mid_ref, mid_out, sems.at[0]), pltpu.make_async_copy(n2_ref, n2_out, sems.at[1])]

    @pl.when(step == 0)
    def _():
        parts = [slice(lo, lo + rb) for lo in range(0, n, rb)]
        project = lambda r: mm(a_ref[r, :], wo_ref[...])
        ahead = project(parts[0])
        for i, r in enumerate(parts):
            mid = hid_ref[r, :] + ahead + line(bo_ref)
            if i + 1 < len(parts):
                ahead = project(parts[i + 1])
            mid_ref[r, :] = mid
            std, _ = row_stats(mid)
            n2_ref[r, :] = (std * line(g_ref) + line(b_ref)).astype(bf16)
        for c in copies:
            c.start()
        acc_ref[...] = jnp.zeros_like(acc_ref)

    fc = w1_ref.shape[1]
    bias = line(b1_ref)
    cut = lambda s: slice(s * sub, (s + 1) * sub)
    before = lambda s: mm(n2_ref[...], w1_ref[:, cut(s)]) + bias[:, cut(s)]
    ahead = before(0)
    for s in range(fc // sub):
        pre = ahead
        if s + 1 < fc // sub:
            ahead = before(s + 1)
        cdf, pdf = normal_cdf_pdf(pre)
        act = (pre * cdf).astype(bf16)
        slope_ref[:, cut(s)] = (cdf + pre * pdf).astype(bf16)
        acc_ref[...] += mm(act, w2_ref[cut(s), :])
        views = [r.at[:, :, cut(s)] if count == 2 else r.at[:, cut(s)] for r in refs]
        put(mm(grt_ref[...], act), views, core_ref[0], m, order)

    @pl.when(step == pl.num_programs(0) - 1)
    def _():
        for c in copies:
            c.wait()


def ff_fwd(core, dp, att, hid, wo, bo, g, b, grt, w1, b1, w2, fc=1024, sub=256):
    n, w = att.shape
    ff = w1.shape[1]
    m = w // dp
    if can_split(w, m):
        specs = [pl.BlockSpec((dp // 2, m, fc), lambda i: (0, i, 0))] * 2
        shapes = [jax.ShapeDtypeStruct((dp // 2, ff // fc * m, fc), f32)] * 2
    else:
        specs = [pl.BlockSpec((w, fc), lambda i: (0, i))]
        shapes = [jax.ShapeDtypeStruct((w, ff), f32)]
    left = pl.BlockSpec(memory_space=pl.ANY)
    res = pl.pallas_call(
        functools.partial(ff_fwd_kernel, m=m, order=ring_order(dp), sub=sub, count=len(specs), rb=n // 3),
        grid=(ff // fc,),
        in_specs=[
            SMEM1,
            whole((n, w)),
            whole((n, w)),
            whole((w, w)),
            whole((w,)),
            whole((w,)),
            whole((w,)),
            whole((w, n)),
            pl.BlockSpec((w, fc), lambda i: (0, i)),
            pl.BlockSpec((fc,), lambda i: (i,)),
            pl.BlockSpec((fc, w), lambda i: (i, 0)),
        ],
        out_specs=[left, left, whole((n, w)), pl.BlockSpec((n, fc), lambda i: (0, i))] + specs,
        out_shape=[
            jax.ShapeDtypeStruct((n, w), f32),
            jax.ShapeDtypeStruct((n, w), bf16),
            jax.ShapeDtypeStruct((n, w), f32),
            jax.ShapeDtypeStruct((n, ff), bf16),
        ]
        + shapes,
        scratch_shapes=[pltpu.VMEM((n, w), f32), pltpu.VMEM((n, w), bf16), pltpu.SemaphoreType.DMA((2,))],
        compiler_params=params(60),
        cost_estimate=cost(6 * n * w * ff, n * w * 10 + ff * w * 8 + n * ff * 2, n * ff * 2),
        name="ff_fwd",
    )(core, att, hid, wo, bo, g, b, grt, w1, b1, w2)
    return res[0], res[1], res[2], res[3], res[4:]


def ff_bwd_kernel(core_ref, n2_ref, gr_ref, w1a_ref, w1b_ref, sla_ref, slb_ref, w2a_ref, w2b_ref, *rest, first, count, m):
    gn_ref, db1_ref = rest[-2 - count : -count]
    refs = rest[-count:]
    side = lambda a, b: jnp.concatenate([a[...], b[...]], axis=1)
    w1 = side(w1a_ref, w1b_ref)
    w2 = jnp.concatenate([w2a_ref[...], w2b_ref[...]], axis=0)
    gpre = (mm(gr_ref[...], w2, NT) * side(sla_ref, slb_ref).astype(f32)).astype(bf16)

    @pl.when(pl.program_id(0) == 0)
    def _():
        gn_ref[...] = jnp.zeros_like(gn_ref) if first else rest[0][...]

    gn_ref[...] += mm(gpre, w1, NT)
    put(mm(gpre, n2_ref[...], TN), refs, core_ref[0], m)
    db1_ref[...] = jnp.sum(gpre.astype(f32), axis=0, keepdims=True)


def ff_bwd(core, dp, n2, gr, w1, slope, w2, base, steps, prev):
    n, w = n2.shape
    ff = w1.shape[1]
    m = ff // dp
    fc = 384
    ring = can_split(fc, m) and fc == 2 * m and dp == 16
    total = ff // (2 * fc)
    steps = total - base if steps is None else steps
    if ring:
        near = lambda i: jnp.where(base + i < 2, 4 * (base + i), 15 - 4 * (base + i))
        far = lambda i: jnp.where(base + i < 2, 4 * (base + i) + 2, 13 - 4 * (base + i))
        specs = [pl.BlockSpec((2, m, w), lambda i: (base + i, 0, 0))] * 2
        shapes = [jax.ShapeDtypeStruct((dp // 2, m, w), f32)] * 2
    else:
        near = lambda i: 2 * (base + i)
        far = lambda i: 2 * (base + i) + 1
        specs = [pl.BlockSpec((2 * fc, w), lambda i: (base + i, 0))]
        shapes = [jax.ShapeDtypeStruct((ff, w), f32)]
    extra = [] if prev is None else list(prev)
    res = pl.pallas_call(
        functools.partial(ff_bwd_kernel, first=prev is None, count=len(specs), m=m),
        grid=(steps,),
        in_specs=[
            SMEM1,
            whole((n, w)),
            whole((n, w)),
            pl.BlockSpec((w, fc), lambda i: (0, near(i))),
            pl.BlockSpec((w, fc), lambda i: (0, far(i))),
            pl.BlockSpec((n, fc), lambda i: (0, near(i))),
            pl.BlockSpec((n, fc), lambda i: (0, far(i))),
            pl.BlockSpec((fc, w), lambda i: (near(i), 0)),
            pl.BlockSpec((fc, w), lambda i: (far(i), 0)),
        ]
        + ([whole((n, w))] + [pl.BlockSpec(memory_space=pl.ANY)] * len(specs) if extra else []),
        out_specs=[whole((n, w)), pl.BlockSpec((1, 2 * fc), lambda i: (0, i))] + specs,
        out_shape=[jax.ShapeDtypeStruct((n, w), f32), jax.ShapeDtypeStruct((1, 2 * fc * steps), f32)] + shapes,
        input_output_aliases={10 + k: 2 + k for k in range(len(specs))} if extra else {},
        compiler_params=params(60),
        cost_estimate=cost(12 * n * w * fc * steps, n * w * 10 + fc * steps * w * 16 + n * fc * steps * 4),
        name="ff_bwd",
    )(core, n2, gr, w1, w1, slope, slope, w2, w2, *extra)
    return (res[0], *res[2:]), res[1]


def back_kernel(core_ref, mid_ref, acc_ref, gn_ref, cot_ref, tw_ref, a_ref, wo_ref, g_ref, b2_ref, *rest, m, count, order, sub):
    out_ref, gm_ref, ga_ref, vec_ref = rest[-5 - count : -1 - count]
    dwo_refs, dwo_ref = rest[-1 - count : -1], rest[-1]
    rb, w = mid_ref.shape
    step = pl.program_id(0)
    add = lambda x: jnp.sum(x, axis=0, keepdims=True)
    parts = [slice(lo, lo + sub) for lo in range(0, rb, sub)]

    @pl.when(step == 0)
    def _():
        dwo_ref[...] = jnp.zeros_like(dwo_ref)
        vec_ref[...] = jnp.zeros_like(vec_ref)

    def norm_part(r):
        mid = mid_ref[r, :]
        out_ref[r, :] = (mid + acc_ref[r, :] + line(b2_ref)).astype(bf16)
        std, inv = row_stats(mid)
        gn = gn_ref[r, :]
        gm = cot_ref[r, :].astype(f32) * tw_ref[r, :] + norm_back(gn, std, inv, line(g_ref))
        gm_ref[r, :] = gm
        gb = gm.astype(bf16)
        vec_ref[...] += jnp.concatenate([add(gb.astype(f32)), add(gn * std), add(gn), jnp.zeros((1, w), f32)], axis=0)
        return gb

    ahead = norm_part(parts[0])
    for i, r in enumerate(parts):
        gb = ahead
        if i + 1 < len(parts):
            ahead = norm_part(parts[i + 1])
        ga_ref[r, :] = mm(gb, wo_ref[...], NT).astype(bf16)
        dwo_ref[...] += mm(gb, a_ref[r, :], TN)

    @pl.when(step == pl.num_programs(0) - 1)
    def _():
        put(dwo_ref[...], dwo_refs, core_ref[0], m, order)


def grad_outs(rows, cols, m):
    if can_split(rows, m):
        shape = (rows // (2 * m), m, cols)
        return [whole(shape)] * 2, [jax.ShapeDtypeStruct(shape, f32)] * 2
    return [whole((rows, cols))], [jax.ShapeDtypeStruct((rows, cols), f32)]


def back_part(core, dp, mid, acc, gn, cot, tw, att, wo, g, b2, rb, sub=384):
    n, w = mid.shape
    row = lambda cols: pl.BlockSpec((rb, cols), lambda i: (i, 0))
    mo, mj = w // dp, 3 * w // dp
    if can_split(w, mo) and can_split(3 * w, mj):
        specs = [pl.BlockSpec((dp // 2, mo, w), lambda i: (0, mj // mo, 0))] * 2
        shapes = [jax.ShapeDtypeStruct((dp // 2, mj + mo, w), f32)] * 2
    else:
        specs, shapes = [whole((w, w))], [jax.ShapeDtypeStruct((w, w), f32)]
    res = pl.pallas_call(
        functools.partial(back_kernel, m=mo, count=len(specs), order=ring_order(dp), sub=sub),
        grid=(n // rb,),
        in_specs=[SMEM1, row(w), row(w), row(w), row(w), row(1), row(w), whole(wo.shape), whole((w,)), whole((w,))],
        out_specs=[row(w), row(w), row(w), whole((4, w))] + specs,
        out_shape=[
            jax.ShapeDtypeStruct((n, w), bf16),
            jax.ShapeDtypeStruct((n, w), f32),
            jax.ShapeDtypeStruct((n, w), bf16),
            jax.ShapeDtypeStruct((4, w), f32),
        ]
        + shapes,
        scratch_shapes=[pltpu.VMEM((w, w), f32)],
        compiler_params=params(),
        cost_estimate=cost(4 * n * w * w, n * w * 28),
        name="back_part",
    )(core, mid, acc, gn, cot, tw, att, wo, g, b2)
    return res[0], res[1], res[2], res[3], res[4:]


def joint_grad_kernel(core_ref, gp_ref, n1_ref, *rest, m, count, order):
    refs, gpt_ref = rest[-1 - count : -1], rest[-1]
    parts, n, w = gp_ref.shape

    @pl.when(pl.program_id(0) == 0)
    def _():
        for p in range(parts):
            gpt_ref[p * w : (p + 1) * w, :] = gp_ref[p].T

    put(mm(gpt_ref[...], n1_ref[...]), refs, core_ref[0], m, order)


def grad_block(rows, cols, cb, m):
    if can_split(rows, m):
        spec = pl.BlockSpec((rows // (2 * m), m, cb), lambda j: (0, 0, j))
        return [spec] * 2, [jax.ShapeDtypeStruct((rows // (2 * m), m, cols), f32)] * 2
    return [pl.BlockSpec((rows, cb), lambda j: (0, j))], [jax.ShapeDtypeStruct((rows, cols), f32)]


def joint_grad(core, dp, gp, n1, into, cb=256):
    parts, n, w = gp.shape
    m = parts * w // dp
    specs, shapes = grad_block(parts * w, w, cb, m)
    if len(into) == 2:
        shapes = [jax.ShapeDtypeStruct(x.shape, f32) for x in into]
    else:
        into = []
    return pl.pallas_call(
        functools.partial(joint_grad_kernel, m=m, count=len(specs), order=ring_order(dp)),
        grid=(w // cb,),
        in_specs=[SMEM1, whole((parts, n, w)), pl.BlockSpec((n, cb), lambda j: (0, j))]
        + [pl.BlockSpec(memory_space=pl.ANY)] * len(into),
        out_specs=specs,
        out_shape=shapes,
        input_output_aliases={3 + k: k for k in range(len(into))},
        scratch_shapes=[pltpu.VMEM((parts * w, n), bf16)],
        compiler_params=params(),
        cost_estimate=cost(2 * parts * n * w * w, n * w * 8 + parts * w * w * 4),
        name="joint_grad",
    )(core, gp, n1, *into)


def tail_kernel(gp_ref, hid_ref, gm_ref, wj_ref, g_ref, gh_ref, vec_ref, *, sub):
    rb, w = hid_ref.shape
    parts = [slice(lo, lo + sub) for lo in range(0, rb, sub)]
    add = lambda x: jnp.sum(x, axis=0, keepdims=True)

    def project(r):
        return sum(mm(gp_ref[p, r, :], wj_ref[:, p * w : (p + 1) * w], NT) for p in range(3))

    ahead = project(parts[0])
    vec = jnp.zeros((4, w), f32)
    for i, r in enumerate(parts):
        gn = ahead
        if i + 1 < len(parts):
            ahead = project(parts[i + 1])
        std, inv = row_stats(hid_ref[r, :])
        gh = (gm_ref[r, :] + norm_back(gn, std, inv, line(g_ref))).astype(bf16)
        gh_ref[r, :] = gh
        vec = vec + jnp.concatenate([add(gn * std), add(gn), add(gh.astype(f32)), jnp.zeros((1, w), f32)], axis=0)
    step = pl.program_id(0)

    @pl.when(step == 0)
    def _():
        vec_ref[...] = vec

    @pl.when(step > 0)
    def _():
        vec_ref[...] += vec


def tail_part(gp, hid, gm, wj, g, rb, sub=384):
    n, w = hid.shape
    row = lambda cols: pl.BlockSpec((rb, cols), lambda i: (i, 0))
    return pl.pallas_call(
        functools.partial(tail_kernel, sub=sub),
        grid=(n // rb,),
        in_specs=[pl.BlockSpec((3, rb, w), lambda i: (0, i, 0)), row(w), row(w), whole(wj.shape), whole((w,))],
        out_specs=[row(w), whole((4, w))],
        out_shape=[jax.ShapeDtypeStruct((n, w), bf16), jax.ShapeDtypeStruct((4, w), f32)],
        compiler_params=params(),
        cost_estimate=cost(6 * n * w * w, n * w * 16),
        name="tail_part",
    )(gp, hid, gm, wj, g)


def skip_grad_kernel(core_ref, gh_ref, x_ref, s_ref, vec_ref, *refs, m, order):
    ght = gh_ref[...].T
    val = jnp.concatenate([mm(ght, x_ref[...]), mm(ght, s_ref[...]), vec_ref[...]], axis=1)
    put(val, refs, core_ref[0], m, order)


def skip_grad(core, dp, gh, x, s, vec):
    n, w = gh.shape
    m = w // dp
    cols = 2 * w + vec.shape[1]
    specs, shapes = grad_block(w, cols, cols, m)
    return pl.pallas_call(
        functools.partial(skip_grad_kernel, m=m, order=ring_order(dp)),
        grid=(1,),
        in_specs=[SMEM1, whole((n, w)), whole((n, w)), whole((n, w)), whole(vec.shape)],
        out_specs=specs,
        out_shape=shapes,
        compiler_params=params(),
        cost_estimate=cost(4 * n * w * w, n * w * 6 + w * w * 8),
        name="skip_grad",
    )(core, gh, x, s, vec)


def in_grad_kernel(gh_ref, ws_ref, a_ref, b_ref):
    w = a_ref.shape[1]
    gh = gh_ref[...]
    a_ref[...] = mm(gh, ws_ref[:w, :], NT).astype(bf16)
    b_ref[...] = mm(gh, ws_ref[w:, :], NT).astype(bf16)


def in_grad(gh, ws, rb):
    n, w = gh.shape
    row = lambda cols: pl.BlockSpec((rb, cols), lambda i: (i, 0))
    return pl.pallas_call(
        in_grad_kernel,
        grid=(n // rb,),
        in_specs=[row(w), whole(ws.shape)],
        out_specs=[row(w), row(w)],
        out_shape=[jax.ShapeDtypeStruct((n, w), bf16)] * 2,
        compiler_params=params(),
        cost_estimate=cost(4 * n * w * w, n * w * 10),
        name="in_grad",
    )(gh, ws)


def pick(x, axis, index):
    return lax.dynamic_index_in_dim(x, index, axis, keepdims=False)


def swap(x, axis, bit=0):
    size = lax.axis_size(axis)
    return lax.ppermute(x, axis, [(i, i ^ (1 << bit)) for i in range(size)])


def pair_terms(refs, cols, dp):
    if len(refs) == 1:
        full = refs[0].reshape(dp // 2, 2, -1, cols)
        core = lax.axis_index("dp") & 1
        refs = [pick(full, 1, core), pick(full, 1, 1 - core)]
    return [refs[0], swap(refs[1], "dp")]


def both_sides(x, side):
    other = swap(x, "rep")
    return jnp.concatenate([jnp.where(side == 0, x, other), jnp.where(side == 0, other, x)], axis=0)


def tie(x, y):
    return lax.optimization_barrier((x, y))


def per_device(*args):
    (inputs, skips, cot, lengths, keep, group_ids, group_counts, ws, bs, g1, s1, wj, wo, bo, g2, s2, w1, b1, w2, b2) = args
    n, w = inputs.shape
    ff = w1.shape[1]
    dp = lax.axis_size("dp")
    tokens_total = n * dp * lax.axis_size("rep")
    scale = float(tokens_total) ** -0.5
    side = lax.axis_index("rep")
    core = (lax.axis_index("dp") & 1).astype(jnp.int32).reshape(1)
    rb = n // 3
    ring = ring_order(dp)
    groups = [[2 * i + c for i in ring] for c in range(2)]
    ring_sum = lambda h: lax.psum_scatter(h, "dp", scatter_dimension=0, tiled=True, axis_index_groups=groups)[0]
    over_rep = lambda h: h + swap(h, "rep")

    hid, n1, packed, qf, kf, tw = front(
        lengths, group_ids, group_counts, keep, inputs, skips, ws, bs, g1, s1, wj, rb, tokens_total // group_counts.shape[0]
    )
    att, feat, gr, grt, gsum = attn_fwd(packed, qf, kf, cot, tw)
    mid, n2, acc, slope, d2 = ff_fwd(core, dp, att, hid, wo, bo, g2, s2, grt, w1, b1, w2)
    half2 = sum(pair_terms(d2, ff, dp))
    carry, db0 = ff_bwd(core, dp, n2, gr, w1, slope, w2, 0, 1, None)
    carry, half2 = tie(carry, half2)
    carry, db1 = ff_bwd(core, dp, n2, gr, w1, slope, w2, 1, None, carry)
    gn2, d1 = carry[0], carry[1:]
    outcome, gm, gatt, vec2, do = back_part(core, dp, mid, acc, gn2, cot, tw, att, wo, g2, b2, rb)
    half1 = sum(pair_terms(d1, w, dp))
    gatt, half1 = tie(gatt, half1)
    sum2 = ring_sum(half2)
    sum1 = ring_sum(half1)

    gp = attn_bwd(packed, att, gatt, feat, kf)
    gp, sum2 = tie(gp, sum2)
    got2 = swap(sum2, "rep")

    dj = joint_grad(core, dp, gp, n1, do)
    gp, dj = tie(gp, dj)
    if len(dj) == 2:
        halfj = sum(pair_terms(dj, w, dp))
    else:
        full = jnp.concatenate([dj[0].reshape(dp, 3 * w // dp, w), do[0].reshape(dp, w // dp, w)], axis=1)
        halfj = sum(pair_terms([full.reshape(-1, w)], w, dp))
    gh, vec1 = tail_part(gp, hid, gm, wj, g1, rb)
    gh, halfj, sum1, got2 = lax.optimization_barrier((gh, halfj, sum1, got2))
    sumj = ring_sum(halfj)
    db = jnp.concatenate([db0, db1], axis=1).reshape(8, ff // 8)
    if len(d1) == 2:
        db = jnp.stack([db[ring.index(i)] for i in range(8)])
    db = db.reshape(w, ff // w)
    vec = jnp.concatenate([vec1.T, vec2[:3].T, gsum.T, db, jnp.zeros((w, PAIR - 8 - ff // w), f32)], axis=1)
    cols = 2 * w + PAIR
    ds = skip_grad(core, dp, gh, inputs, skips, vec)
    terms = [t.reshape(dp // 2, 2, -1, cols) for t in pair_terms(ds, cols, dp)]
    send = sum(pick(t, 1, 1 - side) for t in terms)
    gh, send = tie(gh, send)
    igrad, sgrad = in_grad(gh, ws, rb)
    halfs = sum(pick(t, 1, side) for t in terms) + swap(send, "rep")
    halfs, sumj, sum1, igrad, sgrad = lax.optimization_barrier((halfs, sumj, sum1, igrad, sgrad))
    sums = ring_sum(halfs)
    out2 = sum2 + got2
    out1 = over_rep(sum1)
    outj = over_rep(sumj)
    if len(d2) == 2:
        out2 = out2.reshape(-1, w // dp, 1024).transpose(1, 0, 2).reshape(w // dp, ff)
    outj, outo = outj[: 3 * w // dp], outj[3 * w // dp :]
    outs = both_sides(sums, side)

    ds, dj, do, d1, d2 = [m.T * scale for m in (outs[:, : 2 * w], outj, outo, out1, out2)]
    v = outs[:, 2 * w :] * scale
    col = lambda i: v[:, i]
    db1 = v[:, 8 : 8 + ff // w].reshape(-1)
    return (
        outcome, igrad, sgrad, ds, col(2), col(0), col(1), dj, do, col(4), col(5), col(6), d1, db1, d2, col(7),
    )


def solution(mesh):
    both = ("dp", "rep")
    in_specs = (P(both, None),) * 3 + (P(both),) * 3 + (P(),) * 14
    cols = P(None, "dp")
    vec = P("dp")
    out_specs = (P(both, None),) * 3 + (cols, vec, vec, vec, cols, cols, vec, vec, vec, cols, vec, cols, vec)
    return jax.shard_map(per_device, mesh=mesh, in_specs=in_specs, out_specs=out_specs, check_vma=False)
```

```python
import functools

import jax
import jax.numpy as jnp
from jax import lax
from jax.experimental import pallas as pl
from jax.experimental.pallas import tpu as pltpu
from jax.sharding import PartitionSpec as P

HEAD_DIM = 64
PAIR = 2 * HEAD_DIM
EPS = 1e-05
BIG = 1e30
ITEM_ROWS = 1028
f32 = jnp.float32
bf16 = jnp.bfloat16
NT = (((1,), (1,)), ((), ()))
NN = (((1,), (0,)), ((), ()))
TN = (((0,), (0,)), ((), ()))


def mm(a, b, dims=NN):
    return lax.dot_general(a, b, dims, preferred_element_type=f32)


def params(mb=56):
    return pltpu.CompilerParams(vmem_limit_bytes=mb << 20)


def cost(flops, nbytes, trans=0):
    return pl.CostEstimate(flops=int(flops), bytes_accessed=int(nbytes), transcendentals=int(trans))


def whole(shape):
    return pl.BlockSpec(shape, lambda *_: (0,) * len(shape), pipeline_mode=pl.Buffered(1))


def row_stats(x):
    mean = jnp.mean(x, axis=1, keepdims=True)
    cen = x - mean
    inv = lax.rsqrt(jnp.mean(cen * cen, axis=1, keepdims=True) + EPS)
    return cen * inv, inv


def norm_back(g, std, inv, gain):
    e = g * gain
    return inv * (e - jnp.mean(e, axis=1, keepdims=True) - std * jnp.mean(e * std, axis=1, keepdims=True))


def can_split(rows, m):
    return m % 8 == 0 and rows % (2 * m) == 0


def ring_order(dp):
    if dp != 16:
        return list(range(dp // 2))
    return [2 * z for z in range(4)] + [2 * z + 1 for z in reversed(range(4))]


def split_store(val, refs, core, m, order=None):
    rows, cols = val.shape
    parts = val.reshape(rows // (2 * m), 2, m, cols)
    low, high = parts[:, 0], parts[:, 1]
    keep = jnp.where(core == 0, low, high)
    send = jnp.where(core == 0, high, low)
    if order is None:
        refs[0][...] = keep
        refs[1][...] = send
    else:
        for place, owner in enumerate(order):
            refs[0][place] = keep[owner]
            refs[1][place] = send[owner]


def put(val, refs, core, m, order=None):
    if len(refs) == 2:
        split_store(val, refs, core, m, order)
    else:
        refs[0][...] = val


SMEM1 = pl.BlockSpec(memory_space=pltpu.SMEM)


def eye_mask(t):
    return lax.broadcasted_iota(jnp.int32, (t, t), 0) == lax.broadcasted_iota(jnp.int32, (t, t), 1)


def line(ref):
    return ref[...].astype(f32).reshape(1, -1)


def front_kernel(
    len_ref, gid_ref, cnt_ref, keep_ref, x_ref, s_ref, ws_ref, bs_ref, g_ref, b_ref, wj_ref,
    hid_ref, n1_ref, q_ref, qf_ref, kf_ref, tw_ref, *, group_tokens, sub,
):
    rb, w = x_ref.shape

    def project(r):
        return mm(x_ref[r, :], ws_ref[:w, :]) + mm(s_ref[r, :], ws_ref[w:, :]) + line(bs_ref)

    parts = [slice(lo, lo + sub) for lo in range(0, rb, sub)]
    ahead = project(parts[0])
    for i, r in enumerate(parts):
        hid = ahead
        if i + 1 < len(parts):
            ahead = project(parts[i + 1])
        hid_ref[r, :] = hid
        std, _ = row_stats(hid)
        n1 = (std * line(g_ref) + line(b_ref)).astype(bf16)
        n1_ref[r, :] = n1
        q_ref[r, :] = mm(n1, wj_ref[...]).astype(bf16)

    slots = len_ref.shape[0]
    base = pl.program_id(0) * rb
    lane = lax.broadcasted_iota(jnp.int32, (1, PAIR), 1)
    pos = lax.broadcasted_iota(jnp.int32, (rb, 1), 0) + base
    segment = jnp.zeros((rb, 1), jnp.int32)
    count = jnp.ones((1, PAIR), f32)
    end = 0
    for i in range(slots):
        end = end + len_ref[i]
        segment = segment + (pos >= end).astype(jnp.int32)
        count = jnp.where(lane == i, cnt_ref[gid_ref[i]].astype(f32), count)
    same = segment == lane
    weight = jnp.where(lane < slots, group_tokens / count, 0.0)
    tw_ref[...] = jnp.sum(jnp.where(same, weight, 0.0), axis=1, keepdims=True)
    qf_ref[...] = jnp.where(same, 1.0, 0.0).astype(bf16)
    eye = eye_mask(PAIR)
    for t in range(rb // PAIR):
        rows = slice(t * PAIR, (t + 1) * PAIR)
        keep = keep_ref[pl.ds(pl.multiple_of(base + t * PAIR, PAIR), PAIR)].astype(f32).reshape(1, PAIR)
        kept = jnp.sum(jnp.where(eye, keep, 0.0), axis=1, keepdims=True) == 1.0
        bias = jnp.where(same[rows] & kept, 0.0, -BIG)
        kf_ref[rows, :] = jnp.where(lane <= slots, bias, jnp.where(lane < slots + 4, 1.0, 0.0)).astype(bf16)


def front(lengths, gids, counts, keep, x, s, ws, bs, g, b, wj, rb, group_tokens, sub=192):
    n, w = x.shape
    c = wj.shape[1]
    row = lambda cols: pl.BlockSpec((rb, cols), lambda i: (i, 0))
    return pl.pallas_call(
        functools.partial(front_kernel, group_tokens=float(group_tokens), sub=sub),
        grid=(n // rb,),
        in_specs=[SMEM1, SMEM1, SMEM1, whole((n,)), row(w), row(w), whole(ws.shape), whole((w,)), whole((w,)), whole((w,)), whole(wj.shape)],
        out_specs=[row(w), row(w), row(c), row(PAIR), row(PAIR), row(1)],
        out_shape=[
            jax.ShapeDtypeStruct((n, w), f32),
            jax.ShapeDtypeStruct((n, w), bf16),
            jax.ShapeDtypeStruct((n, c), bf16),
            jax.ShapeDtypeStruct((n, PAIR), bf16),
            jax.ShapeDtypeStruct((n, PAIR), bf16),
            jax.ShapeDtypeStruct((n, 1), f32),
        ],
        compiler_params=params(),
        cost_estimate=cost(2 * n * w * (2 * w + c), n * w * 20 + 5 * w * w * 2),
        name="front",
    )(lengths, gids, counts, keep, x, s, ws, bs, g, b, wj)


def half_mask(h):
    lane = lax.broadcasted_iota(jnp.int32, (1, PAIR), 1)
    return (lane < HEAD_DIM) if h == 0 else (lane >= HEAD_DIM)


def pieces(x):
    a = x.astype(bf16)
    r = x - a.astype(f32)
    b = r.astype(bf16)
    c = (r - b.astype(f32)).astype(bf16)
    return a, b, c


def attn_fwd_kernel(
    q_ref, k_ref, v_ref, qf_ref, kf_ref, cot_ref, tw_ref, o_ref, feat_ref, gr_ref, grt_ref, gsum_ref, ka_ref, vm_ref, s_ref, *, tq, per
):
    n = q_ref.shape[0]
    none = jnp.zeros((1, PAIR), bf16)
    one = jnp.ones((1, PAIR), bf16)
    lane = lax.broadcasted_iota(jnp.int32, (1, PAIR), 1)
    spare = [HEAD_DIM, 0]
    cols = [slice(d * PAIR, (d + 1) * PAIR) for d in range(per)]
    for d in range(per):
        ka_ref[d, :, :PAIR] = k_ref[:, cols[d]]
        ka_ref[d, :, PAIR:] = kf_ref[...]
        for h in range(2):
            vm_ref[d, h] = jnp.where(half_mask(h), v_ref[:, cols[d]], jnp.where(lane == spare[h], one, none))
    eye = eye_mask(PAIR)
    units = [(d, i, h) for d in range(per) for i in range(n // tq) for h in range(2)]

    def scores(u):
        d, i, h = units[u]
        rows = slice(i * tq, (i + 1) * tq)
        qm = jnp.where(half_mask(h), q_ref[rows, cols[d]] * jnp.asarray(HEAD_DIM**-0.5, bf16), none)
        slot = u % 2
        s_ref[slot] = mm(jnp.concatenate([qm, qf_ref[rows, :]], axis=1), ka_ref[d], NT)
        for j in range(tq // PAIR):
            a = slice(j * PAIR, (j + 1) * PAIR)
            c = slice(i * tq + j * PAIR, i * tq + (j + 1) * PAIR)
            s_ref[slot, a, c] = jnp.where(eye, mm(qm[a], k_ref[c, cols[d]], NT), s_ref[slot, a, c])

    scores(0)
    outs = [None, None]
    gsum = [None] * per
    for u, (d, i, h) in enumerate(units):
        if u + 1 < len(units):
            scores(u + 1)
        rows = slice(i * tq, (i + 1) * tq)
        s = s_ref[u % 2]
        top = jnp.max(s, axis=1, keepdims=True)
        pv = mm(jnp.exp(s - top).astype(bf16), vm_ref[d, h])
        total = pv[:, spare[h] : spare[h] + 1]
        outs[h] = pv / total
        a, b, c = pieces(-(top + jnp.log(total)))
        feat_ref[2 * d + h, rows, :] = jnp.where(
            lane == 5, a, jnp.where(lane == 6, b, jnp.where(lane == 7, c, qf_ref[rows, :]))
        )
        if h == 0:
            gr = (cot_ref[rows, cols[d]].astype(f32) * tw_ref[rows, :]).astype(bf16)
            gr_ref[rows, cols[d]] = gr
            grt_ref[cols[d], rows] = gr.T
            part = jnp.sum(gr.astype(f32), axis=0, keepdims=True)
            gsum[d] = part if i == 0 else gsum[d] + part
        else:
            o_ref[rows, cols[d]] = jnp.where(lane < HEAD_DIM, outs[0], outs[1]).astype(bf16)
    for d in range(per):
        gsum_ref[:, cols[d]] = gsum[d]


def attn_fwd(packed, qf, kf, cot, tw, tq=384, per=1):
    n, c = packed.shape
    w = c // 3
    pairs = w // PAIR
    wide = per * PAIR
    part = lambda p: pl.BlockSpec((n, wide), lambda j: (0, p * (pairs // per) + j))
    return pl.pallas_call(
        functools.partial(attn_fwd_kernel, tq=tq, per=per),
        grid=(pairs // per,),
        in_specs=[part(0), part(1), part(2), whole((n, PAIR)), whole((n, PAIR)), part(0), whole((n, 1))],
        out_specs=[
            pl.BlockSpec((n, wide), lambda j: (0, j)),
            pl.BlockSpec((2 * per, n, PAIR), lambda j: (j, 0, 0)),
            pl.BlockSpec((n, wide), lambda j: (0, j)),
            pl.BlockSpec((wide, n), lambda j: (j, 0)),
            pl.BlockSpec((1, wide), lambda j: (0, j)),
        ],
        out_shape=[
            jax.ShapeDtypeStruct((n, w), bf16),
            jax.ShapeDtypeStruct((2 * pairs, n, PAIR), bf16),
            jax.ShapeDtypeStruct((n, w), bf16),
            jax.ShapeDtypeStruct((w, n), bf16),
            jax.ShapeDtypeStruct((1, w), f32),
        ],
        scratch_shapes=[
            pltpu.VMEM((per, n, 2 * PAIR), bf16),
            pltpu.VMEM((per, 2, n, PAIR), bf16),
            pltpu.VMEM((2, tq, n), f32),
        ],
        compiler_params=params(),
        cost_estimate=cost(2 * n * n * (4 * PAIR) * pairs * 2, n * c * 4, n * n * 2 * pairs),
        name="attn_fwd",
    )(packed, packed, packed, qf, kf, cot, tw)


def attn_bwd_kernel(
    q_ref, k_ref, v_ref, o_ref, g_ref, feat_ref, kf_ref, out_ref, ka_ref, va_ref, qa_ref, ga_ref, kt_ref, dq_ref, st_ref, dp_ref,
    *, tk, live, per,
):
    n = q_ref.shape[0]
    lane = lax.broadcasted_iota(jnp.int32, (1, PAIR), 1)
    none = jnp.zeros((1, PAIR), bf16)
    scale = HEAD_DIM**-0.5
    cols = [slice(d * PAIR, (d + 1) * PAIR) for d in range(per)]

    def prepare(d):
        ka_ref[d, :, :PAIR] = k_ref[:, cols[d]]
        ka_ref[d, :, PAIR:] = kf_ref[...]
        va_ref[d, :, :PAIR] = v_ref[:, cols[d]]
        va_ref[d, :, PAIR:] = jnp.broadcast_to(jnp.where(lane < 3, 1.0, 0.0).astype(bf16), (n, PAIR))
        kt_ref[d] = k_ref[:, cols[d]].T
        q = q_ref[:, cols[d]] * jnp.asarray(scale, bf16)
        g = g_ref[:, cols[d]]
        prod = g.astype(f32) * o_ref[:, cols[d]].astype(f32)
        for h in range(2):
            own = half_mask(h)
            delta = jnp.sum(jnp.where(own, prod, 0.0), axis=1, keepdims=True)
            a, b, c = pieces(-delta)
            qa_ref[d, h, :, :PAIR] = jnp.where(own, q, none)
            qa_ref[d, h, :, PAIR:] = feat_ref[2 * d + h]
            ga_ref[d, h, :, :PAIR] = jnp.where(own, g, none)
            ga_ref[d, h, :, PAIR:] = jnp.where(lane == 0, a, jnp.where(lane == 1, b, jnp.where(lane == 2, c, none)))

    eye = eye_mask(PAIR)
    spans = [(i, min(i + tk, live)) for i in range(0, live, tk)]
    units = [(d, span, h) for d in range(per) for span in spans for h in range(2)]

    def scores(u):
        d, (lo, hi), h = units[u]
        size = hi - lo
        slot = u % 2
        st_ref[slot, :size] = mm(ka_ref[d, lo:hi, :], qa_ref[d, h], NT)
        for j in range(0, size, PAIR):
            t = min(PAIR, size - j)
            a = slice(j, j + t)
            r = slice(lo + j, lo + j + t)
            c = slice(lo + j, lo + j + PAIR)
            plain = jnp.concatenate([k_ref[r, cols[d]], jnp.where(lane < 5, none, kf_ref[r, :])], axis=1)
            st_ref[slot, a, c] = jnp.where(eye[:t], mm(plain, qa_ref[d, h, c, :], NT), st_ref[slot, a, c])
        dp_ref[slot, :size] = mm(va_ref[d, lo:hi, :], ga_ref[d, h], NT)

    prepare(0)
    scores(0)
    dv = [None, None]
    dk = [None, None]
    for u, (d, (lo, hi), h) in enumerate(units):
        if (lo, h) == (0, 0) and d + 1 < per:
            prepare(d + 1)
        if u + 1 < len(units):
            scores(u + 1)
        rows = slice(lo, hi)
        own = slice(h * HEAD_DIM, (h + 1) * HEAD_DIM)
        p = jnp.exp(st_ref[u % 2, : hi - lo])
        ds = (p * dp_ref[u % 2, : hi - lo]).astype(bf16)
        part = mm(kt_ref[d, own, rows], ds)
        if lo == 0:
            dq_ref[d, own, :] = part
        else:
            dq_ref[d, own, :] += part
        dv[h] = mm(p.astype(bf16), ga_ref[d, h, :, :PAIR])
        dk[h] = mm(ds, qa_ref[d, h, :, :PAIR])
        if h == 1:
            out_ref[1, rows, cols[d]] = (dk[0] + dk[1]).astype(bf16)
            out_ref[2, rows, cols[d]] = (dv[0] + dv[1]).astype(bf16)
            if hi == live:
                out_ref[0, :, cols[d]] = (dq_ref[d].T * scale).astype(bf16)
    if live < n:
        out_ref[1, live:, :] = jnp.zeros((n - live, per * PAIR), bf16)
        out_ref[2, live:, :] = jnp.zeros((n - live, per * PAIR), bf16)


def attn_bwd(packed, att, grad, feat, kf, tk=384, per=1):
    n, c = packed.shape
    w = c // 3
    pairs = w // PAIR
    wide = per * PAIR
    part = lambda p: pl.BlockSpec((n, wide), lambda j: (0, p * (pairs // per) + j))
    live = min(n, -(-ITEM_ROWS // 16) * 16)
    return pl.pallas_call(
        functools.partial(attn_bwd_kernel, tk=tk, live=live, per=per),
        grid=(pairs // per,),
        in_specs=[
            part(0),
            part(1),
            part(2),
            part(0),
            part(0),
            pl.BlockSpec((2 * per, n, PAIR), lambda j: (j, 0, 0)),
            whole((n, PAIR)),
        ],
        out_specs=pl.BlockSpec((3, n, wide), lambda j: (0, 0, j)),
        out_shape=jax.ShapeDtypeStruct((3, n, w), bf16),
        scratch_shapes=[
            pltpu.VMEM((per, n, 2 * PAIR), bf16),
            pltpu.VMEM((per, n, 2 * PAIR), bf16),
            pltpu.VMEM((per, 2, n, 2 * PAIR), bf16),
            pltpu.VMEM((per, 2, n, 2 * PAIR), bf16),
            pltpu.VMEM((per, PAIR, n), bf16),
            pltpu.VMEM((per, PAIR, n), f32),
            pltpu.VMEM((2, tk, n), f32),
            pltpu.VMEM((2, tk, n), f32),
        ],
        compiler_params=params(),
        cost_estimate=cost(2 * n * n * (9 * PAIR) * pairs * 2, n * c * 8, n * n * 2 * pairs),
        name="attn_bwd",
    )(packed, packed, packed, att, grad, feat, kf)


def normal_cdf_pdf(u):
    a = jnp.abs(u)
    t = 1.0 / (1.0 + a * (0.3275911 * 0.7071067811865476))
    e = jnp.exp(-0.5 * u * u)
    half = 0.5
    poly = t * (
        half * 0.254829592
        + t * (half * -0.284496736 + t * (half * 1.421413741 + t * (half * -1.453152027 + t * (half * 1.061405429))))
    )
    tail = poly * e
    return jnp.where(u < 0, tail, 1.0 - tail), e * 0.3989422804014327


def ff_fwd_kernel(
    core_ref, a_ref, hid_ref, wo_ref, bo_ref, g_ref, b_ref, grt_ref, w1_ref, b1_ref,
    mid_out, n2_out, act_ref, slope_ref, *rest, m, order, sub, count, rb,
):
    refs, (mid_ref, n2_ref, sems) = rest[:count], rest[count:]
    n = a_ref.shape[0]
    step = pl.program_id(0)
    copies = [pltpu.make_async_copy(mid_ref, mid_out, sems.at[0]), pltpu.make_async_copy(n2_ref, n2_out, sems.at[1])]

    @pl.when(step == 0)
    def _():
        parts = [slice(lo, lo + rb) for lo in range(0, n, rb)]
        project = lambda r: mm(a_ref[r, :], wo_ref[...])
        ahead = project(parts[0])
        for i, r in enumerate(parts):
            mid = hid_ref[r, :] + ahead + line(bo_ref)
            if i + 1 < len(parts):
                ahead = project(parts[i + 1])
            mid_ref[r, :] = mid
            std, _ = row_stats(mid)
            n2_ref[r, :] = (std * line(g_ref) + line(b_ref)).astype(bf16)
        for c in copies:
            c.start()

    fc = w1_ref.shape[1]
    bias = line(b1_ref)
    cut = lambda s: slice(s * sub, (s + 1) * sub)
    before = lambda s: mm(n2_ref[...], w1_ref[:, cut(s)]) + bias[:, cut(s)]
    ahead = before(0)
    for s in range(fc // sub):
        pre = ahead
        if s + 1 < fc // sub:
            ahead = before(s + 1)
        cdf, pdf = normal_cdf_pdf(pre)
        act = (pre * cdf).astype(bf16)
        slope_ref[:, cut(s)] = (cdf + pre * pdf).astype(bf16)
        act_ref[:, cut(s)] = act
        views = [r.at[:, :, cut(s)] if count == 2 else r.at[:, cut(s)] for r in refs]
        put(mm(grt_ref[...], act), views, core_ref[0], m, order)

    @pl.when(step == pl.num_programs(0) - 1)
    def _():
        for c in copies:
            c.wait()


def ff_fwd(core, dp, att, hid, wo, bo, g, b, grt, w1, b1, fc=1024, sub=256):
    n, w = att.shape
    ff = w1.shape[1]
    m = w // dp
    if can_split(w, m):
        specs = [pl.BlockSpec((dp // 2, m, fc), lambda i: (0, i, 0))] * 2
        shapes = [jax.ShapeDtypeStruct((dp // 2, ff // fc * m, fc), f32)] * 2
    else:
        specs = [pl.BlockSpec((w, fc), lambda i: (0, i))]
        shapes = [jax.ShapeDtypeStruct((w, ff), f32)]
    left = pl.BlockSpec(memory_space=pl.ANY)
    res = pl.pallas_call(
        functools.partial(ff_fwd_kernel, m=m, order=ring_order(dp), sub=sub, count=len(specs), rb=n // 3),
        grid=(ff // fc,),
        in_specs=[
            SMEM1,
            whole((n, w)),
            whole((n, w)),
            whole((w, w)),
            whole((w,)),
            whole((w,)),
            whole((w,)),
            whole((w, n)),
            pl.BlockSpec((w, fc), lambda i: (0, i)),
            pl.BlockSpec((fc,), lambda i: (i,)),
        ],
        out_specs=[left, left] + [pl.BlockSpec((n, fc), lambda i: (0, i))] * 2 + specs,
        out_shape=[
            jax.ShapeDtypeStruct((n, w), f32),
            jax.ShapeDtypeStruct((n, w), bf16),
            jax.ShapeDtypeStruct((n, ff), bf16),
            jax.ShapeDtypeStruct((n, ff), bf16),
        ]
        + shapes,
        scratch_shapes=[pltpu.VMEM((n, w), f32), pltpu.VMEM((n, w), bf16), pltpu.SemaphoreType.DMA((2,))],
        compiler_params=params(60),
        cost_estimate=cost(6 * n * w * ff, n * w * 10 + ff * w * 8 + n * ff * 2, n * ff * 2),
        name="ff_fwd",
    )(core, att, hid, wo, bo, g, b, grt, w1, b1)
    return res[0], res[1], res[2], res[3], res[4:]


def ff_bwd_kernel(core_ref, n2_ref, gr_ref, w1a_ref, w1b_ref, sla_ref, slb_ref, w2a_ref, w2b_ref, *rest, first, count, m):
    gn_ref, db1_ref = rest[-2 - count : -count]
    refs = rest[-count:]
    side = lambda a, b: jnp.concatenate([a[...], b[...]], axis=1)
    w1 = side(w1a_ref, w1b_ref)
    w2 = jnp.concatenate([w2a_ref[...], w2b_ref[...]], axis=0)
    gpre = (mm(gr_ref[...], w2, NT) * side(sla_ref, slb_ref).astype(f32)).astype(bf16)

    @pl.when(pl.program_id(0) == 0)
    def _():
        gn_ref[...] = jnp.zeros_like(gn_ref) if first else rest[0][...]

    gn_ref[...] += mm(gpre, w1, NT)
    put(mm(gpre, n2_ref[...], TN), refs, core_ref[0], m)
    db1_ref[...] = jnp.sum(gpre.astype(f32), axis=0, keepdims=True)


def ff_bwd(core, dp, n2, gr, w1, slope, w2, base, steps, prev):
    n, w = n2.shape
    ff = w1.shape[1]
    m = ff // dp
    fc = 384
    ring = can_split(fc, m) and fc == 2 * m and dp == 16
    total = ff // (2 * fc)
    steps = total - base if steps is None else steps
    if ring:
        near = lambda i: jnp.where(base + i < 2, 4 * (base + i), 15 - 4 * (base + i))
        far = lambda i: jnp.where(base + i < 2, 4 * (base + i) + 2, 13 - 4 * (base + i))
        specs = [pl.BlockSpec((2, m, w), lambda i: (base + i, 0, 0))] * 2
        shapes = [jax.ShapeDtypeStruct((dp // 2, m, w), f32)] * 2
    else:
        near = lambda i: 2 * (base + i)
        far = lambda i: 2 * (base + i) + 1
        specs = [pl.BlockSpec((2 * fc, w), lambda i: (base + i, 0))]
        shapes = [jax.ShapeDtypeStruct((ff, w), f32)]
    extra = [] if prev is None else list(prev)
    res = pl.pallas_call(
        functools.partial(ff_bwd_kernel, first=prev is None, count=len(specs), m=m),
        grid=(steps,),
        in_specs=[
            SMEM1,
            whole((n, w)),
            whole((n, w)),
            pl.BlockSpec((w, fc), lambda i: (0, near(i))),
            pl.BlockSpec((w, fc), lambda i: (0, far(i))),
            pl.BlockSpec((n, fc), lambda i: (0, near(i))),
            pl.BlockSpec((n, fc), lambda i: (0, far(i))),
            pl.BlockSpec((fc, w), lambda i: (near(i), 0)),
            pl.BlockSpec((fc, w), lambda i: (far(i), 0)),
        ]
        + ([whole((n, w))] + [pl.BlockSpec(memory_space=pl.ANY)] * len(specs) if extra else []),
        out_specs=[whole((n, w)), pl.BlockSpec((1, 2 * fc), lambda i: (0, i))] + specs,
        out_shape=[jax.ShapeDtypeStruct((n, w), f32), jax.ShapeDtypeStruct((1, 2 * fc * steps), f32)] + shapes,
        input_output_aliases={10 + k: 2 + k for k in range(len(specs))} if extra else {},
        compiler_params=params(60),
        cost_estimate=cost(12 * n * w * fc * steps, n * w * 10 + fc * steps * w * 16 + n * fc * steps * 4),
        name="ff_bwd",
    )(core, n2, gr, w1, w1, slope, slope, w2, w2, *extra)
    return (res[0], *res[2:]), res[1]


def back_kernel(core_ref, mid_ref, gn_ref, cot_ref, tw_ref, a_ref, wo_ref, g_ref, *rest, m, count, order, sub):
    gm_ref, ga_ref, vec_ref = rest[-4 - count : -1 - count]
    dwo_refs, dwo_ref = rest[-1 - count : -1], rest[-1]
    rb, w = mid_ref.shape
    step = pl.program_id(0)
    add = lambda x: jnp.sum(x, axis=0, keepdims=True)
    parts = [slice(lo, lo + sub) for lo in range(0, rb, sub)]

    @pl.when(step == 0)
    def _():
        dwo_ref[...] = jnp.zeros_like(dwo_ref)
        vec_ref[...] = jnp.zeros_like(vec_ref)

    def norm_part(r):
        mid = mid_ref[r, :]
        std, inv = row_stats(mid)
        gn = gn_ref[r, :]
        gm = cot_ref[r, :].astype(f32) * tw_ref[r, :] + norm_back(gn, std, inv, line(g_ref))
        gm_ref[r, :] = gm
        gb = gm.astype(bf16)
        vec_ref[...] += jnp.concatenate([add(gb.astype(f32)), add(gn * std), add(gn), jnp.zeros((1, w), f32)], axis=0)
        return gb

    ahead = norm_part(parts[0])
    for i, r in enumerate(parts):
        gb = ahead
        if i + 1 < len(parts):
            ahead = norm_part(parts[i + 1])
        ga_ref[r, :] = mm(gb, wo_ref[...], NT).astype(bf16)
        dwo_ref[...] += mm(gb, a_ref[r, :], TN)

    @pl.when(step == pl.num_programs(0) - 1)
    def _():
        put(dwo_ref[...], dwo_refs, core_ref[0], m, order)


def grad_outs(rows, cols, m):
    if can_split(rows, m):
        shape = (rows // (2 * m), m, cols)
        return [whole(shape)] * 2, [jax.ShapeDtypeStruct(shape, f32)] * 2
    return [whole((rows, cols))], [jax.ShapeDtypeStruct((rows, cols), f32)]


def back_part(core, dp, mid, gn, cot, tw, att, wo, g, rb, sub=384):
    n, w = mid.shape
    row = lambda cols: pl.BlockSpec((rb, cols), lambda i: (i, 0))
    mo, mj = w // dp, 3 * w // dp
    if can_split(w, mo) and can_split(3 * w, mj):
        specs = [pl.BlockSpec((dp // 2, mo, w), lambda i: (0, mj // mo, 0))] * 2
        shapes = [jax.ShapeDtypeStruct((dp // 2, mj + mo, w), f32)] * 2
    else:
        specs, shapes = [whole((w, w))], [jax.ShapeDtypeStruct((w, w), f32)]
    res = pl.pallas_call(
        functools.partial(back_kernel, m=mo, count=len(specs), order=ring_order(dp), sub=sub),
        grid=(n // rb,),
        in_specs=[SMEM1, row(w), row(w), row(w), row(1), row(w), whole(wo.shape), whole((w,))],
        out_specs=[row(w), row(w), whole((4, w))] + specs,
        out_shape=[
            jax.ShapeDtypeStruct((n, w), f32),
            jax.ShapeDtypeStruct((n, w), bf16),
            jax.ShapeDtypeStruct((4, w), f32),
        ]
        + shapes,
        scratch_shapes=[pltpu.VMEM((w, w), f32)],
        compiler_params=params(),
        cost_estimate=cost(4 * n * w * w, n * w * 28),
        name="back_part",
    )(core, mid, gn, cot, tw, att, wo, g)
    return res[0], res[1], res[2], res[3:]


def finish_kernel(mid_ref, act_ref, w2_ref, b2_ref, out_ref):
    out_ref[...] = (mid_ref[...] + mm(act_ref[...], w2_ref[...]) + line(b2_ref)).astype(bf16)


def finish(mid, act, w2, b2, rb):
    n, w = mid.shape
    row = lambda cols: pl.BlockSpec((rb, cols), lambda i: (i, 0))
    return pl.pallas_call(
        finish_kernel,
        grid=(n // rb,),
        in_specs=[row(w), row(act.shape[1]), whole(w2.shape), whole((w,))],
        out_specs=row(w),
        out_shape=jax.ShapeDtypeStruct((n, w), bf16),
        compiler_params=params(),
        cost_estimate=cost(2 * n * w * act.shape[1], n * w * 14),
        name="finish",
    )(mid, act, w2, b2)


def joint_grad_kernel(core_ref, gp_ref, n1_ref, *rest, m, count, order):
    refs, gpt_ref = rest[-1 - count : -1], rest[-1]
    parts, n, w = gp_ref.shape

    @pl.when(pl.program_id(0) == 0)
    def _():
        for p in range(parts):
            gpt_ref[p * w : (p + 1) * w, :] = gp_ref[p].T

    put(mm(gpt_ref[...], n1_ref[...]), refs, core_ref[0], m, order)


def grad_block(rows, cols, cb, m):
    if can_split(rows, m):
        spec = pl.BlockSpec((rows // (2 * m), m, cb), lambda j: (0, 0, j))
        return [spec] * 2, [jax.ShapeDtypeStruct((rows // (2 * m), m, cols), f32)] * 2
    return [pl.BlockSpec((rows, cb), lambda j: (0, j))], [jax.ShapeDtypeStruct((rows, cols), f32)]


def joint_grad(core, dp, gp, n1, into, cb=256):
    parts, n, w = gp.shape
    m = parts * w // dp
    specs, shapes = grad_block(parts * w, w, cb, m)
    if len(into) == 2:
        shapes = [jax.ShapeDtypeStruct(x.shape, f32) for x in into]
    else:
        into = []
    return pl.pallas_call(
        functools.partial(joint_grad_kernel, m=m, count=len(specs), order=ring_order(dp)),
        grid=(w // cb,),
        in_specs=[SMEM1, whole((parts, n, w)), pl.BlockSpec((n, cb), lambda j: (0, j))]
        + [pl.BlockSpec(memory_space=pl.ANY)] * len(into),
        out_specs=specs,
        out_shape=shapes,
        input_output_aliases={3 + k: k for k in range(len(into))},
        scratch_shapes=[pltpu.VMEM((parts * w, n), bf16)],
        compiler_params=params(),
        cost_estimate=cost(2 * parts * n * w * w, n * w * 8 + parts * w * w * 4),
        name="joint_grad",
    )(core, gp, n1, *into)


def tail_kernel(gp_ref, hid_ref, gm_ref, wj_ref, g_ref, gh_ref, vec_ref, *, sub):
    rb, w = hid_ref.shape
    parts = [slice(lo, lo + sub) for lo in range(0, rb, sub)]
    add = lambda x: jnp.sum(x, axis=0, keepdims=True)

    def project(r):
        return sum(mm(gp_ref[p, r, :], wj_ref[:, p * w : (p + 1) * w], NT) for p in range(3))

    ahead = project(parts[0])
    vec = jnp.zeros((4, w), f32)
    for i, r in enumerate(parts):
        gn = ahead
        if i + 1 < len(parts):
            ahead = project(parts[i + 1])
        std, inv = row_stats(hid_ref[r, :])
        gh = (gm_ref[r, :] + norm_back(gn, std, inv, line(g_ref))).astype(bf16)
        gh_ref[r, :] = gh
        vec = vec + jnp.concatenate([add(gn * std), add(gn), add(gh.astype(f32)), jnp.zeros((1, w), f32)], axis=0)
    step = pl.program_id(0)

    @pl.when(step == 0)
    def _():
        vec_ref[...] = vec

    @pl.when(step > 0)
    def _():
        vec_ref[...] += vec


def tail_part(gp, hid, gm, wj, g, rb, sub=384):
    n, w = hid.shape
    row = lambda cols: pl.BlockSpec((rb, cols), lambda i: (i, 0))
    return pl.pallas_call(
        functools.partial(tail_kernel, sub=sub),
        grid=(n // rb,),
        in_specs=[pl.BlockSpec((3, rb, w), lambda i: (0, i, 0)), row(w), row(w), whole(wj.shape), whole((w,))],
        out_specs=[row(w), whole((4, w))],
        out_shape=[jax.ShapeDtypeStruct((n, w), bf16), jax.ShapeDtypeStruct((4, w), f32)],
        compiler_params=params(),
        cost_estimate=cost(6 * n * w * w, n * w * 16),
        name="tail_part",
    )(gp, hid, gm, wj, g)


def skip_grad_kernel(core_ref, gh_ref, x_ref, s_ref, vec_ref, *refs, m, order):
    ght = gh_ref[...].T
    val = jnp.concatenate([mm(ght, x_ref[...]), mm(ght, s_ref[...]), vec_ref[...]], axis=1)
    put(val, refs, core_ref[0], m, order)


def skip_grad(core, dp, gh, x, s, vec):
    n, w = gh.shape
    m = w // dp
    cols = 2 * w + vec.shape[1]
    specs, shapes = grad_block(w, cols, cols, m)
    return pl.pallas_call(
        functools.partial(skip_grad_kernel, m=m, order=ring_order(dp)),
        grid=(1,),
        in_specs=[SMEM1, whole((n, w)), whole((n, w)), whole((n, w)), whole(vec.shape)],
        out_specs=specs,
        out_shape=shapes,
        compiler_params=params(),
        cost_estimate=cost(4 * n * w * w, n * w * 6 + w * w * 8),
        name="skip_grad",
    )(core, gh, x, s, vec)


def in_grad_kernel(gh_ref, ws_ref, a_ref, b_ref):
    w = a_ref.shape[1]
    gh = gh_ref[...]
    a_ref[...] = mm(gh, ws_ref[:w, :], NT).astype(bf16)
    b_ref[...] = mm(gh, ws_ref[w:, :], NT).astype(bf16)


def in_grad(gh, ws, rb):
    n, w = gh.shape
    row = lambda cols: pl.BlockSpec((rb, cols), lambda i: (i, 0))
    return pl.pallas_call(
        in_grad_kernel,
        grid=(n // rb,),
        in_specs=[row(w), whole(ws.shape)],
        out_specs=[row(w), row(w)],
        out_shape=[jax.ShapeDtypeStruct((n, w), bf16)] * 2,
        compiler_params=params(),
        cost_estimate=cost(4 * n * w * w, n * w * 10),
        name="in_grad",
    )(gh, ws)


def pick(x, axis, index):
    return lax.dynamic_index_in_dim(x, index, axis, keepdims=False)


def swap(x, axis, bit=0):
    size = lax.axis_size(axis)
    return lax.ppermute(x, axis, [(i, i ^ (1 << bit)) for i in range(size)])


def pair_terms(refs, cols, dp):
    if len(refs) == 1:
        full = refs[0].reshape(dp // 2, 2, -1, cols)
        core = lax.axis_index("dp") & 1
        refs = [pick(full, 1, core), pick(full, 1, 1 - core)]
    return [refs[0], swap(refs[1], "dp")]


def both_sides(x, side):
    other = swap(x, "rep")
    return jnp.concatenate([jnp.where(side == 0, x, other), jnp.where(side == 0, other, x)], axis=0)


def tie(x, y):
    return lax.optimization_barrier((x, y))


def per_device(*args):
    (inputs, skips, cot, lengths, keep, group_ids, group_counts, ws, bs, g1, s1, wj, wo, bo, g2, s2, w1, b1, w2, b2) = args
    n, w = inputs.shape
    ff = w1.shape[1]
    dp = lax.axis_size("dp")
    tokens_total = n * dp * lax.axis_size("rep")
    scale = float(tokens_total) ** -0.5
    side = lax.axis_index("rep")
    core = (lax.axis_index("dp") & 1).astype(jnp.int32).reshape(1)
    rb = n // 3
    ring = ring_order(dp)
    groups = [[2 * i + c for i in ring] for c in range(2)]
    ring_sum = lambda h: lax.psum_scatter(h, "dp", scatter_dimension=0, tiled=True, axis_index_groups=groups)[0]
    over_rep = lambda h: h + swap(h, "rep")

    hid, n1, packed, qf, kf, tw = front(
        lengths, group_ids, group_counts, keep, inputs, skips, ws, bs, g1, s1, wj, rb, tokens_total // group_counts.shape[0]
    )
    att, feat, gr, grt, gsum = attn_fwd(packed, qf, kf, cot, tw)
    mid, n2, act, slope, d2 = ff_fwd(core, dp, att, hid, wo, bo, g2, s2, grt, w1, b1)
    half2 = sum(pair_terms(d2, ff, dp))
    carry, db0 = ff_bwd(core, dp, n2, gr, w1, slope, w2, 0, 1, None)
    carry, half2 = tie(carry, half2)
    carry, db1 = ff_bwd(core, dp, n2, gr, w1, slope, w2, 1, None, carry)
    gn2, d1 = carry[0], carry[1:]
    gm, gatt, vec2, do = back_part(core, dp, mid, gn2, cot, tw, att, wo, g2, rb)
    half1 = sum(pair_terms(d1, w, dp))
    gatt, half1 = tie(gatt, half1)
    sum2 = ring_sum(half2)
    sum1 = ring_sum(half1)

    gp = attn_bwd(packed, att, gatt, feat, kf)
    gp, sum2 = tie(gp, sum2)
    got2 = swap(sum2, "rep")

    dj = joint_grad(core, dp, gp, n1, do)
    gp, dj = tie(gp, dj)
    if len(dj) == 2:
        halfj = sum(pair_terms(dj, w, dp))
    else:
        full = jnp.concatenate([dj[0].reshape(dp, 3 * w // dp, w), do[0].reshape(dp, w // dp, w)], axis=1)
        halfj = sum(pair_terms([full.reshape(-1, w)], w, dp))
    gh, vec1 = tail_part(gp, hid, gm, wj, g1, rb)
    gh, halfj, sum1, got2 = lax.optimization_barrier((gh, halfj, sum1, got2))
    sumj = ring_sum(halfj)
    db = jnp.concatenate([db0, db1], axis=1).reshape(8, ff // 8)
    if len(d1) == 2:
        db = jnp.stack([db[ring.index(i)] for i in range(8)])
    db = db.reshape(w, ff // w)
    vec = jnp.concatenate([vec1.T, vec2[:3].T, gsum.T, db, jnp.zeros((w, PAIR - 8 - ff // w), f32)], axis=1)
    cols = 2 * w + PAIR
    ds = skip_grad(core, dp, gh, inputs, skips, vec)
    terms = [t.reshape(dp // 2, 2, -1, cols) for t in pair_terms(ds, cols, dp)]
    send = sum(pick(t, 1, 1 - side) for t in terms)
    gh, send = tie(gh, send)
    igrad, sgrad = in_grad(gh, ws, rb)
    act, igrad = tie(act, igrad)
    outcome = finish(mid, act, w2, b2, rb)
    halfs = sum(pick(t, 1, side) for t in terms) + swap(send, "rep")
    halfs, sumj, sum1, outcome, sgrad = lax.optimization_barrier((halfs, sumj, sum1, outcome, sgrad))
    sums = ring_sum(halfs)
    out2 = sum2 + got2
    out1 = over_rep(sum1)
    outj = over_rep(sumj)
    if len(d2) == 2:
        out2 = out2.reshape(-1, w // dp, 1024).transpose(1, 0, 2).reshape(w // dp, ff)
    outj, outo = outj[: 3 * w // dp], outj[3 * w // dp :]
    outs = both_sides(sums, side)

    ds, dj, do, d1, d2 = [m.T * scale for m in (outs[:, : 2 * w], outj, outo, out1, out2)]
    v = outs[:, 2 * w :] * scale
    col = lambda i: v[:, i]
    db1 = v[:, 8 : 8 + ff // w].reshape(-1)
    return (
        outcome, igrad, sgrad, ds, col(2), col(0), col(1), dj, do, col(4), col(5), col(6), d1, db1, d2, col(7),
    )


def solution(mesh):
    both = ("dp", "rep")
    in_specs = (P(both, None),) * 3 + (P(both),) * 3 + (P(),) * 14
    cols = P(None, "dp")
    vec = P("dp")
    out_specs = (P(both, None),) * 3 + (cols, vec, vec, vec, cols, cols, vec, vec, vec, cols, vec, cols, vec)
    return jax.shard_map(per_device, mesh=mesh, in_specs=in_specs, out_specs=out_specs, check_vma=False)
```

```python
import functools

import jax
import jax.numpy as jnp
from jax import lax
from jax.experimental import pallas as pl
from jax.experimental.pallas import tpu as pltpu
from jax.sharding import PartitionSpec as P

HEAD_DIM = 64
PAIR = 2 * HEAD_DIM
EPS = 1e-05
BIG = 1e30
ITEM_ROWS = 1028
f32 = jnp.float32
bf16 = jnp.bfloat16
NT = (((1,), (1,)), ((), ()))
NN = (((1,), (0,)), ((), ()))
TN = (((0,), (0,)), ((), ()))


def mm(a, b, dims=NN):
    return lax.dot_general(a, b, dims, preferred_element_type=f32)


def params(mb=56):
    return pltpu.CompilerParams(vmem_limit_bytes=mb << 20)


def cost(flops, nbytes, trans=0):
    return pl.CostEstimate(flops=int(flops), bytes_accessed=int(nbytes), transcendentals=int(trans))


def whole(shape):
    return pl.BlockSpec(shape, lambda *_: (0,) * len(shape), pipeline_mode=pl.Buffered(1))


def row_stats(x):
    mean = jnp.mean(x, axis=1, keepdims=True)
    cen = x - mean
    inv = lax.rsqrt(jnp.mean(cen * cen, axis=1, keepdims=True) + EPS)
    return cen * inv, inv


def norm_back(g, std, inv, gain):
    e = g * gain
    return inv * (e - jnp.mean(e, axis=1, keepdims=True) - std * jnp.mean(e * std, axis=1, keepdims=True))


def can_split(rows, m):
    return m % 8 == 0 and rows % (2 * m) == 0


def ring_order(dp):
    if dp != 16:
        return list(range(dp // 2))
    return [2 * z for z in range(4)] + [2 * z + 1 for z in reversed(range(4))]


def split_store(val, refs, core, m, order=None):
    rows, cols = val.shape
    parts = val.reshape(rows // (2 * m), 2, m, cols)
    low, high = parts[:, 0], parts[:, 1]
    keep = jnp.where(core == 0, low, high)
    send = jnp.where(core == 0, high, low)
    if order is None:
        refs[0][...] = keep
        refs[1][...] = send
    else:
        for place, owner in enumerate(order):
            refs[0][place] = keep[owner]
            refs[1][place] = send[owner]


def put(val, refs, core, m, order=None):
    if len(refs) == 2:
        split_store(val, refs, core, m, order)
    else:
        refs[0][...] = val


SMEM1 = pl.BlockSpec(memory_space=pltpu.SMEM)


def eye_mask(t):
    return lax.broadcasted_iota(jnp.int32, (t, t), 0) == lax.broadcasted_iota(jnp.int32, (t, t), 1)


def line(ref):
    return ref[...].astype(f32).reshape(1, -1)


def front_kernel(
    len_ref, gid_ref, cnt_ref, keep_ref, x_ref, s_ref, ws_ref, bs_ref, g_ref, b_ref, wj_ref,
    hid_ref, n1_ref, q_ref, qf_ref, kf_ref, tw_ref, *, group_tokens, sub,
):
    rb, w = x_ref.shape

    def project(r):
        return mm(x_ref[r, :], ws_ref[:w, :]) + mm(s_ref[r, :], ws_ref[w:, :]) + line(bs_ref)

    parts = [slice(lo, lo + sub) for lo in range(0, rb, sub)]
    ahead = project(parts[0])
    for i, r in enumerate(parts):
        hid = ahead
        if i + 1 < len(parts):
            ahead = project(parts[i + 1])
        hid_ref[r, :] = hid
        std, _ = row_stats(hid)
        n1 = (std * line(g_ref) + line(b_ref)).astype(bf16)
        n1_ref[r, :] = n1
        q_ref[r, :] = mm(n1, wj_ref[...]).astype(bf16)

    slots = len_ref.shape[0]
    base = pl.program_id(0) * rb
    lane = lax.broadcasted_iota(jnp.int32, (1, PAIR), 1)
    pos = lax.broadcasted_iota(jnp.int32, (rb, 1), 0) + base
    segment = jnp.zeros((rb, 1), jnp.int32)
    count = jnp.ones((1, PAIR), f32)
    end = 0
    for i in range(slots):
        end = end + len_ref[i]
        segment = segment + (pos >= end).astype(jnp.int32)
        count = jnp.where(lane == i, cnt_ref[gid_ref[i]].astype(f32), count)
    same = segment == lane
    weight = jnp.where(lane < slots, group_tokens / count, 0.0)
    tw_ref[...] = jnp.sum(jnp.where(same, weight, 0.0), axis=1, keepdims=True)
    qf_ref[...] = jnp.where(same, 1.0, 0.0).astype(bf16)
    eye = eye_mask(PAIR)
    for t in range(rb // PAIR):
        rows = slice(t * PAIR, (t + 1) * PAIR)
        keep = keep_ref[pl.ds(pl.multiple_of(base + t * PAIR, PAIR), PAIR)].astype(f32).reshape(1, PAIR)
        kept = jnp.sum(jnp.where(eye, keep, 0.0), axis=1, keepdims=True) == 1.0
        bias = jnp.where(same[rows] & kept, 0.0, -BIG)
        kf_ref[rows, :] = jnp.where(lane <= slots, bias, jnp.where(lane < slots + 4, 1.0, 0.0)).astype(bf16)


def front(lengths, gids, counts, keep, x, s, ws, bs, g, b, wj, rb, group_tokens, sub=192):
    n, w = x.shape
    c = wj.shape[1]
    row = lambda cols: pl.BlockSpec((rb, cols), lambda i: (i, 0))
    return pl.pallas_call(
        functools.partial(front_kernel, group_tokens=float(group_tokens), sub=sub),
        grid=(n // rb,),
        in_specs=[SMEM1, SMEM1, SMEM1, whole((n,)), row(w), row(w), whole(ws.shape), whole((w,)), whole((w,)), whole((w,)), whole(wj.shape)],
        out_specs=[row(w), row(w), row(c), row(PAIR), row(PAIR), row(1)],
        out_shape=[
            jax.ShapeDtypeStruct((n, w), f32),
            jax.ShapeDtypeStruct((n, w), bf16),
            jax.ShapeDtypeStruct((n, c), bf16),
            jax.ShapeDtypeStruct((n, PAIR), bf16),
            jax.ShapeDtypeStruct((n, PAIR), bf16),
            jax.ShapeDtypeStruct((n, 1), f32),
        ],
        compiler_params=params(),
        cost_estimate=cost(2 * n * w * (2 * w + c), n * w * 20 + 5 * w * w * 2),
        name="front",
    )(lengths, gids, counts, keep, x, s, ws, bs, g, b, wj)


def half_mask(h):
    lane = lax.broadcasted_iota(jnp.int32, (1, PAIR), 1)
    return (lane < HEAD_DIM) if h == 0 else (lane >= HEAD_DIM)


def pieces(x):
    a = x.astype(bf16)
    r = x - a.astype(f32)
    b = r.astype(bf16)
    c = (r - b.astype(f32)).astype(bf16)
    return a, b, c


def attn_fwd_kernel(
    q_ref, k_ref, v_ref, qf_ref, kf_ref, cot_ref, tw_ref, o_ref, feat_ref, gr_ref, grt_ref, gsum_ref, ka_ref, vm_ref, s_ref, *, tq, per
):
    n = q_ref.shape[0]
    none = jnp.zeros((1, PAIR), bf16)
    one = jnp.ones((1, PAIR), bf16)
    lane = lax.broadcasted_iota(jnp.int32, (1, PAIR), 1)
    spare = [HEAD_DIM, 0]
    cols = [slice(d * PAIR, (d + 1) * PAIR) for d in range(per)]
    for d in range(per):
        ka_ref[d, :, :PAIR] = k_ref[:, cols[d]]
        ka_ref[d, :, PAIR:] = kf_ref[...]
        for h in range(2):
            vm_ref[d, h] = jnp.where(half_mask(h), v_ref[:, cols[d]], jnp.where(lane == spare[h], one, none))
    eye = eye_mask(PAIR)
    units = [(d, i, h) for d in range(per) for i in range(n // tq) for h in range(2)]

    def scores(u):
        d, i, h = units[u]
        rows = slice(i * tq, (i + 1) * tq)
        qm = jnp.where(half_mask(h), q_ref[rows, cols[d]] * jnp.asarray(HEAD_DIM**-0.5, bf16), none)
        slot = u % 2
        s_ref[slot] = mm(jnp.concatenate([qm, qf_ref[rows, :]], axis=1), ka_ref[d], NT)
        for j in range(tq // PAIR):
            a = slice(j * PAIR, (j + 1) * PAIR)
            c = slice(i * tq + j * PAIR, i * tq + (j + 1) * PAIR)
            s_ref[slot, a, c] = jnp.where(eye, mm(qm[a], k_ref[c, cols[d]], NT), s_ref[slot, a, c])

    scores(0)
    outs = [None, None]
    gsum = [None] * per
    for u, (d, i, h) in enumerate(units):
        if u + 1 < len(units):
            scores(u + 1)
        rows = slice(i * tq, (i + 1) * tq)
        s = s_ref[u % 2]
        top = jnp.max(s, axis=1, keepdims=True)
        pv = mm(jnp.exp(s - top).astype(bf16), vm_ref[d, h])
        total = pv[:, spare[h] : spare[h] + 1]
        outs[h] = pv / total
        a, b, c = pieces(-(top + jnp.log(total)))
        feat_ref[2 * d + h, rows, :] = jnp.where(
            lane == 5, a, jnp.where(lane == 6, b, jnp.where(lane == 7, c, qf_ref[rows, :]))
        )
        if h == 0:
            gr = (cot_ref[rows, cols[d]].astype(f32) * tw_ref[rows, :]).astype(bf16)
            gr_ref[rows, cols[d]] = gr
            grt_ref[cols[d], rows] = gr.T
            part = jnp.sum(gr.astype(f32), axis=0, keepdims=True)
            gsum[d] = part if i == 0 else gsum[d] + part
        else:
            o_ref[rows, cols[d]] = jnp.where(lane < HEAD_DIM, outs[0], outs[1]).astype(bf16)
    for d in range(per):
        gsum_ref[:, cols[d]] = gsum[d]


def attn_fwd(packed, qf, kf, cot, tw, tq=384, per=1):
    n, c = packed.shape
    w = c // 3
    pairs = w // PAIR
    wide = per * PAIR
    part = lambda p: pl.BlockSpec((n, wide), lambda j: (0, p * (pairs // per) + j))
    return pl.pallas_call(
        functools.partial(attn_fwd_kernel, tq=tq, per=per),
        grid=(pairs // per,),
        in_specs=[part(0), part(1), part(2), whole((n, PAIR)), whole((n, PAIR)), part(0), whole((n, 1))],
        out_specs=[
            pl.BlockSpec((n, wide), lambda j: (0, j)),
            pl.BlockSpec((2 * per, n, PAIR), lambda j: (j, 0, 0)),
            pl.BlockSpec((n, wide), lambda j: (0, j)),
            pl.BlockSpec((wide, n), lambda j: (j, 0)),
            pl.BlockSpec((1, wide), lambda j: (0, j)),
        ],
        out_shape=[
            jax.ShapeDtypeStruct((n, w), bf16),
            jax.ShapeDtypeStruct((2 * pairs, n, PAIR), bf16),
            jax.ShapeDtypeStruct((n, w), bf16),
            jax.ShapeDtypeStruct((w, n), bf16),
            jax.ShapeDtypeStruct((1, w), f32),
        ],
        scratch_shapes=[
            pltpu.VMEM((per, n, 2 * PAIR), bf16),
            pltpu.VMEM((per, 2, n, PAIR), bf16),
            pltpu.VMEM((2, tq, n), f32),
        ],
        compiler_params=params(),
        cost_estimate=cost(2 * n * n * (4 * PAIR) * pairs * 2, n * c * 4, n * n * 2 * pairs),
        name="attn_fwd",
    )(packed, packed, packed, qf, kf, cot, tw)


def attn_bwd_kernel(
    q_ref, k_ref, v_ref, o_ref, g_ref, feat_ref, kf_ref, out_ref, ka_ref, va_ref, qa_ref, ga_ref, kt_ref, dq_ref, st_ref, dp_ref,
    *, tk, live, per,
):
    n = q_ref.shape[0]
    lane = lax.broadcasted_iota(jnp.int32, (1, PAIR), 1)
    none = jnp.zeros((1, PAIR), bf16)
    scale = HEAD_DIM**-0.5
    cols = [slice(d * PAIR, (d + 1) * PAIR) for d in range(per)]

    def prepare(d):
        ka_ref[d, :, :PAIR] = k_ref[:, cols[d]]
        ka_ref[d, :, PAIR:] = kf_ref[...]
        va_ref[d, :, :PAIR] = v_ref[:, cols[d]]
        va_ref[d, :, PAIR:] = jnp.broadcast_to(jnp.where(lane < 3, 1.0, 0.0).astype(bf16), (n, PAIR))
        kt_ref[d] = k_ref[:, cols[d]].T
        q = q_ref[:, cols[d]] * jnp.asarray(scale, bf16)
        g = g_ref[:, cols[d]]
        prod = g.astype(f32) * o_ref[:, cols[d]].astype(f32)
        for h in range(2):
            own = half_mask(h)
            delta = jnp.sum(jnp.where(own, prod, 0.0), axis=1, keepdims=True)
            a, b, c = pieces(-delta)
            qa_ref[d, h, :, :PAIR] = jnp.where(own, q, none)
            qa_ref[d, h, :, PAIR:] = feat_ref[2 * d + h]
            ga_ref[d, h, :, :PAIR] = jnp.where(own, g, none)
            ga_ref[d, h, :, PAIR:] = jnp.where(lane == 0, a, jnp.where(lane == 1, b, jnp.where(lane == 2, c, none)))

    eye = eye_mask(PAIR)
    spans = [(i, min(i + tk, live)) for i in range(0, live, tk)]
    units = [(d, span, h) for d in range(per) for span in spans for h in range(2)]

    def scores(u):
        d, (lo, hi), h = units[u]
        size = hi - lo
        slot = u % 2
        st_ref[slot, :size] = mm(ka_ref[d, lo:hi, :], qa_ref[d, h], NT)
        for j in range(0, size, PAIR):
            t = min(PAIR, size - j)
            a = slice(j, j + t)
            r = slice(lo + j, lo + j + t)
            c = slice(lo + j, lo + j + PAIR)
            plain = jnp.concatenate([k_ref[r, cols[d]], jnp.where(lane < 5, none, kf_ref[r, :])], axis=1)
            st_ref[slot, a, c] = jnp.where(eye[:t], mm(plain, qa_ref[d, h, c, :], NT), st_ref[slot, a, c])
        dp_ref[slot, :size] = mm(va_ref[d, lo:hi, :], ga_ref[d, h], NT)

    prepare(0)
    scores(0)
    dv = [None, None]
    dk = [None, None]
    for u, (d, (lo, hi), h) in enumerate(units):
        if (lo, h) == (0, 0) and d + 1 < per:
            prepare(d + 1)
        if u + 1 < len(units):
            scores(u + 1)
        rows = slice(lo, hi)
        own = slice(h * HEAD_DIM, (h + 1) * HEAD_DIM)
        p = jnp.exp(st_ref[u % 2, : hi - lo])
        ds = (p * dp_ref[u % 2, : hi - lo]).astype(bf16)
        part = mm(kt_ref[d, own, rows], ds)
        if lo == 0:
            dq_ref[d, own, :] = part
        else:
            dq_ref[d, own, :] += part
        dv[h] = mm(p.astype(bf16), ga_ref[d, h, :, :PAIR])
        dk[h] = mm(ds, qa_ref[d, h, :, :PAIR])
        if h == 1:
            out_ref[1, rows, cols[d]] = (dk[0] + dk[1]).astype(bf16)
            out_ref[2, rows, cols[d]] = (dv[0] + dv[1]).astype(bf16)
            if hi == live:
                out_ref[0, :, cols[d]] = (dq_ref[d].T * scale).astype(bf16)
    if live < n:
        out_ref[1, live:, :] = jnp.zeros((n - live, per * PAIR), bf16)
        out_ref[2, live:, :] = jnp.zeros((n - live, per * PAIR), bf16)


def attn_bwd(packed, att, grad, feat, kf, tk=384, per=1):
    n, c = packed.shape
    w = c // 3
    pairs = w // PAIR
    wide = per * PAIR
    part = lambda p: pl.BlockSpec((n, wide), lambda j: (0, p * (pairs // per) + j))
    live = min(n, -(-ITEM_ROWS // 16) * 16)
    return pl.pallas_call(
        functools.partial(attn_bwd_kernel, tk=tk, live=live, per=per),
        grid=(pairs // per,),
        in_specs=[
            part(0),
            part(1),
            part(2),
            part(0),
            part(0),
            pl.BlockSpec((2 * per, n, PAIR), lambda j: (j, 0, 0)),
            whole((n, PAIR)),
        ],
        out_specs=pl.BlockSpec((3, n, wide), lambda j: (0, 0, j)),
        out_shape=jax.ShapeDtypeStruct((3, n, w), bf16),
        scratch_shapes=[
            pltpu.VMEM((per, n, 2 * PAIR), bf16),
            pltpu.VMEM((per, n, 2 * PAIR), bf16),
            pltpu.VMEM((per, 2, n, 2 * PAIR), bf16),
            pltpu.VMEM((per, 2, n, 2 * PAIR), bf16),
            pltpu.VMEM((per, PAIR, n), bf16),
            pltpu.VMEM((per, PAIR, n), f32),
            pltpu.VMEM((2, tk, n), f32),
            pltpu.VMEM((2, tk, n), f32),
        ],
        compiler_params=params(),
        cost_estimate=cost(2 * n * n * (9 * PAIR) * pairs * 2, n * c * 8, n * n * 2 * pairs),
        name="attn_bwd",
    )(packed, packed, packed, att, grad, feat, kf)


def normal_cdf_pdf(u):
    a = jnp.abs(u)
    t = 1.0 / (1.0 + a * (0.3275911 * 0.7071067811865476))
    e = jnp.exp(-0.5 * u * u)
    half = 0.5
    poly = t * (
        half * 0.254829592
        + t * (half * -0.284496736 + t * (half * 1.421413741 + t * (half * -1.453152027 + t * (half * 1.061405429))))
    )
    tail = poly * e
    return jnp.where(u < 0, tail, 1.0 - tail), e * 0.3989422804014327


def ff_fwd_kernel(
    core_ref, a_ref, hid_ref, wo_ref, bo_ref, g_ref, b_ref, grt_ref, w1_ref, b1_ref,
    mid_out, n2_out, act_ref, slope_ref, *rest, m, order, sub, count, rb,
):
    refs, (mid_ref, n2_ref, sems) = rest[:count], rest[count:]
    n = a_ref.shape[0]
    step = pl.program_id(0)
    copies = [pltpu.make_async_copy(mid_ref, mid_out, sems.at[0]), pltpu.make_async_copy(n2_ref, n2_out, sems.at[1])]

    @pl.when(step == 0)
    def _():
        parts = [slice(lo, lo + rb) for lo in range(0, n, rb)]
        project = lambda r: mm(a_ref[r, :], wo_ref[...])
        ahead = project(parts[0])
        for i, r in enumerate(parts):
            mid = hid_ref[r, :] + ahead + line(bo_ref)
            if i + 1 < len(parts):
                ahead = project(parts[i + 1])
            mid_ref[r, :] = mid
            std, _ = row_stats(mid)
            n2_ref[r, :] = (std * line(g_ref) + line(b_ref)).astype(bf16)
        for c in copies:
            c.start()

    fc = w1_ref.shape[1]
    bias = line(b1_ref)
    cut = lambda s: slice(s * sub, (s + 1) * sub)
    before = lambda s: mm(n2_ref[...], w1_ref[:, cut(s)]) + bias[:, cut(s)]
    ahead = before(0)
    for s in range(fc // sub):
        pre = ahead
        if s + 1 < fc // sub:
            ahead = before(s + 1)
        cdf, pdf = normal_cdf_pdf(pre)
        act = (pre * cdf).astype(bf16)
        slope_ref[:, cut(s)] = (cdf + pre * pdf).astype(bf16)
        act_ref[:, cut(s)] = act
        views = [r.at[:, :, cut(s)] if count == 2 else r.at[:, cut(s)] for r in refs]
        put(mm(grt_ref[...], act), views, core_ref[0], m, order)

    @pl.when(step == pl.num_programs(0) - 1)
    def _():
        for c in copies:
            c.wait()


def ff_fwd(core, dp, att, hid, wo, bo, g, b, grt, w1, b1, fc=1024, sub=256):
    n, w = att.shape
    ff = w1.shape[1]
    m = w // dp
    if can_split(w, m):
        specs = [pl.BlockSpec((dp // 2, m, fc), lambda i: (0, i, 0))] * 2
        shapes = [jax.ShapeDtypeStruct((dp // 2, ff // fc * m, fc), f32)] * 2
    else:
        specs = [pl.BlockSpec((w, fc), lambda i: (0, i))]
        shapes = [jax.ShapeDtypeStruct((w, ff), f32)]
    left = pl.BlockSpec(memory_space=pl.ANY)
    res = pl.pallas_call(
        functools.partial(ff_fwd_kernel, m=m, order=ring_order(dp), sub=sub, count=len(specs), rb=n // 3),
        grid=(ff // fc,),
        in_specs=[
            SMEM1,
            whole((n, w)),
            whole((n, w)),
            whole((w, w)),
            whole((w,)),
            whole((w,)),
            whole((w,)),
            whole((w, n)),
            pl.BlockSpec((w, fc), lambda i: (0, i)),
            pl.BlockSpec((fc,), lambda i: (i,)),
        ],
        out_specs=[left, left] + [pl.BlockSpec((n, fc), lambda i: (0, i))] * 2 + specs,
        out_shape=[
            jax.ShapeDtypeStruct((n, w), f32),
            jax.ShapeDtypeStruct((n, w), bf16),
            jax.ShapeDtypeStruct((n, ff), bf16),
            jax.ShapeDtypeStruct((n, ff), bf16),
        ]
        + shapes,
        scratch_shapes=[pltpu.VMEM((n, w), f32), pltpu.VMEM((n, w), bf16), pltpu.SemaphoreType.DMA((2,))],
        compiler_params=params(60),
        cost_estimate=cost(6 * n * w * ff, n * w * 10 + ff * w * 8 + n * ff * 2, n * ff * 2),
        name="ff_fwd",
    )(core, att, hid, wo, bo, g, b, grt, w1, b1)
    return res[0], res[1], res[2], res[3], res[4:]


def ff_bwd_kernel(core_ref, n2_ref, gr_ref, w1a_ref, w1b_ref, sla_ref, slb_ref, w2a_ref, w2b_ref, *rest, first, count, m):
    gn_ref, db1_ref = rest[-2 - count : -count]
    refs = rest[-count:]
    side = lambda a, b: jnp.concatenate([a[...], b[...]], axis=1)
    w1 = side(w1a_ref, w1b_ref)
    w2 = jnp.concatenate([w2a_ref[...], w2b_ref[...]], axis=0)
    gpre = (mm(gr_ref[...], w2, NT) * side(sla_ref, slb_ref).astype(f32)).astype(bf16)

    @pl.when(pl.program_id(0) == 0)
    def _():
        gn_ref[...] = jnp.zeros_like(gn_ref) if first else rest[0][...]

    gn_ref[...] += mm(gpre, w1, NT)
    put(mm(gpre, n2_ref[...], TN), refs, core_ref[0], m)
    db1_ref[...] = jnp.sum(gpre.astype(f32), axis=0, keepdims=True)


def ff_bwd(core, dp, n2, gr, w1, slope, w2, base, steps, prev):
    n, w = n2.shape
    ff = w1.shape[1]
    m = ff // dp
    fc = 384
    ring = can_split(fc, m) and fc == 2 * m and dp == 16
    total = ff // (2 * fc)
    steps = total - base if steps is None else steps
    if ring:
        near = lambda i: jnp.where(base + i < 2, 4 * (base + i), 15 - 4 * (base + i))
        far = lambda i: jnp.where(base + i < 2, 4 * (base + i) + 2, 13 - 4 * (base + i))
        specs = [pl.BlockSpec((2, m, w), lambda i: (base + i, 0, 0))] * 2
        shapes = [jax.ShapeDtypeStruct((dp // 2, m, w), f32)] * 2
    else:
        near = lambda i: 2 * (base + i)
        far = lambda i: 2 * (base + i) + 1
        specs = [pl.BlockSpec((2 * fc, w), lambda i: (base + i, 0))]
        shapes = [jax.ShapeDtypeStruct((ff, w), f32)]
    extra = [] if prev is None else list(prev)
    res = pl.pallas_call(
        functools.partial(ff_bwd_kernel, first=prev is None, count=len(specs), m=m),
        grid=(steps,),
        in_specs=[
            SMEM1,
            whole((n, w)),
            whole((n, w)),
            pl.BlockSpec((w, fc), lambda i: (0, near(i))),
            pl.BlockSpec((w, fc), lambda i: (0, far(i))),
            pl.BlockSpec((n, fc), lambda i: (0, near(i))),
            pl.BlockSpec((n, fc), lambda i: (0, far(i))),
            pl.BlockSpec((fc, w), lambda i: (near(i), 0)),
            pl.BlockSpec((fc, w), lambda i: (far(i), 0)),
        ]
        + ([whole((n, w))] + [pl.BlockSpec(memory_space=pl.ANY)] * len(specs) if extra else []),
        out_specs=[whole((n, w)), pl.BlockSpec((1, 2 * fc), lambda i: (0, i))] + specs,
        out_shape=[jax.ShapeDtypeStruct((n, w), f32), jax.ShapeDtypeStruct((1, 2 * fc * steps), f32)] + shapes,
        input_output_aliases={10 + k: 2 + k for k in range(len(specs))} if extra else {},
        compiler_params=params(60),
        cost_estimate=cost(12 * n * w * fc * steps, n * w * 10 + fc * steps * w * 16 + n * fc * steps * 4),
        name="ff_bwd",
    )(core, n2, gr, w1, w1, slope, slope, w2, w2, *extra)
    return (res[0], *res[2:]), res[1]


def back_kernel(core_ref, mid_ref, gn_ref, cot_ref, tw_ref, a_ref, wo_ref, g_ref, *rest, m, count, order, sub):
    gm_ref, ga_ref, vec_ref = rest[-4 - count : -1 - count]
    dwo_refs, dwo_ref = rest[-1 - count : -1], rest[-1]
    rb, w = mid_ref.shape
    step = pl.program_id(0)
    add = lambda x: jnp.sum(x, axis=0, keepdims=True)
    parts = [slice(lo, lo + sub) for lo in range(0, rb, sub)]

    @pl.when(step == 0)
    def _():
        dwo_ref[...] = jnp.zeros_like(dwo_ref)
        vec_ref[...] = jnp.zeros_like(vec_ref)

    def norm_part(r):
        mid = mid_ref[r, :]
        std, inv = row_stats(mid)
        gn = gn_ref[r, :]
        gm = cot_ref[r, :].astype(f32) * tw_ref[r, :] + norm_back(gn, std, inv, line(g_ref))
        gm_ref[r, :] = gm
        gb = gm.astype(bf16)
        vec_ref[...] += jnp.concatenate([add(gb.astype(f32)), add(gn * std), add(gn), jnp.zeros((1, w), f32)], axis=0)
        return gb

    ahead = norm_part(parts[0])
    for i, r in enumerate(parts):
        gb = ahead
        if i + 1 < len(parts):
            ahead = norm_part(parts[i + 1])
        ga_ref[r, :] = mm(gb, wo_ref[...], NT).astype(bf16)
        dwo_ref[...] += mm(gb, a_ref[r, :], TN)

    @pl.when(step == pl.num_programs(0) - 1)
    def _():
        put(dwo_ref[...], dwo_refs, core_ref[0], m, order)


def grad_outs(rows, cols, m):
    if can_split(rows, m):
        shape = (rows // (2 * m), m, cols)
        return [whole(shape)] * 2, [jax.ShapeDtypeStruct(shape, f32)] * 2
    return [whole((rows, cols))], [jax.ShapeDtypeStruct((rows, cols), f32)]


def back_part(core, dp, mid, gn, cot, tw, att, wo, g, rb, sub=384):
    n, w = mid.shape
    row = lambda cols: pl.BlockSpec((rb, cols), lambda i: (i, 0))
    mo, mj = w // dp, 3 * w // dp
    if can_split(w, mo) and can_split(3 * w, mj):
        specs = [pl.BlockSpec((dp // 2, mo, w), lambda i: (0, mj // mo, 0))] * 2
        shapes = [jax.ShapeDtypeStruct((dp // 2, mj + mo, w), f32)] * 2
    else:
        specs, shapes = [whole((w, w))], [jax.ShapeDtypeStruct((w, w), f32)]
    res = pl.pallas_call(
        functools.partial(back_kernel, m=mo, count=len(specs), order=ring_order(dp), sub=sub),
        grid=(n // rb,),
        in_specs=[SMEM1, row(w), row(w), row(w), row(1), row(w), whole(wo.shape), whole((w,))],
        out_specs=[row(w), row(w), whole((4, w))] + specs,
        out_shape=[
            jax.ShapeDtypeStruct((n, w), f32),
            jax.ShapeDtypeStruct((n, w), bf16),
            jax.ShapeDtypeStruct((4, w), f32),
        ]
        + shapes,
        scratch_shapes=[pltpu.VMEM((w, w), f32)],
        compiler_params=params(),
        cost_estimate=cost(4 * n * w * w, n * w * 28),
        name="back_part",
    )(core, mid, gn, cot, tw, att, wo, g)
    return res[0], res[1], res[2], res[3:]


def finish_kernel(mid_ref, act_ref, w2_ref, b2_ref, out_ref):
    out_ref[...] = (mid_ref[...] + mm(act_ref[...], w2_ref[...]) + line(b2_ref)).astype(bf16)


def finish(mid, act, w2, b2, rb):
    n, w = mid.shape
    row = lambda cols: pl.BlockSpec((rb, cols), lambda i: (i, 0))
    return pl.pallas_call(
        finish_kernel,
        grid=(n // rb,),
        in_specs=[row(w), row(act.shape[1]), whole(w2.shape), whole((w,))],
        out_specs=row(w),
        out_shape=jax.ShapeDtypeStruct((n, w), bf16),
        compiler_params=params(),
        cost_estimate=cost(2 * n * w * act.shape[1], n * w * 14),
        name="finish",
    )(mid, act, w2, b2)


def joint_grad_kernel(core_ref, gp_ref, n1_ref, *rest, m, count, order):
    refs, gpt_ref = rest[-1 - count : -1], rest[-1]
    parts, n, w = gp_ref.shape

    @pl.when(pl.program_id(0) == 0)
    def _():
        for p in range(parts):
            gpt_ref[p * w : (p + 1) * w, :] = gp_ref[p].T

    put(mm(gpt_ref[...], n1_ref[...]), refs, core_ref[0], m, order)


def grad_block(rows, cols, cb, m):
    if can_split(rows, m):
        spec = pl.BlockSpec((rows // (2 * m), m, cb), lambda j: (0, 0, j))
        return [spec] * 2, [jax.ShapeDtypeStruct((rows // (2 * m), m, cols), f32)] * 2
    return [pl.BlockSpec((rows, cb), lambda j: (0, j))], [jax.ShapeDtypeStruct((rows, cols), f32)]


def joint_grad(core, dp, gp, n1, into, cb=256):
    parts, n, w = gp.shape
    m = parts * w // dp
    specs, shapes = grad_block(parts * w, w, cb, m)
    if len(into) == 2:
        shapes = [jax.ShapeDtypeStruct(x.shape, f32) for x in into]
    else:
        into = []
    return pl.pallas_call(
        functools.partial(joint_grad_kernel, m=m, count=len(specs), order=ring_order(dp)),
        grid=(w // cb,),
        in_specs=[SMEM1, whole((parts, n, w)), pl.BlockSpec((n, cb), lambda j: (0, j))]
        + [pl.BlockSpec(memory_space=pl.ANY)] * len(into),
        out_specs=specs,
        out_shape=shapes,
        input_output_aliases={3 + k: k for k in range(len(into))},
        scratch_shapes=[pltpu.VMEM((parts * w, n), bf16)],
        compiler_params=params(),
        cost_estimate=cost(2 * parts * n * w * w, n * w * 8 + parts * w * w * 4),
        name="joint_grad",
    )(core, gp, n1, *into)


def tail_kernel(gp_ref, hid_ref, gm_ref, wj_ref, g_ref, gh_ref, vec_ref, *, sub):
    rb, w = hid_ref.shape
    parts = [slice(lo, lo + sub) for lo in range(0, rb, sub)]
    add = lambda x: jnp.sum(x, axis=0, keepdims=True)

    def project(r):
        return sum(mm(gp_ref[p, r, :], wj_ref[:, p * w : (p + 1) * w], NT) for p in range(3))

    ahead = project(parts[0])
    vec = jnp.zeros((4, w), f32)
    for i, r in enumerate(parts):
        gn = ahead
        if i + 1 < len(parts):
            ahead = project(parts[i + 1])
        std, inv = row_stats(hid_ref[r, :])
        gh = (gm_ref[r, :] + norm_back(gn, std, inv, line(g_ref))).astype(bf16)
        gh_ref[r, :] = gh
        vec = vec + jnp.concatenate([add(gn * std), add(gn), add(gh.astype(f32)), jnp.zeros((1, w), f32)], axis=0)
    step = pl.program_id(0)

    @pl.when(step == 0)
    def _():
        vec_ref[...] = vec

    @pl.when(step > 0)
    def _():
        vec_ref[...] += vec


def tail_part(gp, hid, gm, wj, g, rb, sub=384):
    n, w = hid.shape
    row = lambda cols: pl.BlockSpec((rb, cols), lambda i: (i, 0))
    return pl.pallas_call(
        functools.partial(tail_kernel, sub=sub),
        grid=(n // rb,),
        in_specs=[pl.BlockSpec((3, rb, w), lambda i: (0, i, 0)), row(w), row(w), whole(wj.shape), whole((w,))],
        out_specs=[row(w), whole((4, w))],
        out_shape=[jax.ShapeDtypeStruct((n, w), bf16), jax.ShapeDtypeStruct((4, w), f32)],
        compiler_params=params(),
        cost_estimate=cost(6 * n * w * w, n * w * 16),
        name="tail_part",
    )(gp, hid, gm, wj, g)


def skip_grad_kernel(core_ref, gh_ref, x_ref, s_ref, vec_ref, *refs, m, order):
    ght = gh_ref[...].T
    val = jnp.concatenate([mm(ght, x_ref[...]), mm(ght, s_ref[...]), vec_ref[...]], axis=1)
    put(val, refs, core_ref[0], m, order)


def skip_grad(core, dp, gh, x, s, vec):
    n, w = gh.shape
    m = w // dp
    cols = 2 * w + vec.shape[1]
    specs, shapes = grad_block(w, cols, cols, m)
    return pl.pallas_call(
        functools.partial(skip_grad_kernel, m=m, order=ring_order(dp)),
        grid=(1,),
        in_specs=[SMEM1, whole((n, w)), whole((n, w)), whole((n, w)), whole(vec.shape)],
        out_specs=specs,
        out_shape=shapes,
        compiler_params=params(),
        cost_estimate=cost(4 * n * w * w, n * w * 6 + w * w * 8),
        name="skip_grad",
    )(core, gh, x, s, vec)


def in_grad_kernel(gh_ref, ws_ref, a_ref, b_ref):
    w = a_ref.shape[1]
    gh = gh_ref[...]
    a_ref[...] = mm(gh, ws_ref[:w, :], NT).astype(bf16)
    b_ref[...] = mm(gh, ws_ref[w:, :], NT).astype(bf16)


def in_grad(gh, ws, rb):
    n, w = gh.shape
    row = lambda cols: pl.BlockSpec((rb, cols), lambda i: (i, 0))
    return pl.pallas_call(
        in_grad_kernel,
        grid=(n // rb,),
        in_specs=[row(w), whole(ws.shape)],
        out_specs=[row(w), row(w)],
        out_shape=[jax.ShapeDtypeStruct((n, w), bf16)] * 2,
        compiler_params=params(),
        cost_estimate=cost(4 * n * w * w, n * w * 10),
        name="in_grad",
    )(gh, ws)


def pick(x, axis, index):
    return lax.dynamic_index_in_dim(x, index, axis, keepdims=False)


def swap(x, axis, bit=0):
    size = lax.axis_size(axis)
    return lax.ppermute(x, axis, [(i, i ^ (1 << bit)) for i in range(size)])


def pair_terms(refs, cols, dp):
    if len(refs) == 1:
        full = refs[0].reshape(dp // 2, 2, -1, cols)
        core = lax.axis_index("dp") & 1
        refs = [pick(full, 1, core), pick(full, 1, 1 - core)]
    return [refs[0], swap(refs[1], "dp")]


def both_sides(x, side):
    other = swap(x, "rep")
    return jnp.concatenate([jnp.where(side == 0, x, other), jnp.where(side == 0, other, x)], axis=0)


def add_kernel(a_ref, b_ref, out_ref):
    out_ref[...] = a_ref[...] + b_ref[...]


def add_blocks(a, b, per=4):
    places, rows, cols = a.shape
    spec = pl.BlockSpec((per, rows, cols), lambda i: (i, 0, 0))
    return pl.pallas_call(
        add_kernel,
        grid=(places // per,),
        in_specs=[spec, spec],
        out_specs=spec,
        out_shape=jax.ShapeDtypeStruct(a.shape, f32),
        compiler_params=params(),
        name="add_blocks",
    )(a, b)


def tie(x, y):
    return lax.optimization_barrier((x, y))


def per_device(*args):
    (inputs, skips, cot, lengths, keep, group_ids, group_counts, ws, bs, g1, s1, wj, wo, bo, g2, s2, w1, b1, w2, b2) = args
    n, w = inputs.shape
    ff = w1.shape[1]
    dp = lax.axis_size("dp")
    tokens_total = n * dp * lax.axis_size("rep")
    scale = float(tokens_total) ** -0.5
    side = lax.axis_index("rep")
    core = (lax.axis_index("dp") & 1).astype(jnp.int32).reshape(1)
    rb = n // 3
    ring = ring_order(dp)
    groups = [[2 * i + c for i in ring] for c in range(2)]
    ring_sum = lambda h: lax.psum_scatter(h, "dp", scatter_dimension=0, tiled=True, axis_index_groups=groups)[0]
    over_rep = lambda h: h + swap(h, "rep")

    hid, n1, packed, qf, kf, tw = front(
        lengths, group_ids, group_counts, keep, inputs, skips, ws, bs, g1, s1, wj, rb, tokens_total // group_counts.shape[0]
    )
    att, feat, gr, grt, gsum = attn_fwd(packed, qf, kf, cot, tw)
    mid, n2, act, slope, d2 = ff_fwd(core, dp, att, hid, wo, bo, g2, s2, grt, w1, b1)
    terms2 = pair_terms(d2, ff, dp)
    half2 = add_blocks(*terms2) if len(d2) == 2 else sum(terms2)
    carry, db0 = ff_bwd(core, dp, n2, gr, w1, slope, w2, 0, 1, None)
    carry, half2 = tie(carry, half2)
    carry, db1 = ff_bwd(core, dp, n2, gr, w1, slope, w2, 1, None, carry)
    gn2, d1 = carry[0], carry[1:]
    gm, gatt, vec2, do = back_part(core, dp, mid, gn2, cot, tw, att, wo, g2, rb)
    half1 = sum(pair_terms(d1, w, dp))
    gatt, half1 = tie(gatt, half1)
    sum2 = ring_sum(half2)
    sum1 = ring_sum(half1)

    gp = attn_bwd(packed, att, gatt, feat, kf)
    gp, sum2 = tie(gp, sum2)
    got2 = swap(sum2, "rep")

    dj = joint_grad(core, dp, gp, n1, do)
    gp, dj = tie(gp, dj)
    if len(dj) == 2:
        halfj = sum(pair_terms(dj, w, dp))
    else:
        full = jnp.concatenate([dj[0].reshape(dp, 3 * w // dp, w), do[0].reshape(dp, w // dp, w)], axis=1)
        halfj = sum(pair_terms([full.reshape(-1, w)], w, dp))
    gh, vec1 = tail_part(gp, hid, gm, wj, g1, rb)
    gh, halfj, sum1, got2 = lax.optimization_barrier((gh, halfj, sum1, got2))
    sumj = ring_sum(halfj)
    db = jnp.concatenate([db0, db1], axis=1).reshape(8, ff // 8)
    if len(d1) == 2:
        db = jnp.stack([db[ring.index(i)] for i in range(8)])
    db = db.reshape(w, ff // w)
    vec = jnp.concatenate([vec1.T, vec2[:3].T, gsum.T, db, jnp.zeros((w, PAIR - 8 - ff // w), f32)], axis=1)
    cols = 2 * w + PAIR
    ds = skip_grad(core, dp, gh, inputs, skips, vec)
    terms = [t.reshape(dp // 2, 2, -1, cols) for t in pair_terms(ds, cols, dp)]
    send = sum(pick(t, 1, 1 - side) for t in terms)
    gh, send = tie(gh, send)
    igrad, sgrad = in_grad(gh, ws, rb)
    act, igrad = tie(act, igrad)
    outcome = finish(mid, act, w2, b2, rb)
    halfs = sum(pick(t, 1, side) for t in terms) + swap(send, "rep")
    halfs, sumj, sum1, outcome, sgrad = lax.optimization_barrier((halfs, sumj, sum1, outcome, sgrad))
    sums = ring_sum(halfs)
    out2 = sum2 + got2
    out1 = over_rep(sum1)
    outj = over_rep(sumj)
    if len(d2) == 2:
        out2 = out2.reshape(-1, w // dp, 1024).transpose(1, 0, 2).reshape(w // dp, ff)
    outj, outo = outj[: 3 * w // dp], outj[3 * w // dp :]
    outs = both_sides(sums, side)

    ds, dj, do, d1, d2 = [m.T * scale for m in (outs[:, : 2 * w], outj, outo, out1, out2)]
    v = outs[:, 2 * w :] * scale
    col = lambda i: v[:, i]
    db1 = v[:, 8 : 8 + ff // w].reshape(-1)
    return (
        outcome, igrad, sgrad, ds, col(2), col(0), col(1), dj, do, col(4), col(5), col(6), d1, db1, d2, col(7),
    )


def solution(mesh):
    both = ("dp", "rep")
    in_specs = (P(both, None),) * 3 + (P(both),) * 3 + (P(),) * 14
    cols = P(None, "dp")
    vec = P("dp")
    out_specs = (P(both, None),) * 3 + (cols, vec, vec, vec, cols, cols, vec, vec, vec, cols, vec, cols, vec)
    return jax.shard_map(per_device, mesh=mesh, in_specs=in_specs, out_specs=out_specs, check_vma=False)
```

```python
import functools

import jax
import jax.numpy as jnp
from jax import lax
from jax.experimental import pallas as pl
from jax.experimental.pallas import tpu as pltpu
from jax.sharding import PartitionSpec as P

HEAD_DIM = 64
PAIR = 2 * HEAD_DIM
EPS = 1e-05
BIG = 1e30
ITEM_ROWS = 1028
f32 = jnp.float32
bf16 = jnp.bfloat16
NT = (((1,), (1,)), ((), ()))
NN = (((1,), (0,)), ((), ()))
TN = (((0,), (0,)), ((), ()))


def mm(a, b, dims=NN):
    return lax.dot_general(a, b, dims, preferred_element_type=f32)


def params(mb=56):
    return pltpu.CompilerParams(vmem_limit_bytes=mb << 20)


def cost(flops, nbytes, trans=0):
    return pl.CostEstimate(flops=int(flops), bytes_accessed=int(nbytes), transcendentals=int(trans))


def whole(shape):
    return pl.BlockSpec(shape, lambda *_: (0,) * len(shape), pipeline_mode=pl.Buffered(1))


def row_stats(x):
    mean = jnp.mean(x, axis=1, keepdims=True)
    cen = x - mean
    inv = lax.rsqrt(jnp.mean(cen * cen, axis=1, keepdims=True) + EPS)
    return cen * inv, inv


def norm_back(g, std, inv, gain):
    e = g * gain
    return inv * (e - jnp.mean(e, axis=1, keepdims=True) - std * jnp.mean(e * std, axis=1, keepdims=True))


def can_split(rows, m):
    return m % 8 == 0 and rows % (2 * m) == 0


def ring_order(dp):
    if dp != 16:
        return list(range(dp // 2))
    return [2 * z for z in range(4)] + [2 * z + 1 for z in reversed(range(4))]


def split_store(val, refs, core, m, order=None):
    rows, cols = val.shape
    parts = val.reshape(rows // (2 * m), 2, m, cols)
    low, high = parts[:, 0], parts[:, 1]
    keep = jnp.where(core == 0, low, high)
    send = jnp.where(core == 0, high, low)
    if order is None:
        refs[0][...] = keep
        refs[1][...] = send
    else:
        for place, owner in enumerate(order):
            refs[0][place] = keep[owner]
            refs[1][place] = send[owner]


def put(val, refs, core, m, order=None):
    if len(refs) == 2:
        split_store(val, refs, core, m, order)
    else:
        refs[0][...] = val


SMEM1 = pl.BlockSpec(memory_space=pltpu.SMEM)


def eye_mask(t):
    return lax.broadcasted_iota(jnp.int32, (t, t), 0) == lax.broadcasted_iota(jnp.int32, (t, t), 1)


def line(ref):
    return ref[...].astype(f32).reshape(1, -1)


def front_kernel(
    len_ref, gid_ref, cnt_ref, keep_ref, x_ref, s_ref, ws_ref, bs_ref, g_ref, b_ref, wj_ref,
    hid_ref, n1_ref, q_ref, qf_ref, kf_ref, tw_ref, *, group_tokens, sub,
):
    rb, w = x_ref.shape

    def project(r):
        return mm(x_ref[r, :], ws_ref[:w, :]) + mm(s_ref[r, :], ws_ref[w:, :]) + line(bs_ref)

    parts = [slice(lo, lo + sub) for lo in range(0, rb, sub)]
    ahead = project(parts[0])
    for i, r in enumerate(parts):
        hid = ahead
        if i + 1 < len(parts):
            ahead = project(parts[i + 1])
        hid_ref[r, :] = hid
        std, _ = row_stats(hid)
        n1 = (std * line(g_ref) + line(b_ref)).astype(bf16)
        n1_ref[r, :] = n1
        q_ref[r, :] = mm(n1, wj_ref[...]).astype(bf16)

    slots = len_ref.shape[0]
    base = pl.program_id(0) * rb
    lane = lax.broadcasted_iota(jnp.int32, (1, PAIR), 1)
    pos = lax.broadcasted_iota(jnp.int32, (rb, 1), 0) + base
    segment = jnp.zeros((rb, 1), jnp.int32)
    count = jnp.ones((1, PAIR), f32)
    end = 0
    for i in range(slots):
        end = end + len_ref[i]
        segment = segment + (pos >= end).astype(jnp.int32)
        count = jnp.where(lane == i, cnt_ref[gid_ref[i]].astype(f32), count)
    same = segment == lane
    weight = jnp.where(lane < slots, group_tokens / count, 0.0)
    tw_ref[...] = jnp.sum(jnp.where(same, weight, 0.0), axis=1, keepdims=True)
    qf_ref[...] = jnp.where(same, 1.0, 0.0).astype(bf16)
    eye = eye_mask(PAIR)
    for t in range(rb // PAIR):
        rows = slice(t * PAIR, (t + 1) * PAIR)
        keep = keep_ref[pl.ds(pl.multiple_of(base + t * PAIR, PAIR), PAIR)].astype(f32).reshape(1, PAIR)
        kept = jnp.sum(jnp.where(eye, keep, 0.0), axis=1, keepdims=True) == 1.0
        bias = jnp.where(same[rows] & kept, 0.0, -BIG)
        kf_ref[rows, :] = jnp.where(lane <= slots, bias, jnp.where(lane < slots + 4, 1.0, 0.0)).astype(bf16)


def front(lengths, gids, counts, keep, x, s, ws, bs, g, b, wj, rb, group_tokens, sub=192):
    n, w = x.shape
    c = wj.shape[1]
    row = lambda cols: pl.BlockSpec((rb, cols), lambda i: (i, 0))
    return pl.pallas_call(
        functools.partial(front_kernel, group_tokens=float(group_tokens), sub=sub),
        grid=(n // rb,),
        in_specs=[SMEM1, SMEM1, SMEM1, whole((n,)), row(w), row(w), whole(ws.shape), whole((w,)), whole((w,)), whole((w,)), whole(wj.shape)],
        out_specs=[row(w), row(w), row(c), row(PAIR), row(PAIR), row(1)],
        out_shape=[
            jax.ShapeDtypeStruct((n, w), f32),
            jax.ShapeDtypeStruct((n, w), bf16),
            jax.ShapeDtypeStruct((n, c), bf16),
            jax.ShapeDtypeStruct((n, PAIR), bf16),
            jax.ShapeDtypeStruct((n, PAIR), bf16),
            jax.ShapeDtypeStruct((n, 1), f32),
        ],
        compiler_params=params(),
        cost_estimate=cost(2 * n * w * (2 * w + c), n * w * 20 + 5 * w * w * 2),
        name="front",
    )(lengths, gids, counts, keep, x, s, ws, bs, g, b, wj)


def half_mask(h):
    lane = lax.broadcasted_iota(jnp.int32, (1, PAIR), 1)
    return (lane < HEAD_DIM) if h == 0 else (lane >= HEAD_DIM)


def pieces(x):
    a = x.astype(bf16)
    r = x - a.astype(f32)
    b = r.astype(bf16)
    c = (r - b.astype(f32)).astype(bf16)
    return a, b, c


def attn_fwd_kernel(
    q_ref, k_ref, v_ref, qf_ref, kf_ref, cot_ref, tw_ref, o_ref, feat_ref, gr_ref, grt_ref, gsum_ref, ka_ref, vm_ref, s_ref, *, tq, per
):
    n = q_ref.shape[0]
    none = jnp.zeros((1, PAIR), bf16)
    one = jnp.ones((1, PAIR), bf16)
    lane = lax.broadcasted_iota(jnp.int32, (1, PAIR), 1)
    spare = [HEAD_DIM, 0]
    cols = [slice(d * PAIR, (d + 1) * PAIR) for d in range(per)]
    for d in range(per):
        ka_ref[d, :, :PAIR] = k_ref[:, cols[d]]
        ka_ref[d, :, PAIR:] = kf_ref[...]
        for h in range(2):
            vm_ref[d, h] = jnp.where(half_mask(h), v_ref[:, cols[d]], jnp.where(lane == spare[h], one, none))
    eye = eye_mask(PAIR)
    units = [(d, i, h) for d in range(per) for i in range(n // tq) for h in range(2)]

    def scores(u):
        d, i, h = units[u]
        rows = slice(i * tq, (i + 1) * tq)
        qm = jnp.where(half_mask(h), q_ref[rows, cols[d]] * jnp.asarray(HEAD_DIM**-0.5, bf16), none)
        slot = u % 2
        s_ref[slot] = mm(jnp.concatenate([qm, qf_ref[rows, :]], axis=1), ka_ref[d], NT)
        for j in range(tq // PAIR):
            a = slice(j * PAIR, (j + 1) * PAIR)
            c = slice(i * tq + j * PAIR, i * tq + (j + 1) * PAIR)
            s_ref[slot, a, c] = jnp.where(eye, mm(qm[a], k_ref[c, cols[d]], NT), s_ref[slot, a, c])

    scores(0)
    outs = [None, None]
    gsum = [None] * per
    for u, (d, i, h) in enumerate(units):
        if u + 1 < len(units):
            scores(u + 1)
        rows = slice(i * tq, (i + 1) * tq)
        s = s_ref[u % 2]
        top = jnp.max(s, axis=1, keepdims=True)
        pv = mm(jnp.exp(s - top).astype(bf16), vm_ref[d, h])
        total = pv[:, spare[h] : spare[h] + 1]
        outs[h] = pv / total
        a, b, c = pieces(-(top + jnp.log(total)))
        feat_ref[2 * d + h, rows, :] = jnp.where(
            lane == 5, a, jnp.where(lane == 6, b, jnp.where(lane == 7, c, qf_ref[rows, :]))
        )
        if h == 0:
            gr = (cot_ref[rows, cols[d]].astype(f32) * tw_ref[rows, :]).astype(bf16)
            gr_ref[rows, cols[d]] = gr
            grt_ref[cols[d], rows] = gr.T
            part = jnp.sum(gr.astype(f32), axis=0, keepdims=True)
            gsum[d] = part if i == 0 else gsum[d] + part
        else:
            o_ref[rows, cols[d]] = jnp.where(lane < HEAD_DIM, outs[0], outs[1]).astype(bf16)
    for d in range(per):
        gsum_ref[:, cols[d]] = gsum[d]


def attn_fwd(packed, qf, kf, cot, tw, tq=384, per=1):
    n, c = packed.shape
    w = c // 3
    pairs = w // PAIR
    wide = per * PAIR
    part = lambda p: pl.BlockSpec((n, wide), lambda j: (0, p * (pairs // per) + j))
    return pl.pallas_call(
        functools.partial(attn_fwd_kernel, tq=tq, per=per),
        grid=(pairs // per,),
        in_specs=[part(0), part(1), part(2), whole((n, PAIR)), whole((n, PAIR)), part(0), whole((n, 1))],
        out_specs=[
            pl.BlockSpec((n, wide), lambda j: (0, j)),
            pl.BlockSpec((2 * per, n, PAIR), lambda j: (j, 0, 0)),
            pl.BlockSpec((n, wide), lambda j: (0, j)),
            pl.BlockSpec((wide, n), lambda j: (j, 0)),
            pl.BlockSpec((1, wide), lambda j: (0, j)),
        ],
        out_shape=[
            jax.ShapeDtypeStruct((n, w), bf16),
            jax.ShapeDtypeStruct((2 * pairs, n, PAIR), bf16),
            jax.ShapeDtypeStruct((n, w), bf16),
            jax.ShapeDtypeStruct((w, n), bf16),
            jax.ShapeDtypeStruct((1, w), f32),
        ],
        scratch_shapes=[
            pltpu.VMEM((per, n, 2 * PAIR), bf16),
            pltpu.VMEM((per, 2, n, PAIR), bf16),
            pltpu.VMEM((2, tq, n), f32),
        ],
        compiler_params=params(),
        cost_estimate=cost(2 * n * n * (4 * PAIR) * pairs * 2, n * c * 4, n * n * 2 * pairs),
        name="attn_fwd",
    )(packed, packed, packed, qf, kf, cot, tw)


def attn_bwd_kernel(
    q_ref, k_ref, v_ref, o_ref, g_ref, feat_ref, kf_ref, out_ref, ka_ref, va_ref, qa_ref, ga_ref, kt_ref, dq_ref, st_ref, dp_ref,
    *, tk, live, per,
):
    n = q_ref.shape[0]
    lane = lax.broadcasted_iota(jnp.int32, (1, PAIR), 1)
    none = jnp.zeros((1, PAIR), bf16)
    scale = HEAD_DIM**-0.5
    cols = [slice(d * PAIR, (d + 1) * PAIR) for d in range(per)]

    def prepare(d):
        ka_ref[d, :, :PAIR] = k_ref[:, cols[d]]
        ka_ref[d, :, PAIR:] = kf_ref[...]
        va_ref[d, :, :PAIR] = v_ref[:, cols[d]]
        va_ref[d, :, PAIR:] = jnp.broadcast_to(jnp.where(lane < 3, 1.0, 0.0).astype(bf16), (n, PAIR))
        kt_ref[d] = k_ref[:, cols[d]].T
        q = q_ref[:, cols[d]] * jnp.asarray(scale, bf16)
        g = g_ref[:, cols[d]]
        prod = g.astype(f32) * o_ref[:, cols[d]].astype(f32)
        for h in range(2):
            own = half_mask(h)
            delta = jnp.sum(jnp.where(own, prod, 0.0), axis=1, keepdims=True)
            a, b, c = pieces(-delta)
            qa_ref[d, h, :, :PAIR] = jnp.where(own, q, none)
            qa_ref[d, h, :, PAIR:] = feat_ref[2 * d + h]
            ga_ref[d, h, :, :PAIR] = jnp.where(own, g, none)
            ga_ref[d, h, :, PAIR:] = jnp.where(lane == 0, a, jnp.where(lane == 1, b, jnp.where(lane == 2, c, none)))

    eye = eye_mask(PAIR)
    spans = [(i, min(i + tk, live)) for i in range(0, live, tk)]
    units = [(d, span, h) for d in range(per) for span in spans for h in range(2)]

    def scores(u):
        d, (lo, hi), h = units[u]
        size = hi - lo
        slot = u % 2
        st_ref[slot, :size] = mm(ka_ref[d, lo:hi, :], qa_ref[d, h], NT)
        for j in range(0, size, PAIR):
            t = min(PAIR, size - j)
            a = slice(j, j + t)
            r = slice(lo + j, lo + j + t)
            c = slice(lo + j, lo + j + PAIR)
            plain = jnp.concatenate([k_ref[r, cols[d]], jnp.where(lane < 5, none, kf_ref[r, :])], axis=1)
            st_ref[slot, a, c] = jnp.where(eye[:t], mm(plain, qa_ref[d, h, c, :], NT), st_ref[slot, a, c])
        dp_ref[slot, :size] = mm(va_ref[d, lo:hi, :], ga_ref[d, h], NT)

    prepare(0)
    scores(0)
    dv = [None, None]
    dk = [None, None]
    for u, (d, (lo, hi), h) in enumerate(units):
        if (lo, h) == (0, 0) and d + 1 < per:
            prepare(d + 1)
        if u + 1 < len(units):
            scores(u + 1)
        rows = slice(lo, hi)
        own = slice(h * HEAD_DIM, (h + 1) * HEAD_DIM)
        p = jnp.exp(st_ref[u % 2, : hi - lo])
        ds = (p * dp_ref[u % 2, : hi - lo]).astype(bf16)
        part = mm(kt_ref[d, own, rows], ds)
        if lo == 0:
            dq_ref[d, own, :] = part
        else:
            dq_ref[d, own, :] += part
        dv[h] = mm(p.astype(bf16), ga_ref[d, h, :, :PAIR])
        dk[h] = mm(ds, qa_ref[d, h, :, :PAIR])
        if h == 1:
            out_ref[1, rows, cols[d]] = (dk[0] + dk[1]).astype(bf16)
            out_ref[2, rows, cols[d]] = (dv[0] + dv[1]).astype(bf16)
            if hi == live:
                out_ref[0, :, cols[d]] = (dq_ref[d].T * scale).astype(bf16)
    if live < n:
        out_ref[1, live:, :] = jnp.zeros((n - live, per * PAIR), bf16)
        out_ref[2, live:, :] = jnp.zeros((n - live, per * PAIR), bf16)


def attn_bwd(packed, att, grad, feat, kf, tk=384, per=1):
    n, c = packed.shape
    w = c // 3
    pairs = w // PAIR
    wide = per * PAIR
    part = lambda p: pl.BlockSpec((n, wide), lambda j: (0, p * (pairs // per) + j))
    live = min(n, -(-ITEM_ROWS // 16) * 16)
    return pl.pallas_call(
        functools.partial(attn_bwd_kernel, tk=tk, live=live, per=per),
        grid=(pairs // per,),
        in_specs=[
            part(0),
            part(1),
            part(2),
            part(0),
            part(0),
            pl.BlockSpec((2 * per, n, PAIR), lambda j: (j, 0, 0)),
            whole((n, PAIR)),
        ],
        out_specs=pl.BlockSpec((3, n, wide), lambda j: (0, 0, j)),
        out_shape=jax.ShapeDtypeStruct((3, n, w), bf16),
        scratch_shapes=[
            pltpu.VMEM((per, n, 2 * PAIR), bf16),
            pltpu.VMEM((per, n, 2 * PAIR), bf16),
            pltpu.VMEM((per, 2, n, 2 * PAIR), bf16),
            pltpu.VMEM((per, 2, n, 2 * PAIR), bf16),
            pltpu.VMEM((per, PAIR, n), bf16),
            pltpu.VMEM((per, PAIR, n), f32),
            pltpu.VMEM((2, tk, n), f32),
            pltpu.VMEM((2, tk, n), f32),
        ],
        compiler_params=params(),
        cost_estimate=cost(2 * n * n * (9 * PAIR) * pairs * 2, n * c * 8, n * n * 2 * pairs),
        name="attn_bwd",
    )(packed, packed, packed, att, grad, feat, kf)


def normal_cdf_pdf(u):
    a = jnp.abs(u)
    t = 1.0 / (1.0 + a * (0.3275911 * 0.7071067811865476))
    e = jnp.exp(-0.5 * u * u)
    half = 0.5
    poly = t * (
        half * 0.254829592
        + t * (half * -0.284496736 + t * (half * 1.421413741 + t * (half * -1.453152027 + t * (half * 1.061405429))))
    )
    tail = poly * e
    return jnp.where(u < 0, tail, 1.0 - tail), e * 0.3989422804014327


def ff_fwd_kernel(
    core_ref, a_ref, hid_ref, wo_ref, bo_ref, g_ref, b_ref, grt_ref, w1_ref, b1_ref,
    mid_out, n2_out, act_ref, slope_ref, *rest, m, order, sub, count, rb,
):
    refs, (mid_ref, n2_ref, sems) = rest[:count], rest[count:]
    n = a_ref.shape[0]
    step = pl.program_id(0)
    copies = [pltpu.make_async_copy(mid_ref, mid_out, sems.at[0]), pltpu.make_async_copy(n2_ref, n2_out, sems.at[1])]

    @pl.when(step == 0)
    def _():
        parts = [slice(lo, lo + rb) for lo in range(0, n, rb)]
        project = lambda r: mm(a_ref[r, :], wo_ref[...])
        ahead = project(parts[0])
        for i, r in enumerate(parts):
            mid = hid_ref[r, :] + ahead + line(bo_ref)
            if i + 1 < len(parts):
                ahead = project(parts[i + 1])
            mid_ref[r, :] = mid
            std, _ = row_stats(mid)
            n2_ref[r, :] = (std * line(g_ref) + line(b_ref)).astype(bf16)
        for c in copies:
            c.start()

    fc = w1_ref.shape[1]
    bias = line(b1_ref)
    cut = lambda s: slice(s * sub, (s + 1) * sub)
    before = lambda s: mm(n2_ref[...], w1_ref[:, cut(s)]) + bias[:, cut(s)]
    ahead = before(0)
    for s in range(fc // sub):
        pre = ahead
        if s + 1 < fc // sub:
            ahead = before(s + 1)
        cdf, pdf = normal_cdf_pdf(pre)
        act = (pre * cdf).astype(bf16)
        slope_ref[:, cut(s)] = (cdf + pre * pdf).astype(bf16)
        act_ref[:, cut(s)] = act
        views = [r.at[:, :, cut(s)] if count == 2 else r.at[:, cut(s)] for r in refs]
        put(mm(grt_ref[...], act), views, core_ref[0], m, order)

    @pl.when(step == pl.num_programs(0) - 1)
    def _():
        for c in copies:
            c.wait()


def ff_fwd(core, dp, att, hid, wo, bo, g, b, grt, w1, b1, fc=1024, sub=1024):
    n, w = att.shape
    ff = w1.shape[1]
    m = w // dp
    if can_split(w, m):
        specs = [pl.BlockSpec((dp // 2, m, fc), lambda i: (0, i, 0))] * 2
        shapes = [jax.ShapeDtypeStruct((dp // 2, ff // fc * m, fc), f32)] * 2
    else:
        specs = [pl.BlockSpec((w, fc), lambda i: (0, i))]
        shapes = [jax.ShapeDtypeStruct((w, ff), f32)]
    left = pl.BlockSpec(memory_space=pl.ANY)
    res = pl.pallas_call(
        functools.partial(ff_fwd_kernel, m=m, order=ring_order(dp), sub=sub, count=len(specs), rb=n // 3),
        grid=(ff // fc,),
        in_specs=[
            SMEM1,
            whole((n, w)),
            whole((n, w)),
            whole((w, w)),
            whole((w,)),
            whole((w,)),
            whole((w,)),
            whole((w, n)),
            pl.BlockSpec((w, fc), lambda i: (0, i)),
            pl.BlockSpec((fc,), lambda i: (i,)),
        ],
        out_specs=[left, left] + [pl.BlockSpec((n, fc), lambda i: (0, i))] * 2 + specs,
        out_shape=[
            jax.ShapeDtypeStruct((n, w), f32),
            jax.ShapeDtypeStruct((n, w), bf16),
            jax.ShapeDtypeStruct((n, ff), bf16),
            jax.ShapeDtypeStruct((n, ff), bf16),
        ]
        + shapes,
        scratch_shapes=[pltpu.VMEM((n, w), f32), pltpu.VMEM((n, w), bf16), pltpu.SemaphoreType.DMA((2,))],
        compiler_params=params(60),
        cost_estimate=cost(6 * n * w * ff, n * w * 10 + ff * w * 8 + n * ff * 2, n * ff * 2),
        name="ff_fwd",
    )(core, att, hid, wo, bo, g, b, grt, w1, b1)
    return res[0], res[1], res[2], res[3], res[4:]


def ff_bwd_kernel(core_ref, n2_ref, gr_ref, w1a_ref, w1b_ref, sla_ref, slb_ref, w2a_ref, w2b_ref, *rest, first, count, m):
    gn_ref, db1_ref = rest[-2 - count : -count]
    refs = rest[-count:]
    side = lambda a, b: jnp.concatenate([a[...], b[...]], axis=1)
    w1 = side(w1a_ref, w1b_ref)
    w2 = jnp.concatenate([w2a_ref[...], w2b_ref[...]], axis=0)
    gpre = (mm(gr_ref[...], w2, NT) * side(sla_ref, slb_ref).astype(f32)).astype(bf16)

    @pl.when(pl.program_id(0) == 0)
    def _():
        gn_ref[...] = jnp.zeros_like(gn_ref) if first else rest[0][...]

    gn_ref[...] += mm(gpre, w1, NT)
    put(mm(gpre, n2_ref[...], TN), refs, core_ref[0], m)
    db1_ref[...] = jnp.sum(gpre.astype(f32), axis=0, keepdims=True)


def ff_bwd(core, dp, n2, gr, w1, slope, w2, base, steps, prev):
    n, w = n2.shape
    ff = w1.shape[1]
    m = ff // dp
    fc = 384
    ring = can_split(fc, m) and fc == 2 * m and dp == 16
    total = ff // (2 * fc)
    steps = total - base if steps is None else steps
    if ring:
        near = lambda i: jnp.where(base + i < 2, 4 * (base + i), 15 - 4 * (base + i))
        far = lambda i: jnp.where(base + i < 2, 4 * (base + i) + 2, 13 - 4 * (base + i))
        specs = [pl.BlockSpec((2, m, w), lambda i: (base + i, 0, 0))] * 2
        shapes = [jax.ShapeDtypeStruct((dp // 2, m, w), f32)] * 2
    else:
        near = lambda i: 2 * (base + i)
        far = lambda i: 2 * (base + i) + 1
        specs = [pl.BlockSpec((2 * fc, w), lambda i: (base + i, 0))]
        shapes = [jax.ShapeDtypeStruct((ff, w), f32)]
    extra = [] if prev is None else list(prev)
    res = pl.pallas_call(
        functools.partial(ff_bwd_kernel, first=prev is None, count=len(specs), m=m),
        grid=(steps,),
        in_specs=[
            SMEM1,
            whole((n, w)),
            whole((n, w)),
            pl.BlockSpec((w, fc), lambda i: (0, near(i))),
            pl.BlockSpec((w, fc), lambda i: (0, far(i))),
            pl.BlockSpec((n, fc), lambda i: (0, near(i))),
            pl.BlockSpec((n, fc), lambda i: (0, far(i))),
            pl.BlockSpec((fc, w), lambda i: (near(i), 0)),
            pl.BlockSpec((fc, w), lambda i: (far(i), 0)),
        ]
        + ([whole((n, w))] + [pl.BlockSpec(memory_space=pl.ANY)] * len(specs) if extra else []),
        out_specs=[whole((n, w)), pl.BlockSpec((1, 2 * fc), lambda i: (0, i))] + specs,
        out_shape=[jax.ShapeDtypeStruct((n, w), f32), jax.ShapeDtypeStruct((1, 2 * fc * steps), f32)] + shapes,
        input_output_aliases={10 + k: 2 + k for k in range(len(specs))} if extra else {},
        compiler_params=params(60),
        cost_estimate=cost(12 * n * w * fc * steps, n * w * 10 + fc * steps * w * 16 + n * fc * steps * 4),
        name="ff_bwd",
    )(core, n2, gr, w1, w1, slope, slope, w2, w2, *extra)
    return (res[0], *res[2:]), res[1]


def back_kernel(core_ref, mid_ref, gn_ref, cot_ref, tw_ref, a_ref, wo_ref, g_ref, *rest, m, count, order, sub):
    gm_ref, ga_ref, vec_ref = rest[-4 - count : -1 - count]
    dwo_refs, dwo_ref = rest[-1 - count : -1], rest[-1]
    rb, w = mid_ref.shape
    step = pl.program_id(0)
    add = lambda x: jnp.sum(x, axis=0, keepdims=True)
    parts = [slice(lo, lo + sub) for lo in range(0, rb, sub)]

    @pl.when(step == 0)
    def _():
        dwo_ref[...] = jnp.zeros_like(dwo_ref)
        vec_ref[...] = jnp.zeros_like(vec_ref)

    def norm_part(r):
        mid = mid_ref[r, :]
        std, inv = row_stats(mid)
        gn = gn_ref[r, :]
        gm = cot_ref[r, :].astype(f32) * tw_ref[r, :] + norm_back(gn, std, inv, line(g_ref))
        gm_ref[r, :] = gm
        gb = gm.astype(bf16)
        vec_ref[...] += jnp.concatenate([add(gb.astype(f32)), add(gn * std), add(gn), jnp.zeros((1, w), f32)], axis=0)
        return gb

    ahead = norm_part(parts[0])
    for i, r in enumerate(parts):
        gb = ahead
        if i + 1 < len(parts):
            ahead = norm_part(parts[i + 1])
        ga_ref[r, :] = mm(gb, wo_ref[...], NT).astype(bf16)
        dwo_ref[...] += mm(gb, a_ref[r, :], TN)

    @pl.when(step == pl.num_programs(0) - 1)
    def _():
        put(dwo_ref[...], dwo_refs, core_ref[0], m, order)


def grad_outs(rows, cols, m):
    if can_split(rows, m):
        shape = (rows // (2 * m), m, cols)
        return [whole(shape)] * 2, [jax.ShapeDtypeStruct(shape, f32)] * 2
    return [whole((rows, cols))], [jax.ShapeDtypeStruct((rows, cols), f32)]


def back_part(core, dp, mid, gn, cot, tw, att, wo, g, rb, sub=384):
    n, w = mid.shape
    row = lambda cols: pl.BlockSpec((rb, cols), lambda i: (i, 0))
    mo, mj = w // dp, 3 * w // dp
    if can_split(w, mo) and can_split(3 * w, mj):
        specs = [pl.BlockSpec((dp // 2, mo, w), lambda i: (0, mj // mo, 0))] * 2
        shapes = [jax.ShapeDtypeStruct((dp // 2, mj + mo, w), f32)] * 2
    else:
        specs, shapes = [whole((w, w))], [jax.ShapeDtypeStruct((w, w), f32)]
    res = pl.pallas_call(
        functools.partial(back_kernel, m=mo, count=len(specs), order=ring_order(dp), sub=sub),
        grid=(n // rb,),
        in_specs=[SMEM1, row(w), row(w), row(w), row(1), row(w), whole(wo.shape), whole((w,))],
        out_specs=[row(w), row(w), whole((4, w))] + specs,
        out_shape=[
            jax.ShapeDtypeStruct((n, w), f32),
            jax.ShapeDtypeStruct((n, w), bf16),
            jax.ShapeDtypeStruct((4, w), f32),
        ]
        + shapes,
        scratch_shapes=[pltpu.VMEM((w, w), f32)],
        compiler_params=params(),
        cost_estimate=cost(4 * n * w * w, n * w * 28),
        name="back_part",
    )(core, mid, gn, cot, tw, att, wo, g)
    return res[0], res[1], res[2], res[3:]


def finish_kernel(mid_ref, act_ref, w2_ref, b2_ref, out_ref):
    out_ref[...] = (mid_ref[...] + mm(act_ref[...], w2_ref[...]) + line(b2_ref)).astype(bf16)


def finish(mid, act, w2, b2, rb):
    n, w = mid.shape
    row = lambda cols: pl.BlockSpec((rb, cols), lambda i: (i, 0))
    return pl.pallas_call(
        finish_kernel,
        grid=(n // rb,),
        in_specs=[row(w), row(act.shape[1]), whole(w2.shape), whole((w,))],
        out_specs=row(w),
        out_shape=jax.ShapeDtypeStruct((n, w), bf16),
        compiler_params=params(),
        cost_estimate=cost(2 * n * w * act.shape[1], n * w * 14),
        name="finish",
    )(mid, act, w2, b2)


def joint_grad_kernel(core_ref, gp_ref, n1_ref, *rest, m, count, order):
    refs, gpt_ref = rest[-1 - count : -1], rest[-1]
    parts, n, w = gp_ref.shape

    @pl.when(pl.program_id(0) == 0)
    def _():
        for p in range(parts):
            gpt_ref[p * w : (p + 1) * w, :] = gp_ref[p].T

    put(mm(gpt_ref[...], n1_ref[...]), refs, core_ref[0], m, order)


def grad_block(rows, cols, cb, m):
    if can_split(rows, m):
        spec = pl.BlockSpec((rows // (2 * m), m, cb), lambda j: (0, 0, j))
        return [spec] * 2, [jax.ShapeDtypeStruct((rows // (2 * m), m, cols), f32)] * 2
    return [pl.BlockSpec((rows, cb), lambda j: (0, j))], [jax.ShapeDtypeStruct((rows, cols), f32)]


def joint_grad(core, dp, gp, n1, into, cb=256):
    parts, n, w = gp.shape
    m = parts * w // dp
    specs, shapes = grad_block(parts * w, w, cb, m)
    if len(into) == 2:
        shapes = [jax.ShapeDtypeStruct(x.shape, f32) for x in into]
    else:
        into = []
    return pl.pallas_call(
        functools.partial(joint_grad_kernel, m=m, count=len(specs), order=ring_order(dp)),
        grid=(w // cb,),
        in_specs=[SMEM1, whole((parts, n, w)), pl.BlockSpec((n, cb), lambda j: (0, j))]
        + [pl.BlockSpec(memory_space=pl.ANY)] * len(into),
        out_specs=specs,
        out_shape=shapes,
        input_output_aliases={3 + k: k for k in range(len(into))},
        scratch_shapes=[pltpu.VMEM((parts * w, n), bf16)],
        compiler_params=params(),
        cost_estimate=cost(2 * parts * n * w * w, n * w * 8 + parts * w * w * 4),
        name="joint_grad",
    )(core, gp, n1, *into)


def tail_kernel(gp_ref, hid_ref, gm_ref, wj_ref, g_ref, gh_ref, vec_ref, *, sub):
    rb, w = hid_ref.shape
    parts = [slice(lo, lo + sub) for lo in range(0, rb, sub)]
    add = lambda x: jnp.sum(x, axis=0, keepdims=True)

    def project(r):
        return sum(mm(gp_ref[p, r, :], wj_ref[:, p * w : (p + 1) * w], NT) for p in range(3))

    ahead = project(parts[0])
    vec = jnp.zeros((4, w), f32)
    for i, r in enumerate(parts):
        gn = ahead
        if i + 1 < len(parts):
            ahead = project(parts[i + 1])
        std, inv = row_stats(hid_ref[r, :])
        gh = (gm_ref[r, :] + norm_back(gn, std, inv, line(g_ref))).astype(bf16)
        gh_ref[r, :] = gh
        vec = vec + jnp.concatenate([add(gn * std), add(gn), add(gh.astype(f32)), jnp.zeros((1, w), f32)], axis=0)
    step = pl.program_id(0)

    @pl.when(step == 0)
    def _():
        vec_ref[...] = vec

    @pl.when(step > 0)
    def _():
        vec_ref[...] += vec


def tail_part(gp, hid, gm, wj, g, rb, sub=384):
    n, w = hid.shape
    row = lambda cols: pl.BlockSpec((rb, cols), lambda i: (i, 0))
    return pl.pallas_call(
        functools.partial(tail_kernel, sub=sub),
        grid=(n // rb,),
        in_specs=[pl.BlockSpec((3, rb, w), lambda i: (0, i, 0)), row(w), row(w), whole(wj.shape), whole((w,))],
        out_specs=[row(w), whole((4, w))],
        out_shape=[jax.ShapeDtypeStruct((n, w), bf16), jax.ShapeDtypeStruct((4, w), f32)],
        compiler_params=params(),
        cost_estimate=cost(6 * n * w * w, n * w * 16),
        name="tail_part",
    )(gp, hid, gm, wj, g)


def skip_grad_kernel(core_ref, gh_ref, x_ref, s_ref, vec_ref, *refs, m, order):
    ght = gh_ref[...].T
    val = jnp.concatenate([mm(ght, x_ref[...]), mm(ght, s_ref[...]), vec_ref[...]], axis=1)
    put(val, refs, core_ref[0], m, order)


def skip_grad(core, dp, gh, x, s, vec):
    n, w = gh.shape
    m = w // dp
    cols = 2 * w + vec.shape[1]
    specs, shapes = grad_block(w, cols, cols, m)
    return pl.pallas_call(
        functools.partial(skip_grad_kernel, m=m, order=ring_order(dp)),
        grid=(1,),
        in_specs=[SMEM1, whole((n, w)), whole((n, w)), whole((n, w)), whole(vec.shape)],
        out_specs=specs,
        out_shape=shapes,
        compiler_params=params(),
        cost_estimate=cost(4 * n * w * w, n * w * 6 + w * w * 8),
        name="skip_grad",
    )(core, gh, x, s, vec)


def in_grad_kernel(gh_ref, ws_ref, a_ref, b_ref):
    w = a_ref.shape[1]
    gh = gh_ref[...]
    a_ref[...] = mm(gh, ws_ref[:w, :], NT).astype(bf16)
    b_ref[...] = mm(gh, ws_ref[w:, :], NT).astype(bf16)


def in_grad(gh, ws, rb):
    n, w = gh.shape
    row = lambda cols: pl.BlockSpec((rb, cols), lambda i: (i, 0))
    return pl.pallas_call(
        in_grad_kernel,
        grid=(n // rb,),
        in_specs=[row(w), whole(ws.shape)],
        out_specs=[row(w), row(w)],
        out_shape=[jax.ShapeDtypeStruct((n, w), bf16)] * 2,
        compiler_params=params(),
        cost_estimate=cost(4 * n * w * w, n * w * 10),
        name="in_grad",
    )(gh, ws)


def pick(x, axis, index):
    return lax.dynamic_index_in_dim(x, index, axis, keepdims=False)


def swap(x, axis, bit=0):
    size = lax.axis_size(axis)
    return lax.ppermute(x, axis, [(i, i ^ (1 << bit)) for i in range(size)])


def pair_terms(refs, cols, dp):
    if len(refs) == 1:
        full = refs[0].reshape(dp // 2, 2, -1, cols)
        core = lax.axis_index("dp") & 1
        refs = [pick(full, 1, core), pick(full, 1, 1 - core)]
    return [refs[0], swap(refs[1], "dp")]


def both_sides(x, side):
    other = swap(x, "rep")
    return jnp.concatenate([jnp.where(side == 0, x, other), jnp.where(side == 0, other, x)], axis=0)


def add_kernel(a_ref, b_ref, out_ref):
    out_ref[...] = a_ref[...] + b_ref[...]


def add_blocks(a, b, per=4):
    places, rows, cols = a.shape
    spec = pl.BlockSpec((per, rows, cols), lambda i: (i, 0, 0))
    return pl.pallas_call(
        add_kernel,
        grid=(places // per,),
        in_specs=[spec, spec],
        out_specs=spec,
        out_shape=jax.ShapeDtypeStruct(a.shape, f32),
        compiler_params=params(),
        name="add_blocks",
    )(a, b)


def tie(x, y):
    return lax.optimization_barrier((x, y))


def per_device(*args):
    (inputs, skips, cot, lengths, keep, group_ids, group_counts, ws, bs, g1, s1, wj, wo, bo, g2, s2, w1, b1, w2, b2) = args
    n, w = inputs.shape
    ff = w1.shape[1]
    dp = lax.axis_size("dp")
    tokens_total = n * dp * lax.axis_size("rep")
    scale = float(tokens_total) ** -0.5
    side = lax.axis_index("rep")
    core = (lax.axis_index("dp") & 1).astype(jnp.int32).reshape(1)
    rb = n // 3
    ring = ring_order(dp)
    groups = [[2 * i + c for i in ring] for c in range(2)]
    ring_sum = lambda h: lax.psum_scatter(h, "dp", scatter_dimension=0, tiled=True, axis_index_groups=groups)[0]
    over_rep = lambda h: h + swap(h, "rep")

    hid, n1, packed, qf, kf, tw = front(
        lengths, group_ids, group_counts, keep, inputs, skips, ws, bs, g1, s1, wj, rb, tokens_total // group_counts.shape[0]
    )
    att, feat, gr, grt, gsum = attn_fwd(packed, qf, kf, cot, tw)
    mid, n2, act, slope, d2 = ff_fwd(core, dp, att, hid, wo, bo, g2, s2, grt, w1, b1)
    terms2 = pair_terms(d2, ff, dp)
    half2 = add_blocks(*terms2) if len(d2) == 2 else sum(terms2)
    carry, db0 = ff_bwd(core, dp, n2, gr, w1, slope, w2, 0, 1, None)
    carry, half2 = tie(carry, half2)
    carry, db1 = ff_bwd(core, dp, n2, gr, w1, slope, w2, 1, None, carry)
    gn2, d1 = carry[0], carry[1:]
    gm, gatt, vec2, do = back_part(core, dp, mid, gn2, cot, tw, att, wo, g2, n, rb)
    half1 = sum(pair_terms(d1, w, dp))
    gatt, half1 = tie(gatt, half1)
    sum2 = ring_sum(half2)
    sum1 = ring_sum(half1)

    gp = attn_bwd(packed, att, gatt, feat, kf)
    gp, sum2 = tie(gp, sum2)
    got2 = swap(sum2, "rep")

    dj = joint_grad(core, dp, gp, n1, do)
    gp, dj = tie(gp, dj)
    if len(dj) == 2:
        halfj = sum(pair_terms(dj, w, dp))
    else:
        full = jnp.concatenate([dj[0].reshape(dp, 3 * w // dp, w), do[0].reshape(dp, w // dp, w)], axis=1)
        halfj = sum(pair_terms([full.reshape(-1, w)], w, dp))
    gh, vec1 = tail_part(gp, hid, gm, wj, g1, rb)
    gh, halfj, sum1, got2 = lax.optimization_barrier((gh, halfj, sum1, got2))
    sumj = ring_sum(halfj)
    db = jnp.concatenate([db0, db1], axis=1).reshape(8, ff // 8)
    if len(d1) == 2:
        db = jnp.stack([db[ring.index(i)] for i in range(8)])
    db = db.reshape(w, ff // w)
    vec = jnp.concatenate([vec1.T, vec2[:3].T, gsum.T, db, jnp.zeros((w, PAIR - 8 - ff // w), f32)], axis=1)
    cols = 2 * w + PAIR
    ds = skip_grad(core, dp, gh, inputs, skips, vec)
    terms = [t.reshape(dp // 2, 2, -1, cols) for t in pair_terms(ds, cols, dp)]
    send = sum(pick(t, 1, 1 - side) for t in terms)
    gh, send = tie(gh, send)
    igrad, sgrad = in_grad(gh, ws, rb)
    act, igrad = tie(act, igrad)
    outcome = finish(mid, act, w2, b2, rb)
    halfs = sum(pick(t, 1, side) for t in terms) + swap(send, "rep")
    halfs, sumj, sum1, outcome, sgrad = lax.optimization_barrier((halfs, sumj, sum1, outcome, sgrad))
    sums = ring_sum(halfs)
    out2 = sum2 + got2
    out1 = over_rep(sum1)
    outj = over_rep(sumj)
    if len(d2) == 2:
        out2 = out2.reshape(-1, w // dp, 1024).transpose(1, 0, 2).reshape(w // dp, ff)
    outj, outo = outj[: 3 * w // dp], outj[3 * w // dp :]
    outs = both_sides(sums, side)

    ds, dj, do, d1, d2 = [m.T * scale for m in (outs[:, : 2 * w], outj, outo, out1, out2)]
    v = outs[:, 2 * w :] * scale
    col = lambda i: v[:, i]
    db1 = v[:, 8 : 8 + ff // w].reshape(-1)
    return (
        outcome, igrad, sgrad, ds, col(2), col(0), col(1), dj, do, col(4), col(5), col(6), d1, db1, d2, col(7),
    )


def solution(mesh):
    both = ("dp", "rep")
    in_specs = (P(both, None),) * 3 + (P(both),) * 3 + (P(),) * 14
    cols = P(None, "dp")
    vec = P("dp")
    out_specs = (P(both, None),) * 3 + (cols, vec, vec, vec, cols, cols, vec, vec, vec, cols, vec, cols, vec)
    return jax.shard_map(per_device, mesh=mesh, in_specs=in_specs, out_specs=out_specs, check_vma=False)
```
